256 devices in a mesh: wide: 32 (over z, x_lo, core), narrow: 8 (over x_hi, y).
Axes of the slice: x: 4 (x_hi: 2, x_lo: 2; x = x_hi * 2 + x_lo), y: 4, z: 8, core: 2. Of those that a mesh axis runs over, the one named last changes fastest.
Arguments:
- tokens: bfloat16 [4096, 2048], P('wide'), may hold values from -6 to 6
- request_lengths: int32 [32, 3], replicated, may hold values from 1 to 64, 128 in all within a row
- w_qkv: bfloat16 [2048, 3, 2048], P(None, None, 'narrow'), may hold values from -0.19921875 to 0.19921875
- qk_gain: float32 [2, 2048], P(None, 'narrow'), may hold values from 0.5 to 7
- w_out: bfloat16 [2048, 2048], P('narrow'), may hold values from -0.125 to 0.125
- norm_gains: float32 [3, 2048], replicated, may hold values from 0.25 to 1.75
- w_router: bfloat16 [2048, 64], replicated, may hold values from -0.0625 to 0.0625
- routes: int32 [4096, 8], P('wide'), may hold values from 0 to 63, all different within a row; in each aligned block of 128 rows (0 to 127, 128 to 255, ...) at most 20 rows name the same one
- w_gate: bfloat16 [64, 2048, 1024], P('wide', None, 'narrow'), may hold values from -0.125 to 0.125
- w_up: bfloat16 [64, 2048, 1024], P('wide', None, 'narrow'), may hold values from -0.125 to 0.125
- w_down: bfloat16 [64, 1024, 2048], P('wide', 'narrow'), may hold values from -0.1875 to 0.1875
- w_proj: bfloat16 [2048, 128], replicated, may hold values from -0.125 to 0.125
- doc_vectors: bfloat16 [262144, 128], P(('wide', 'narrow')), may hold values from -6 to 6
- doc_segment: int32 [256, 1024], P(('wide', 'narrow')), may hold values from 0 to 15, never falling along the last dimension, each value on 1 to 128 neighbouring positions
- doc_request: int32 [256, 16], P(('wide', 'narrow')), may hold values from 0 to 95
Outputs:
- layer_out: bfloat16 [4096, 2048], P('wide')
- doc_scores: float32 [256, 16], P(('wide', 'narrow'))
The draws below stay inside these ranges and needn't reach their ends.
Inputs may be any that keep to these rules, and one draw needn't show every extreme that they name: `request_lengths`: each row sums to 128, and its largest entry is exactly 64. `routes`: each row names 8 different experts. In the rows of one index of wide (aligned blocks of 128 rows) no expert is named by more than 20 rows, a bound that some block reaches. `doc_segment`: in each row the numbers never fall, every document has one or more rows, and one document has exactly 128.
All inputs are finite; a program needn't handle non-finite values.
Results may differ from the reference program's by a relative error of at most 0.009.
Values may be sent and summed in bfloat16 or wider, within the bound.
No kernel may reach another device: no remote copies, remote signals or barrier semaphores. Data moves between devices by JAX's collectives and lax.ppermute only.
A program may use at most 128 MiB of HBM per device.

```python
import math
import jax
import jax.numpy as jnp
import numpy as np
from jax import lax

D = 2048
HEADS = 16
HD = 128
FF = 1024
TOPK = 8
EMB = 128
TOK_DEV = 128
REQ_DEV = 3
DOCS_DEV = 16
DOC_MOST = 128
EXPERTS = 64
SHARDS = 32
TOKENS = 4096
REQUESTS = 96
MOST_REQ = 64
CAP = 20
DOC_TOK = 1024
HOLDERS = 256
N_NARROW = 8


LIMIT = 0.19921875


def draw_tokens(key, part):
    values = jax.random.normal(key, (TOKENS, D), jnp.float32)
    return jnp.clip(values, -6.0, 6.0).astype(jnp.bfloat16)


def draw_w_qkv(key, part):
    std = D ** (-0.5)
    query = jax.random.normal(jax.random.fold_in(key, 1), (D, 1, D), jnp.float32) * std
    value = jax.random.normal(jax.random.fold_in(key, 3), (D, 1, D), jnp.float32) * std
    keyed = jax.random.normal(jax.random.fold_in(key, 2), (D, 1, D), jnp.float32) * std
    return jnp.clip(jnp.concatenate([query, keyed, value], axis=1), -LIMIT, LIMIT).astype(jnp.bfloat16)


def draw_qk_gain(key, part):
    gains = jax.random.uniform(key, (2, HEADS, HD), jnp.float32, 0.6, 1.6)
    return gains.reshape(2, D)


def touch_ends(result, key, least, largest):
    longest = result.shape.index(max(result.shape))
    spots = []
    for shift in (0, 1):
        where = [jax.random.randint(jax.random.fold_in(key, axis), (), 0, length) for axis, length in enumerate(result.shape)]
        where[longest] = (where[longest] + shift) % result.shape[longest]
        spots.append(tuple(where))
    return result.at[spots[0]].set(least).at[spots[1]].set(largest)


def steps_of(stream_key, extent, pieces, low, top_value):
    def one(dim, blocks):
        heights = jax.random.uniform(jax.random.fold_in(jax.random.fold_in(stream_key, 6), dim), (blocks,), jnp.float32, low / len(pieces), top_value / len(pieces))
        return jnp.repeat(jnp.exp(heights), extent[dim] // blocks).reshape((-1,) + (1,) * (len(extent) - dim - 1))

    level = one(*pieces[0])
    for cut in pieces[1:]:
        level = level * one(*cut)
    return level


def split_up(amount, total, reach, slope):
    loads = [(1 << 20) // math.isqrt(standing ** slope) + 1 for standing in range(2, amount + 1)]
    rest, given = total - reach - (amount - 1), [1] * (amount - 1)
    while rest > 0:
        candidates = [i for i in range(amount - 1) if given[i] < reach]
        mass, remaining = sum([loads[i] for i in candidates]), rest
        for i in candidates:
            addition = min(reach - given[i], max(1, remaining * loads[i] // mass), rest)
            given[i] = given[i] + addition
            rest = rest - addition
    return np.array([reach] + given)


def ragged_sizes(key, amount, total, most, slope):
    if amount == 2:
        one = jax.random.randint(key, (), max(1, total - most), min(most, total - 1) + 1)
        return jnp.stack([one, total - one])
    lengths = jnp.asarray(split_up(amount, total, most, slope), jnp.int32)
    couples = (amount - 1) // 2
    source_of, sink = lengths[1:1 + 2 * couples:2], lengths[2:2 + 2 * couples:2]
    margin = jnp.minimum(source_of - 1, most - sink)
    passed = jax.random.randint(jax.random.fold_in(key, 1), (couples,), 0, 1 << 20) % (margin + 1)
    lengths = lengths.at[1:1 + 2 * couples:2].set(source_of - passed).at[2:2 + 2 * couples:2].set(sink + passed)
    return lengths[jax.random.permutation(jax.random.fold_in(key, 2), amount)]


def deal_out(stream_key, own, number, rows, amount, top, most, slope):
    ranking = jax.random.permutation(stream_key, amount)
    heavy_load, usual = shares(amount, rows * top, most, slope, True), shares(amount, rows * top, most, slope, False)
    places = jnp.arange(amount)

    def named(tallies, rotation):
        used = int((tallies > 0).sum())
        fixed = max(1, used // 4)
        passed = fixed + (places - fixed + rotation * (used - fixed)) % max(1, amount - fixed)
        return jnp.zeros((amount,), jnp.int32).at[ranking[jnp.where(places < fixed, places, passed)]].set(jnp.asarray(tallies, jnp.int32))

    tallies = jnp.where(number % 4 == 0, named(heavy_load, number // 4), named(usual, number - number // 4 - 1))
    mixed = jax.random.permutation(jax.random.fold_in(own, 3), amount)
    source_of, taker = mixed[0:amount // 2 * 2:2], mixed[1:amount // 2 * 2:2]
    room = jnp.minimum(tallies[source_of] - 1, most - tallies[taker]) // 2
    room = jnp.where((source_of == ranking[0]) | (taker == ranking[0]) | (tallies[taker] == 0), 0, jnp.maximum(room, 0))
    passed = jax.random.randint(jax.random.fold_in(own, 4), (amount // 2,), 0, 1 << 20) % (room + 1)
    tallies = tallies.at[source_of].add(-passed).at[taker].add(passed)
    members = jnp.searchsorted(jnp.cumsum(tallies), jnp.arange(rows * top), side="right").astype(jnp.int32)
    table = members.reshape(top, rows).T
    table = table[jax.random.permutation(jax.random.fold_in(own, 1), rows)]
    rotation = jax.random.randint(jax.random.fold_in(own, 2), (rows, 1), 0, top)
    return jnp.take_along_axis(table, (jnp.arange(top)[None, :] + rotation) % top, axis=1)


def shares(amount, total, most, skew, full):
    weights = [(1 << 20) // math.isqrt(standing ** skew) + 1 for standing in range(1, amount + 1)]
    largest = most if full else min(most, max(-(-total // amount), total * weights[0] // sum(weights)))
    least = 1 if total - largest >= amount - 1 else 0
    given, spare = [largest] + [least] * (amount - 1), total - largest - least * (amount - 1)
    while spare > 0:
        movable = [i for i in range(1, amount) if given[i] < largest] or [i for i in range(1, amount) if given[i] < most]
        pool, remaining = sum([weights[i] for i in movable]), spare
        for i in movable:
            more = min(most - given[i], max(1, remaining * weights[i] // pool), spare)
            given[i] = given[i] + more
            spare = spare - more
    return np.array(given)


def centred(key, shape, width, reach, cuts=(), kind=jnp.bfloat16):
    result = width * jax.random.normal(key, shape, jnp.float32)
    if cuts:
        result = result * steps_of(key, shape, cuts, -0.22, 0.18)
    return jnp.clip(result, -reach, reach).astype(kind)


def setup_inputs(seed: int = 0) -> dict:
    key_of = jax.random.split(jax.random.key(seed), 16)
    tokens = draw_tokens(jax.random.fold_in(key_of[15], 71), 0)
    request_lengths = jax.vmap(lambda own: ragged_sizes(own, REQ_DEV, TOK_DEV, MOST_REQ, 2))(jax.random.split(key_of[1], SHARDS)).reshape((SHARDS, REQ_DEV)).astype(jnp.int32)
    w_qkv = draw_w_qkv(jax.random.fold_in(key_of[15], 71), 0)
    qk_gain = draw_qk_gain(jax.random.fold_in(key_of[15], 71), 0)
    w_out = centred(key_of[4], (D, D), D ** -0.5, 0.125, ((0, 8),))
    norm_gains = jnp.clip(1.0 + 0.15 * jax.random.normal(key_of[5], (3, D), jnp.float32), 0.25, 1.75)
    w_router = centred(key_of[6], (D, EXPERTS), (4 * D) ** -0.5, 0.0625)
    routes_keys = jax.random.split(jax.random.fold_in(key_of[7], 1), TOKENS // TOK_DEV)
    routes_turns = jax.random.permutation(jax.random.fold_in(key_of[7], 3), TOKENS // TOK_DEV)
    routes = jax.vmap(lambda own, number: deal_out(jax.random.fold_in(key_of[7], 2), own, number, TOK_DEV, EXPERTS, TOPK, CAP, 2))(routes_keys, routes_turns).reshape((TOKENS, TOPK))
    w_gate = centred(key_of[8], (EXPERTS, D, FF), D ** -0.5, 0.125, ((0, 32), (2, 8)))
    w_up = centred(key_of[9], (EXPERTS, D, FF), D ** -0.5, 0.125, ((0, 32), (2, 8)))
    w_down = centred(key_of[10], (EXPERTS, FF, D), FF ** -0.5, 0.1875, ((0, 32), (1, 8)))
    w_proj = centred(key_of[11], (D, EMB), D ** -0.5, 0.125)
    doc_vectors = centred(key_of[12], (HOLDERS * DOC_TOK, EMB), 1.0, 6.0, ((0, 256),))
    doc_segment = jax.vmap(lambda own: jnp.searchsorted(jnp.cumsum(ragged_sizes(own, DOCS_DEV, DOC_TOK, DOC_MOST, 2)), jnp.arange(DOC_TOK), side="right"))(jax.random.split(key_of[13], HOLDERS)).reshape((HOLDERS, DOC_TOK)).astype(jnp.int32)
    doc_request = touch_ends(jax.random.randint(key_of[14], (HOLDERS, DOCS_DEV), 0, REQUESTS), jax.random.fold_in(key_of[14], 1), 0, REQUESTS - 1).astype(jnp.int32)
    return {"tokens": tokens, "request_lengths": request_lengths, "w_qkv": w_qkv, "qk_gain": qk_gain, "w_out": w_out, "norm_gains": norm_gains, "w_router": w_router, "routes": routes, "w_gate": w_gate, "w_up": w_up, "w_down": w_down, "w_proj": w_proj, "doc_vectors": doc_vectors, "doc_segment": doc_segment, "doc_request": doc_request}


EPS = 1e-06
THETA = 50000.0
NEG = -1e+30

def rms_norm(values, gain):
    return values * lax.rsqrt(lax.optimization_barrier(jnp.mean(values * values, axis=-1, keepdims=True)) + EPS) * gain

def rotary(values, offsets):
    half = values.shape[-1] // 2
    freq = THETA ** (-jnp.arange(half, dtype=jnp.float32) / half)
    angle = offsets.astype(jnp.float32)[:, None] * freq[None, :]
    cosine = jnp.cos(angle)[:, None, :]
    sine = jnp.sin(angle)[:, None, :]
    first = values[..., :half]
    second = values[..., half:]
    return jnp.concatenate([first * cosine - second * sine, second * cosine + first * sine], axis=-1)

def request_layout(lengths_row, count):
    bounds = jnp.cumsum(lengths_row).astype(jnp.int32)
    places = jnp.arange(count, dtype=jnp.int32)
    member = lax.optimization_barrier(jnp.sum((places[:, None] >= bounds[None, :-1]).astype(jnp.int32), axis=1)).astype(jnp.int32)
    starts = (bounds - lengths_row).astype(jnp.int32)
    pick = member[:, None] == jnp.arange(lengths_row.shape[0], dtype=jnp.int32)[None, :]
    offsets = places - lax.optimization_barrier(jnp.sum(jnp.where(pick, starts[None, :], 0), axis=1)).astype(jnp.int32)
    return (member, offsets)

def reference(tokens, request_lengths, w_qkv, qk_gain, w_out, norm_gains, w_router, routes, w_gate, w_up, w_down, w_proj, doc_vectors, doc_segment, doc_request):
    f32 = jnp.float32
    bf16 = jnp.bfloat16
    scale = HD ** (-0.5)
    flat_qkv = w_qkv.reshape(D, 3 * D)
    expert_ids = jnp.arange(EXPERTS, dtype=jnp.int32)

    def front(item):
        x, lengths_row, route_rows = item
        member, offsets = request_layout(lengths_row, TOK_DEV)
        xf = x.astype(f32)
        normed = rms_norm(xf, norm_gains[0]).astype(bf16)
        proj = jnp.dot(normed, flat_qkv, preferred_element_type=f32).reshape(TOK_DEV, 3, HEADS, HD)
        query = rotary(rms_norm(proj[:, 0], qk_gain[0].reshape(HEADS, HD)), offsets).astype(bf16)
        keys = rotary(rms_norm(proj[:, 1], qk_gain[1].reshape(HEADS, HD)), offsets).astype(bf16)
        values = proj[:, 2].astype(bf16)
        scores = jnp.einsum('qhd,khd->hqk', query.astype(f32), keys.astype(f32)) * scale
        scores = jnp.where((member[:, None] == member[None, :])[None], scores, NEG)
        peak = lax.optimization_barrier(jnp.max(scores, axis=-1, keepdims=True))
        weights = jnp.exp(scores - peak)
        probs = (weights / lax.optimization_barrier(jnp.sum(weights, axis=-1, keepdims=True))).astype(bf16)
        mixed = jnp.einsum('hqk,khd->qhd', probs.astype(f32), values.astype(f32)).astype(bf16).reshape(TOK_DEV, D)
        attn = jnp.dot(mixed, w_out, preferred_element_type=f32)
        hidden = (xf + attn).astype(bf16)
        normed_two = rms_norm(hidden.astype(f32), norm_gains[1]).astype(bf16)
        logits = jnp.dot(normed_two, w_router, preferred_element_type=f32)
        onehot = route_rows[:, :, None] == expert_ids[None, None, :]
        chosen = lax.optimization_barrier(jnp.sum(jnp.where(onehot, logits[:, None, :], 0.0), axis=-1))
        lifted = jax.nn.sigmoid(chosen)
        gates = lifted / lax.optimization_barrier(jnp.sum(lifted, axis=-1, keepdims=True))
        counts = lax.optimization_barrier(jnp.sum(onehot.astype(f32), axis=1))
        before = jnp.cumsum(counts, axis=0) - counts
        slots = lax.optimization_barrier(jnp.sum(jnp.where(onehot, before[:, None, :], 0.0), axis=-1)).astype(jnp.int32)
        places = (route_rows * CAP + slots).astype(jnp.int32)
        owner = jnp.full((EXPERTS * CAP,), TOK_DEV, jnp.int32).at[places.reshape(-1)].set(jnp.repeat(jnp.arange(TOK_DEV, dtype=jnp.int32), TOPK))
        padded = jnp.concatenate([normed_two, jnp.zeros((1, D), bf16)], axis=0)
        buffer = padded[owner].reshape(EXPERTS, CAP, D)
        return (hidden, gates, slots, buffer)
    hiddens, gates, slots, buffers = lax.map(front, (tokens.reshape(SHARDS, TOK_DEV, D), request_lengths, routes.reshape(SHARDS, TOK_DEV, TOPK)))
    rows = buffers.transpose(1, 0, 2, 3).reshape(EXPERTS, SHARDS * CAP, D)
    narrow_ff = FF // N_NARROW

    def expert(item):
        block, wg, wu, wd = item
        gate = jnp.dot(block, wg, preferred_element_type=f32)
        upward = jnp.dot(block, wu, preferred_element_type=f32)
        act = (jax.nn.silu(gate) * upward).astype(bf16).reshape(SHARDS * CAP, N_NARROW, narrow_ff)
        parts = jnp.einsum('rnf,nfd->nrd', act.astype(f32), wd.reshape(N_NARROW, narrow_ff, D).astype(f32)).astype(bf16)
        parts = lax.optimization_barrier(parts)
        return lax.optimization_barrier(jnp.sum(parts.astype(f32), axis=0))
    outputs = lax.map(expert, (rows, w_gate, w_up, w_down)).reshape(EXPERTS * SHARDS * CAP, D)

    def back(item):
        hidden, gate_rows, slot_rows, route_rows, shard = item
        index = (route_rows * (SHARDS * CAP) + shard * CAP + slot_rows).astype(jnp.int32)
        picked = outputs[index]
        moe = lax.optimization_barrier(jnp.sum(gate_rows[:, :, None] * picked, axis=1))
        layer = (hidden.astype(f32) + moe).astype(bf16)
        normed_three = rms_norm(layer.astype(f32), norm_gains[2]).astype(bf16)
        embedded = jnp.dot(normed_three, w_proj, preferred_element_type=f32)
        vectors = (embedded * lax.rsqrt(lax.optimization_barrier(jnp.sum(embedded * embedded, axis=-1, keepdims=True)) + EPS)).astype(bf16)
        return (layer, vectors)
    layers, vectors = lax.map(back, (hiddens, gates, slots, routes.reshape(SHARDS, TOK_DEV, TOPK), jnp.arange(SHARDS, dtype=jnp.int32)))
    layer_out = layers.reshape(TOKENS, D)
    vectors = vectors.reshape(TOKENS, EMB)
    padded_q = jnp.concatenate([vectors, jnp.zeros((MOST_REQ, EMB), bf16)], axis=0)
    docs = jnp.concatenate([doc_vectors.reshape(HOLDERS, DOC_TOK, EMB), jnp.zeros((HOLDERS, DOC_MOST, EMB), bf16)], axis=1)
    bounds = jnp.cumsum(request_lengths, axis=1).astype(jnp.int32)
    starts = (bounds - request_lengths).astype(jnp.int32)
    flat_lengths = request_lengths.reshape(-1).astype(jnp.int32)
    flat_starts = (starts + jnp.arange(SHARDS, dtype=jnp.int32)[:, None] * TOK_DEV).reshape(-1).astype(jnp.int32)
    request_ids = jnp.arange(REQUESTS, dtype=jnp.int32)

    def holder_scores(item):
        held, segment_row, requests = item

        def one(doc, request):
            first = jnp.sum((segment_row < doc).astype(jnp.int32)).astype(jnp.int32)
            size = jnp.sum((segment_row == doc).astype(jnp.int32)).astype(jnp.int32)
            doc_rows = lax.dynamic_slice_in_dim(held, first, DOC_MOST, 0)
            pick = request == request_ids
            q_first = jnp.sum(jnp.where(pick, flat_starts, 0)).astype(jnp.int32)
            q_size = jnp.sum(jnp.where(pick, flat_lengths, 0)).astype(jnp.int32)
            queries = lax.dynamic_slice_in_dim(padded_q, q_first, MOST_REQ, 0)
            sims = jnp.dot(queries, doc_rows.T, preferred_element_type=f32)
            sims = jnp.where(jnp.arange(DOC_MOST, dtype=jnp.int32)[None, :] < size, sims, NEG)
            best = lax.optimization_barrier(jnp.max(sims, axis=1))
            used = jnp.arange(MOST_REQ, dtype=jnp.int32) < q_size
            return jnp.sum(jnp.where(used, best, 0.0)) / q_size.astype(f32)
        return jax.vmap(one)(jnp.arange(DOCS_DEV, dtype=jnp.int32), requests)
    doc_scores = lax.map(holder_scores, (docs, doc_segment, doc_request))
    return (layer_out, doc_scores)
```

```python
import functools

import jax
import jax.numpy as jnp
from jax import lax
from jax.experimental import pallas as pl
from jax.experimental.pallas import tpu as pltpu
from jax.sharding import Mesh, PartitionSpec as P

HD = 128
TOPK = 8
TOK = 128
CAP = 20
EXPERTS = 64
WIDE = 32
EPS = 1e-06
THETA = 50000.0
NEG = -1e30
W = ("z", "xl", "core")
N = ("xh", "y")
f32 = jnp.float32
bf16 = jnp.bfloat16


def rms_norm(values, gain):
    return values * lax.rsqrt(jnp.mean(values * values, axis=-1, keepdims=True) + EPS) * gain


def rotary(values, offsets):
    half = values.shape[-1] // 2
    freq = THETA ** (-jnp.arange(half, dtype=f32) / half)
    angle = offsets.astype(f32)[:, None] * freq[None, :]
    cosine = jnp.cos(angle)[:, None, :]
    sine = jnp.sin(angle)[:, None, :]
    first = values[..., :half]
    second = values[..., half:]
    return jnp.concatenate(
        [first * cosine - second * sine, second * cosine + first * sine], axis=-1
    )


def request_layout(lengths_row, count):
    bounds = jnp.cumsum(lengths_row)
    places = jnp.arange(count, dtype=jnp.int32)
    member = jnp.sum((places[:, None] >= bounds[None, :-1]).astype(jnp.int32), axis=1)
    starts = bounds - lengths_row
    pick = member[:, None] == jnp.arange(lengths_row.shape[0], dtype=jnp.int32)[None, :]
    offsets = places - jnp.sum(jnp.where(pick, starts[None, :], 0), axis=1)
    return (member, offsets)


def y_shift(x, k):
    return lax.ppermute(x, "y", [(s, (s + k) % 4) for s in range(4)])


def x_swap(x):
    return lax.ppermute(x, "xh", [(0, 1), (1, 0)])


def gate_up_kernel(j_ref, x0, x1, x2, x3, w_own, w_par, gain_ref, out_ref):
    j = j_ref[0]
    xs = (x0, x1, x2, x3)
    total = jnp.zeros((x0.shape[0], 1), f32)
    for x in xs:
        v = x[...].astype(f32)
        total = total + jnp.sum(v * v, axis=1, keepdims=True)
    scale = lax.rsqrt(total / 2048.0 + EPS)
    own = jnp.zeros((x0.shape[0], 256), f32)
    par = jnp.zeros((x0.shape[0], 256), f32)
    for k, x in enumerate(xs):
        part = lax.rem(j - k + 4, 4)
        at = pl.multiple_of(part * 512, 512)
        normed = (x[...].astype(f32) * scale * gain_ref[part]).astype(bf16)
        own = own + jnp.dot(normed, w_own[pl.ds(at, 512), :], preferred_element_type=f32)
        par = par + jnp.dot(normed, w_par[pl.ds(at, 512), :], preferred_element_type=f32)
    for at, both in ((0, own), (128, par)):
        gate, up = both[:, :128], both[:, 128:]
        out_ref[:, at : at + 128] = (gate / (1.0 + jnp.exp(-gate)) * up).astype(bf16)


def down_kernel(a0, a1, a2, a3, w0, w1, w2, w3, out_ref):
    total = jnp.dot(a0[...], w0[...], preferred_element_type=f32)
    for a, w in ((a1, w1), (a2, w2), (a3, w3)):
        total = total + jnp.dot(a[...], w[...], preferred_element_type=f32)
    for s in range(WIDE):
        out_ref[s] = total[s * CAP : (s + 1) * CAP].astype(bf16)


def score_kernel(info_ref, vec_ref, doc_ref, out_ref):
    lane = lax.broadcasted_iota(jnp.int32, (1, 16), 1)
    scores = jnp.zeros((1, 16), f32)
    rows = lax.broadcasted_iota(jnp.int32, (144, 128), 0)
    columns = lax.broadcasted_iota(jnp.int32, (1, 128), 1)
    for d in range(16):
        first, size = info_ref[0, d], info_ref[1, d]
        q_first, q_size = info_ref[2, d], info_ref[3, d]
        at = pl.multiple_of(jnp.minimum((first // 16) * 16, 1024 - 144), 16)
        q_at = pl.multiple_of(jnp.minimum((q_first // 16) * 16, 4096 - 128), 16)
        sims = lax.dot_general(
            doc_ref[pl.ds(at, 144), :],
            vec_ref[pl.ds(q_at, 128), :],
            (((1,), (1,)), ((), ())),
            preferred_element_type=f32,
        )
        keep = (rows >= first - at) & (rows < first - at + size)
        best = jnp.max(jnp.where(keep, sims, NEG), axis=0, keepdims=True)
        used = (columns >= q_first - q_at) & (columns < q_first - q_at + q_size)
        value = jnp.sum(jnp.where(used, best, 0.0), axis=1, keepdims=True) / q_size.astype(f32)
        scores = jnp.where(lane == d, value, scores)
    out_ref[...] = scores


def vmem():
    return pl.BlockSpec(memory_space=pltpu.VMEM)


def smem():
    return pl.BlockSpec(memory_space=pltpu.SMEM)


def body(
    tokens,
    request_lengths,
    w_qkv,
    qk_gain,
    w_out,
    norm_gains,
    w_router,
    routes,
    w_gate,
    w_up,
    w_down,
    w_proj,
    doc_vectors,
    doc_segment,
    doc_request,
):
    i = lax.axis_index("xh")
    j = lax.axis_index("y")
    wide = lax.axis_index(W)

    def pick(array, which):
        return lax.dynamic_index_in_dim(array, which, 0, keepdims=False)

    w_own = jnp.concatenate([pick(w_gate, i), pick(w_up, i)], axis=1)
    w_par = x_swap(jnp.concatenate([pick(w_gate, 1 - i), pick(w_up, 1 - i)], axis=1))
    d_par = x_swap(pick(w_down, 1 - i))
    d_both = jnp.concatenate([pick(w_down, i), d_par], axis=0)

    def d_columns(which):
        return lax.dynamic_slice_in_dim(d_both, lax.rem(which, 4) * 512, 512, 1)

    downs = [d_columns(j)] + [y_shift(d_columns(j + k), k) for k in (1, 2, 3)]

    experts_here = 2 * jnp.arange(WIDE, dtype=jnp.int32) + i
    hit = jnp.sum((routes.T[None, :, :] == experts_here[:, None, None]).astype(f32), axis=1)
    places = jnp.arange(TOK, dtype=jnp.int32)
    earlier = (places[:, None] < places[None, :]).astype(bf16)
    before = jnp.dot(hit.astype(bf16), earlier, preferred_element_type=f32)
    slot = jnp.arange(CAP, dtype=jnp.int32).astype(f32)
    chosen = (before[:, None, :] == slot[None, :, None]) & (hit[:, None, :] > 0)

    heads = w_qkv.shape[2] // HD
    lengths_row = lax.dynamic_slice_in_dim(request_lengths, wide, 1, 0)[0]
    member, offsets = request_layout(lengths_row, TOK)
    xf = tokens.astype(f32)
    normed = rms_norm(xf, norm_gains[0]).astype(bf16)
    proj = jnp.dot(normed, w_qkv.reshape(2048, -1), preferred_element_type=f32).reshape(
        TOK, 3, heads, HD
    )
    query = rotary(rms_norm(proj[:, 0], qk_gain[0].reshape(heads, HD)), offsets).astype(bf16)
    keys = rotary(rms_norm(proj[:, 1], qk_gain[1].reshape(heads, HD)), offsets).astype(bf16)
    values = proj[:, 2].astype(bf16)
    scores = jnp.einsum("qhd,khd->hqk", query, keys, preferred_element_type=f32) * HD ** (-0.5)
    scores = jnp.where((member[:, None] == member[None, :])[None], scores, NEG)
    peak = jnp.max(scores, axis=-1, keepdims=True)
    weights = jnp.exp(scores - peak)
    probs = (weights / jnp.sum(weights, axis=-1, keepdims=True)).astype(bf16)
    mixed = (
        jnp.einsum("hqk,khd->qhd", probs, values, preferred_element_type=f32)
        .astype(bf16)
        .reshape(TOK, heads * HD)
    )
    w_out4 = w_out.reshape(heads * HD, 4, 512)
    attn = jnp.einsum("th,hyd->ytd", mixed, w_out4, preferred_element_type=f32).astype(bf16)
    attn = lax.all_to_all(attn, "y", 0, 0, tiled=True)
    attn = jnp.sum(attn.astype(f32), axis=0).astype(bf16)
    attn_par = x_swap(attn)
    mine = lax.dynamic_slice_in_dim(tokens, j * 512, 512, 1)
    hidden = (mine.astype(f32) + (attn.astype(f32) + attn_par.astype(f32))).astype(bf16)

    rows = lax.dot_general(
        chosen.astype(bf16), hidden, (((2,), (0,)), ((), ())), preferred_element_type=f32
    ).astype(bf16)
    rows = lax.all_to_all(rows, W, 0, 0, tiled=True).reshape(WIDE * CAP, 512)
    gathered = [rows] + [y_shift(rows, k) for k in (1, 2, 3)]

    hf = hidden.astype(f32)
    gain_mine = lax.dynamic_slice_in_dim(norm_gains[1], j * 512, 512, 0)
    router_mine = lax.dynamic_slice_in_dim(w_router, j * 512, 512, 0)
    part = jnp.dot((hf * gain_mine).astype(bf16), router_mine, preferred_element_type=f32)
    square = jnp.sum(hf * hf, axis=1, keepdims=True)
    part = jnp.concatenate([part, jnp.broadcast_to(square, (TOK, EXPERTS))], axis=1)
    whole = part
    for k in (1, 2, 3):
        whole = whole + y_shift(part, k)
    logits = whole[:, :EXPERTS] * lax.rsqrt(whole[:, EXPERTS : EXPERTS + 1] / 2048.0 + EPS)
    lifted = jax.nn.sigmoid(logits)
    onehot = jnp.sum(
        (routes[:, :, None] == jnp.arange(EXPERTS, dtype=jnp.int32)[None, None, :]).astype(f32),
        axis=1,
    )
    lifted = lifted * onehot
    gates = lifted / jnp.sum(lifted, axis=1, keepdims=True)
    gates = lax.dynamic_index_in_dim(gates.reshape(TOK, WIDE, 2), i, 2, keepdims=False).T
    mixing = jnp.where(chosen, gates[:, None, :], 0.0)
    mixing_hi = lax.reduce_precision(mixing, 8, 7)
    mixing_lo = (mixing - mixing_hi).astype(bf16)
    mixing_hi = mixing_hi.astype(bf16)

    act = pl.pallas_call(
        gate_up_kernel,
        out_shape=jax.ShapeDtypeStruct((WIDE * CAP, 256), bf16),
        in_specs=[smem()] + [vmem()] * 7,
        out_specs=vmem(),
        compiler_params=pltpu.CompilerParams(vmem_limit_bytes=40 << 20),
        name="gate_up",
    )(j.reshape(1), *gathered, w_own, w_par, norm_gains[1].reshape(4, 1, 512))
    acts = [act] + [y_shift(act, k) for k in (1, 2, 3)]
    out = pl.pallas_call(
        down_kernel,
        out_shape=jax.ShapeDtypeStruct((WIDE, CAP, 512), bf16),
        in_specs=[vmem()] * 8,
        out_specs=vmem(),
        compiler_params=pltpu.CompilerParams(vmem_limit_bytes=40 << 20),
        name="down",
    )(*acts, *downs)
    out = lax.all_to_all(out, W, 0, 0, tiled=True)

    contract = (((0, 1), (0, 1)), ((), ()))
    moe = lax.dot_general(mixing_hi, out, contract, preferred_element_type=f32)
    moe = moe + lax.dot_general(mixing_lo, out, contract, preferred_element_type=f32)
    moe = moe.astype(bf16)
    moe_par = x_swap(moe)
    layer = (hf + (moe.astype(f32) + moe_par.astype(f32))).astype(bf16)
    layer = lax.all_to_all(jnp.broadcast_to(layer[None], (4, TOK, 512)), "y", 0, 0, tiled=True)
    layer_out = layer.transpose(1, 0, 2).reshape(TOK, 2048)

    normed_three = rms_norm(layer_out.astype(f32), norm_gains[2]).astype(bf16)
    embedded = jnp.dot(normed_three, w_proj, preferred_element_type=f32)
    vectors = (
        embedded * lax.rsqrt(jnp.sum(embedded * embedded, axis=-1, keepdims=True) + EPS)
    ).astype(bf16)
    piece = lax.all_to_all(
        jnp.broadcast_to(vectors[None], (WIDE, TOK, 128)), W, 0, 0, tiled=True
    ).reshape(WIDE * TOK, 128)
    segment = doc_segment[0]
    requests = doc_request[0]
    docs = jnp.arange(16, dtype=jnp.int32)
    first = jnp.sum((segment[None, :] < docs[:, None]).astype(jnp.int32), axis=1)
    size = jnp.sum((segment[None, :] == docs[:, None]).astype(jnp.int32), axis=1)
    starts = jnp.cumsum(request_lengths, axis=1) - request_lengths
    starts = (starts + TOK * jnp.arange(WIDE, dtype=jnp.int32)[:, None]).reshape(-1)
    match = requests[:, None] == jnp.arange(96, dtype=jnp.int32)[None, :]
    q_first = jnp.sum(jnp.where(match, starts[None, :], 0), axis=1)
    q_size = jnp.sum(jnp.where(match, request_lengths.reshape(-1)[None, :], 0), axis=1)
    info = jnp.stack([first, size, q_first, q_size])
    doc_scores = pl.pallas_call(
        score_kernel,
        out_shape=jax.ShapeDtypeStruct((1, 16), f32),
        in_specs=[smem(), vmem(), vmem()],
        out_specs=vmem(),
        name="score",
    )(info, piece, doc_vectors)
    return (layer_out, doc_scores)


def solution(mesh):
    split = Mesh(mesh.devices.reshape(8, 2, 2, 2, 4), ("z", "xl", "core", "xh", "y"))
    placed = (
        P(W, None),
        P(),
        P(None, None, N),
        P(None, N),
        P(N, None),
        P(),
        P(),
        P(W, None),
        P(W, None, N),
        P(W, None, N),
        P(W, N, None),
        P(),
        P(W + N, None),
        P(W + N, None),
        P(W + N, None),
    )
    return jax.shard_map(
        body,
        mesh=split,
        in_specs=placed,
        out_specs=(P(W, None), P(W + N, None)),
        check_vma=False,
    )
```

```python
import math

import jax
import jax.numpy as jnp
from jax import lax
from jax.experimental import pallas as pl
from jax.experimental.pallas import tpu as pltpu
from jax.sharding import Mesh, PartitionSpec as P

HD = 128
TOPK = 8
TOK = 128
CAP = 20
EXPERTS = 64
WIDE = 32
EPS = 1e-06
THETA = 50000.0
NEG = -1e30
W = ("z", "xl", "core")
N = ("xh", "y")
f32 = jnp.float32
bf16 = jnp.bfloat16


def y_shift(x, k):
    return lax.ppermute(x, "y", [(s, (s + k) % 4) for s in range(4)])


def x_swap(x):
    return lax.ppermute(x, "xh", [(0, 1), (1, 0)])


def attention_kernel(wide_ref, lengths_ref, x_ref, w_ref, qk_ref, out_w_ref, gain_ref, out_ref):
    wide = wide_ref[0]
    one, two = lengths_ref[wide, 0], lengths_ref[wide, 0] + lengths_ref[wide, 1]

    def member_of(places):
        return (places >= one).astype(jnp.int32) + (places >= two).astype(jnp.int32)

    down_places = lax.broadcasted_iota(jnp.int32, (TOK, HD), 0)
    across_places = lax.broadcasted_iota(jnp.int32, (TOK, HD), 1)
    member = member_of(down_places)
    same = member == member_of(across_places)
    start = jnp.where(member == 0, 0, jnp.where(member == 1, one, two))
    half = lax.rem(across_places, HD // 2).astype(f32)
    freq = jnp.exp(half * (-math.log(THETA) / (HD // 2)))
    angle = (down_places - start).astype(f32) * freq
    cosine = jnp.cos(angle)
    sine = jnp.sin(angle)
    sine = jnp.where(across_places < HD // 2, -sine, sine)

    x = x_ref[...].astype(f32)
    scale = lax.rsqrt(jnp.mean(x * x, axis=1, keepdims=True) + EPS)
    normed = (x * scale * gain_ref[...]).astype(bf16)
    query, keys, values = (
        jnp.dot(normed, w_ref[part], preferred_element_type=f32) for part in range(3)
    )

    def turned(v, gain):
        v = v * lax.rsqrt(jnp.mean(v * v, axis=1, keepdims=True) + EPS) * gain
        return (v * cosine + pltpu.roll(v, HD // 2, 1) * sine).astype(bf16)

    mixed = []
    for head in range(2):
        at = slice(head * HD, (head + 1) * HD)
        q = turned(query[:, at], qk_ref[0:1, at])
        k = turned(keys[:, at], qk_ref[1:2, at])
        scores = lax.dot_general(q, k, (((1,), (1,)), ((), ())), preferred_element_type=f32)
        scores = jnp.where(same, scores * HD ** (-0.5), NEG)
        weights = jnp.exp(scores - jnp.max(scores, axis=1, keepdims=True))
        probs = (weights / jnp.sum(weights, axis=1, keepdims=True)).astype(bf16)
        mixed.append(
            jnp.dot(probs, values[:, at].astype(bf16), preferred_element_type=f32).astype(bf16)
        )
    mixed = jnp.concatenate(mixed, axis=1)
    for part in range(4):
        out_ref[part] = jnp.dot(
            mixed, out_w_ref[:, part * 512 : (part + 1) * 512], preferred_element_type=f32
        ).astype(bf16)


def gate_up_kernel(at_ref, x0, x1, x2, x3, gate_ref, up_ref, gate_par, up_par, gain_ref, out_ref):
    i, j = at_ref[0], at_ref[1]
    xs = (x0, x1, x2, x3)
    total = jnp.zeros((x0.shape[0], 1), f32)
    for x in xs:
        v = x[...].astype(f32)
        total = total + jnp.sum(v * v, axis=1, keepdims=True)
    scale = lax.rsqrt(total / 2048.0 + EPS)
    own = jnp.zeros((x0.shape[0], 256), f32)
    par = jnp.zeros((x0.shape[0], 256), f32)
    for k, x in enumerate(xs):
        part = lax.rem(j - k + 4, 4)
        rows = pl.ds(pl.multiple_of(part * 512, 512), 512)
        normed = (x[...].astype(f32) * scale * gain_ref[part]).astype(bf16)
        w_own = jnp.concatenate([gate_ref[i, rows, :], up_ref[i, rows, :]], axis=1)
        w_par = jnp.concatenate([gate_par[rows, :], up_par[rows, :]], axis=1)
        own = own + jnp.dot(normed, w_own, preferred_element_type=f32)
        par = par + jnp.dot(normed, w_par, preferred_element_type=f32)
    for at, both in ((0, own), (128, par)):
        gate, up = both[:, :128], both[:, 128:]
        out_ref[:, at : at + 128] = (gate / (1.0 + jnp.exp(-gate)) * up).astype(bf16)


def down_kernel(at_ref, a0, a1, a2, a3, w0, w1, w2, w3, par_ref, out_ref):
    i = at_ref[0]
    total = jnp.zeros((a0.shape[0], 512), f32)
    for k, (a, w) in enumerate(((a0, w0), (a1, w1), (a2, w2), (a3, w3))):
        weight = jnp.concatenate([w[i], par_ref[k]], axis=0)
        total = total + jnp.dot(a[...], weight, preferred_element_type=f32)
    for s in range(WIDE):
        out_ref[s] = total[s * CAP : (s + 1) * CAP].astype(bf16)


def embed_kernel(hidden_ref, moe_ref, par_ref, gain_ref, w_ref, layer_ref, part_ref):
    layer = hidden_ref[...].astype(f32) + (moe_ref[...].astype(f32) + par_ref[...].astype(f32))
    layer = layer.astype(bf16)
    layer_ref[...] = layer
    layer = layer.astype(f32)
    scaled = (layer * gain_ref[...]).astype(bf16)
    part_ref[0:TOK, :] = jnp.dot(scaled, w_ref[...], preferred_element_type=f32)
    square = jnp.broadcast_to(jnp.sum(layer * layer, axis=1, keepdims=True), (TOK, TOK))
    part_ref[TOK:, :] = jnp.transpose(square)[0:8]


def vector_kernel(p0, p1, p2, p3, out_ref):
    whole = p0[...] + p1[...] + p2[...] + p3[...]
    square = jnp.transpose(jnp.broadcast_to(whole[TOK : TOK + 1], (TOK, TOK)))
    embedded = whole[0:TOK] * lax.rsqrt(square / 2048.0 + EPS)
    norm = jnp.sum(embedded * embedded, axis=1, keepdims=True)
    vectors = (embedded * lax.rsqrt(norm + EPS)).astype(bf16)
    for copy in range(16):
        out_ref[copy] = vectors


def assemble_kernel(at_ref, p0, p1, p2, p3, out_ref):
    j = at_ref[1]
    for k, piece in enumerate((p0, p1, p2, p3)):
        part = lax.rem(j - k + 4, 4)
        out_ref[:, pl.ds(pl.multiple_of(part * 512, 512), 512)] = piece[...]


def score_kernel(info_ref, own_ref, other_ref, doc_ref, out_ref):
    lane = lax.broadcasted_iota(jnp.int32, (1, 16), 1)
    scores = jnp.zeros((1, 16), f32)
    rows = lax.broadcasted_iota(jnp.int32, (144, 128), 0)
    columns = lax.broadcasted_iota(jnp.int32, (1, 128), 1)
    for d in range(16):
        first, size = info_ref[0, d], info_ref[1, d]
        q_first, q_size = info_ref[2, d], info_ref[3, d]
        at = pl.multiple_of(jnp.minimum((first // 16) * 16, 1024 - 144), 16)
        q_at = pl.multiple_of(jnp.minimum((q_first // 16) * 16, 2048 - 128), 16)
        query = jnp.where(
            info_ref[4, d] == 0, own_ref[pl.ds(q_at, 128), :], other_ref[pl.ds(q_at, 128), :]
        )
        sims = lax.dot_general(
            doc_ref[pl.ds(at, 144), :],
            query,
            (((1,), (1,)), ((), ())),
            preferred_element_type=f32,
        )
        keep = (rows >= first - at) & (rows < first - at + size)
        best = jnp.max(jnp.where(keep, sims, NEG), axis=0, keepdims=True)
        used = (columns >= q_first - q_at) & (columns < q_first - q_at + q_size)
        value = jnp.sum(jnp.where(used, best, 0.0), axis=1, keepdims=True) / q_size.astype(f32)
        scores = jnp.where(lane == d, value, scores)
    out_ref[...] = scores


def vmem():
    return pl.BlockSpec(memory_space=pltpu.VMEM)


def smem():
    return pl.BlockSpec(memory_space=pltpu.SMEM)


def body(
    tokens,
    request_lengths,
    w_qkv,
    qk_gain,
    w_out,
    norm_gains,
    w_router,
    routes,
    w_gate,
    w_up,
    w_down,
    w_proj,
    doc_vectors,
    doc_segment,
    doc_request,
):
    i = lax.axis_index("xh")
    j = lax.axis_index("y")
    core = lax.axis_index("core")
    wide = lax.axis_index(W)
    here = jnp.stack([i, j])

    def pick(array, which):
        return lax.dynamic_index_in_dim(array, which, 0, keepdims=False)

    def cut(array, part, axis):
        return lax.dynamic_slice_in_dim(array, lax.rem(part, 4) * 512, 512, axis)

    gate_par = x_swap(pick(w_gate, 1 - i))
    up_par = x_swap(pick(w_up, 1 - i))
    downs = [cut(w_down, j, 2)] + [y_shift(cut(w_down, j + k, 2), k) for k in (1, 2, 3)]
    down_par = x_swap(jnp.stack([pick(d, 1 - i) for d in downs]))

    experts_here = 2 * jnp.arange(WIDE, dtype=jnp.int32) + i
    hit = jnp.sum((routes.T[None, :, :] == experts_here[:, None, None]).astype(f32), axis=1)
    places = jnp.arange(TOK, dtype=jnp.int32)
    earlier = (places[:, None] < places[None, :]).astype(bf16)
    before = jnp.dot(hit.astype(bf16), earlier, preferred_element_type=f32)
    slot = jnp.arange(CAP, dtype=jnp.int32).astype(f32)
    chosen = (before[:, None, :] == slot[None, :, None]) & (hit[:, None, :] > 0)

    attn = pl.pallas_call(
        attention_kernel,
        out_shape=jax.ShapeDtypeStruct((4, TOK, 512), bf16),
        in_specs=[smem()] * 2 + [vmem()] * 5,
        out_specs=vmem(),
        compiler_params=pltpu.CompilerParams(vmem_limit_bytes=40 << 20),
        name="attention",
    )(
        wide.reshape(1),
        request_lengths,
        tokens,
        w_qkv.transpose(1, 0, 2),
        qk_gain,
        w_out,
        norm_gains[0:1],
    )
    attn = lax.all_to_all(attn, "y", 0, 0, tiled=True)
    attn = jnp.sum(attn.astype(f32), axis=0).astype(bf16)
    attn_par = x_swap(attn)
    mine = lax.dynamic_slice_in_dim(tokens, j * 512, 512, 1)
    hidden = (mine.astype(f32) + (attn.astype(f32) + attn_par.astype(f32))).astype(bf16)

    rows = lax.dot_general(
        chosen.astype(bf16), hidden, (((2,), (0,)), ((), ())), preferred_element_type=f32
    ).astype(bf16)
    rows = lax.all_to_all(rows, W, 0, 0, tiled=True).reshape(WIDE * CAP, 512)
    rows, gate_par, up_par = lax.optimization_barrier((rows, gate_par, up_par))
    gathered = [rows] + [y_shift(rows, k) for k in (1, 2, 3)]

    hf = hidden.astype(f32)
    gain_mine = lax.dynamic_slice_in_dim(norm_gains[1], j * 512, 512, 0)
    router_mine = lax.dynamic_slice_in_dim(w_router, j * 512, 512, 0)
    part = jnp.dot((hf * gain_mine).astype(bf16), router_mine, preferred_element_type=f32)
    square = jnp.sum(hf * hf, axis=1, keepdims=True)
    part = jnp.concatenate([part, jnp.broadcast_to(square, (TOK, EXPERTS))], axis=1)
    whole = part
    for k in (1, 2, 3):
        whole = whole + y_shift(part, k)
    logits = whole[:, :EXPERTS] * lax.rsqrt(whole[:, EXPERTS : EXPERTS + 1] / 2048.0 + EPS)
    lifted = jax.nn.sigmoid(logits)
    onehot = jnp.sum(
        (routes[:, :, None] == jnp.arange(EXPERTS, dtype=jnp.int32)[None, None, :]).astype(f32),
        axis=1,
    )
    lifted = lifted * onehot
    gates = lifted / jnp.sum(lifted, axis=1, keepdims=True)
    gates = lax.dynamic_index_in_dim(gates.reshape(TOK, WIDE, 2), i, 2, keepdims=False).T
    mixing = jnp.where(chosen, gates[:, None, :], 0.0)
    mixing_hi = lax.reduce_precision(mixing, 8, 7)
    mixing_lo = (mixing - mixing_hi).astype(bf16)
    mixing_hi = mixing_hi.astype(bf16)

    act = pl.pallas_call(
        gate_up_kernel,
        out_shape=jax.ShapeDtypeStruct((WIDE * CAP, 256), bf16),
        in_specs=[smem()] + [vmem()] * 9,
        out_specs=vmem(),
        compiler_params=pltpu.CompilerParams(vmem_limit_bytes=40 << 20),
        name="gate_up",
    )(here, *gathered, w_gate, w_up, gate_par, up_par, norm_gains[1].reshape(4, 1, 512))
    act, down_par = lax.optimization_barrier((act, down_par))
    acts = [act] + [y_shift(act, k) for k in (1, 2, 3)]
    out = pl.pallas_call(
        down_kernel,
        out_shape=jax.ShapeDtypeStruct((WIDE, CAP, 512), bf16),
        in_specs=[smem()] + [vmem()] * 9,
        out_specs=vmem(),
        compiler_params=pltpu.CompilerParams(vmem_limit_bytes=40 << 20),
        name="down",
    )(here, *acts, *downs, down_par)
    out = lax.all_to_all(out, W, 0, 0, tiled=True)

    contract = (((0, 1), (0, 1)), ((), ()))
    moe = lax.dot_general(mixing_hi, out, contract, preferred_element_type=f32)
    moe = moe + lax.dot_general(mixing_lo, out, contract, preferred_element_type=f32)
    moe = moe.astype(bf16)
    moe_par = x_swap(moe)
    layer, part = pl.pallas_call(
        embed_kernel,
        out_shape=(
            jax.ShapeDtypeStruct((TOK, 512), bf16),
            jax.ShapeDtypeStruct((TOK + 8, 128), f32),
        ),
        in_specs=[vmem()] * 5,
        out_specs=(vmem(), vmem()),
        name="embed",
    )(hidden, moe, moe_par, cut(norm_gains[2:3], j, 1), cut(w_proj, j, 0))
    parts = [part] + [y_shift(part, k) for k in (1, 2, 3)]
    layers = [layer] + [y_shift(layer, k) for k in (1, 2, 3)]

    vectors = pl.pallas_call(
        vector_kernel,
        out_shape=jax.ShapeDtypeStruct((16, TOK, 128), bf16),
        in_specs=[vmem()] * 4,
        out_specs=vmem(),
        name="vectors",
    )(*parts)
    own = lax.all_to_all(vectors, ("z", "xl"), 0, 0, tiled=True).reshape(16 * TOK, 128)
    other = lax.ppermute(own, "core", [(0, 1), (1, 0)])
    layer_out = pl.pallas_call(
        assemble_kernel,
        out_shape=jax.ShapeDtypeStruct((TOK, 2048), bf16),
        in_specs=[smem()] + [vmem()] * 4,
        out_specs=vmem(),
        name="assemble",
    )(here, *layers)
    segment = doc_segment[0]
    requests = doc_request[0]
    docs = jnp.arange(16, dtype=jnp.int32)
    first = jnp.sum((segment[None, :] < docs[:, None]).astype(jnp.int32), axis=1)
    size = jnp.sum((segment[None, :] == docs[:, None]).astype(jnp.int32), axis=1)
    starts = jnp.cumsum(request_lengths, axis=1) - request_lengths
    starts = (starts + TOK * (jnp.arange(WIDE, dtype=jnp.int32) // 2)[:, None]).reshape(-1)
    match = requests[:, None] == jnp.arange(96, dtype=jnp.int32)[None, :]
    q_first = jnp.sum(jnp.where(match, starts[None, :], 0), axis=1)
    q_size = jnp.sum(jnp.where(match, request_lengths.reshape(-1)[None, :], 0), axis=1)
    away = lax.rem(requests // 3, 2) ^ core
    info = jnp.stack([first, size, q_first, q_size, away])
    doc_scores = pl.pallas_call(
        score_kernel,
        out_shape=jax.ShapeDtypeStruct((1, 16), f32),
        in_specs=[smem(), vmem(), vmem(), vmem()],
        out_specs=vmem(),
        name="score",
    )(info, own, other, doc_vectors)
    return (layer_out, doc_scores)


def solution(mesh):
    split = Mesh(mesh.devices.reshape(8, 2, 2, 2, 4), ("z", "xl", "core", "xh", "y"))
    placed = (
        P(W, None),
        P(),
        P(None, None, N),
        P(None, N),
        P(N, None),
        P(),
        P(),
        P(W, None),
        P(W, None, N),
        P(W, None, N),
        P(W, N, None),
        P(),
        P(W + N, None),
        P(W + N, None),
        P(W + N, None),
    )
    return jax.shard_map(
        body,
        mesh=split,
        in_specs=placed,
        out_specs=(P(W, None), P(W + N, None)),
        check_vma=False,
    )
```

```python
import math

import jax
import jax.numpy as jnp
from jax import lax
from jax.experimental import pallas as pl
from jax.experimental.pallas import tpu as pltpu
from jax.sharding import Mesh, PartitionSpec as P

HD = 128
TOPK = 8
TOK = 128
CAP = 20
EXPERTS = 64
WIDE = 32
GROUPS = ((0, 20),)
EPS = 1e-06
THETA = 50000.0
NEG = -1e30
W = ("z", "xl", "core")
N = ("xh", "y")
f32 = jnp.float32
bf16 = jnp.bfloat16


def y_shift(x, k):
    return lax.ppermute(x, "y", [(s, (s + k) % 4) for s in range(4)])


def x_swap(x):
    return lax.ppermute(x, "xh", [(0, 1), (1, 0)])


def attention_kernel(
    here_ref,
    lengths_ref,
    qk_ref,
    gain_ref,
    x_hbm,
    w_hbm,
    out_hbm,
    out0,
    out1,
    out2,
    out3,
    x_ref,
    w_ref,
    out_w_ref,
    sems,
):
    copies = [pltpu.make_async_copy(x_hbm, x_ref, sems.at[0])]
    copies += [
        pltpu.make_async_copy(w_hbm.at[part], w_ref.at[part], sems.at[1 + part]) for part in range(3)
    ]
    copies += [pltpu.make_async_copy(out_hbm, out_w_ref, sems.at[4])]
    for copy in copies:
        copy.start()
    wide = here_ref[2]
    one = lengths_ref[0, wide]
    two = one + lengths_ref[1, wide]

    def member_of(places):
        return (places >= one).astype(jnp.int32) + (places >= two).astype(jnp.int32)

    down_places = lax.broadcasted_iota(jnp.int32, (TOK, HD), 0)
    across_places = lax.broadcasted_iota(jnp.int32, (TOK, HD), 1)
    member = member_of(down_places)
    same = member == member_of(across_places)
    start = jnp.where(member == 0, 0, jnp.where(member == 1, one, two))
    half = lax.rem(across_places, HD // 2).astype(f32)
    freq = jnp.exp(half * (-math.log(THETA) / (HD // 2)))
    angle = (down_places - start).astype(f32) * freq
    cosine = jnp.cos(angle)
    sine = jnp.sin(angle)
    sine = jnp.where(across_places < HD // 2, -sine, sine)

    copies[0].wait()
    x = x_ref[...].astype(f32)
    scale = lax.rsqrt(jnp.mean(x * x, axis=1, keepdims=True) + EPS)
    normed = (x * scale * gain_ref[0:1, :]).astype(bf16)
    parts = []
    for part in range(3):
        copies[1 + part].wait()
        parts.append(jnp.dot(normed, w_ref[part], preferred_element_type=f32))
    query, keys, values = parts

    def turned(v, gain):
        v = v * lax.rsqrt(jnp.mean(v * v, axis=1, keepdims=True) + EPS) * gain
        return (v * cosine + pltpu.roll(v, HD // 2, 1) * sine).astype(bf16)

    mixed = []
    for head in range(2):
        at = slice(head * HD, (head + 1) * HD)
        q = turned(query[:, at], qk_ref[0:1, at])
        k = turned(keys[:, at], qk_ref[1:2, at])
        scores = lax.dot_general(q, k, (((1,), (1,)), ((), ())), preferred_element_type=f32)
        scores = jnp.where(same, scores * HD ** (-0.5), NEG)
        weights = jnp.exp(scores - jnp.max(scores, axis=1, keepdims=True))
        probs = (weights / jnp.sum(weights, axis=1, keepdims=True)).astype(bf16)
        mixed.append(
            jnp.dot(probs, values[:, at].astype(bf16), preferred_element_type=f32).astype(bf16)
        )
    mixed = jnp.concatenate(mixed, axis=1)
    copies[4].wait()
    j = here_ref[1]
    for k, out_ref in enumerate((out0, out1, out2, out3)):
        part = lax.rem(j + k, 4)
        columns = pl.ds(pl.multiple_of(part * 512, 512), 512)
        out_ref[...] = jnp.dot(mixed, out_w_ref[:, columns], preferred_element_type=f32).astype(bf16)


def dispatch_kernel(here_ref, x_ref, own_ref, par_ref, choose_ref, hidden_ref, *rows_refs):
    j = here_ref[1]
    mine = x_ref[:, pl.ds(pl.multiple_of(j * 512, 512), 512)].astype(f32)
    hidden = (mine + (own_ref[...].astype(f32) + par_ref[...].astype(f32))).astype(bf16)
    hidden_ref[...] = hidden
    rows = jnp.dot(choose_ref[...], hidden, preferred_element_type=f32)
    at = 0
    for rows_ref in rows_refs:
        size = rows_ref.shape[1]
        for s in range(WIDE):
            rows_ref[s] = rows[at : at + size].astype(bf16)
            at += size


def gate_up_kernel(
    here_ref, x0, x1, x2, x3, gain_ref, gate_hbm, up_hbm, gate_par, up_par, out_ref, w_ref, sems
):
    i, j = here_ref[0], here_ref[1]
    sources = (gate_hbm.at[i], up_hbm.at[i], gate_par, up_par)
    copies = [
        pltpu.make_async_copy(source, w_ref.at[n], sems.at[n]) for n, source in enumerate(sources)
    ]
    for copy in copies:
        copy.start()
    xs = (x0, x1, x2, x3)
    total = jnp.zeros((x0.shape[0], 1), f32)
    for x in xs:
        v = x[...].astype(f32)
        total = total + jnp.sum(v * v, axis=1, keepdims=True)
    scale = lax.rsqrt(total / 2048.0 + EPS)
    for copy in copies:
        copy.wait()
    own = jnp.zeros((x0.shape[0], 256), f32)
    par = jnp.zeros((x0.shape[0], 256), f32)
    for k, x in enumerate(xs):
        part = lax.rem(j - k + 4, 4)
        rows = pl.ds(pl.multiple_of(part * 512, 512), 512)
        normed = (x[...].astype(f32) * scale * gain_ref[1:2, rows]).astype(bf16)
        w_own = jnp.concatenate([w_ref[0, rows, :], w_ref[1, rows, :]], axis=1)
        w_par = jnp.concatenate([w_ref[2, rows, :], w_ref[3, rows, :]], axis=1)
        own = own + jnp.dot(normed, w_own, preferred_element_type=f32)
        par = par + jnp.dot(normed, w_par, preferred_element_type=f32)
    for at, both in ((0, own), (128, par)):
        gate, up = both[:, :128], both[:, 128:]
        out_ref[:, at : at + 128] = (gate / (1.0 + jnp.exp(-gate)) * up).astype(bf16)


def down_kernel(here_ref, a0, a1, a2, a3, w0, w1, w2, w3, par_ref, out_ref, w_ref, sems):
    i = here_ref[0]
    copies = []
    for k, w in enumerate((w0, w1, w2, w3)):
        copies.append(
            (
                pltpu.make_async_copy(w.at[i], w_ref.at[k, 0:128], sems.at[0, k]),
                pltpu.make_async_copy(par_ref.at[k], w_ref.at[k, 128:256], sems.at[1, k]),
            )
        )
    for pair in copies:
        for copy in pair:
            copy.start()
    total = jnp.zeros((a0.shape[0], 512), f32)
    for k, a in enumerate((a0, a1, a2, a3)):
        for copy in copies[k]:
            copy.wait()
        total = total + jnp.dot(a[...], w_ref[k], preferred_element_type=f32)
    size = out_ref.shape[1]
    for s in range(WIDE):
        out_ref[s] = total[s * size : (s + 1) * size].astype(bf16)


def embed_kernel(here_ref, hidden_ref, moe_ref, par_ref, gain_ref, w_ref, layer_ref, part_ref):
    mine = pl.ds(pl.multiple_of(here_ref[1] * 512, 512), 512)
    layer = hidden_ref[...].astype(f32) + (moe_ref[...].astype(f32) + par_ref[...].astype(f32))
    layer = layer.astype(bf16)
    layer_ref[...] = layer
    layer = layer.astype(f32)
    scaled = (layer * gain_ref[2:3, mine]).astype(bf16)
    part_ref[0:TOK, :] = jnp.dot(scaled, w_ref[mine, :], preferred_element_type=f32)
    square = jnp.broadcast_to(jnp.sum(layer * layer, axis=1, keepdims=True), (TOK, TOK))
    part_ref[TOK:, :] = jnp.transpose(square)[0:8]


def vector_kernel(p0, p1, p2, p3, out_ref):
    whole = p0[...] + p1[...] + p2[...] + p3[...]
    square = jnp.transpose(jnp.broadcast_to(whole[TOK : TOK + 1], (TOK, TOK)))
    embedded = whole[0:TOK] * lax.rsqrt(square / 2048.0 + EPS)
    norm = jnp.sum(embedded * embedded, axis=1, keepdims=True)
    vectors = (embedded * lax.rsqrt(norm + EPS)).astype(bf16)
    for copy in range(16):
        out_ref[copy] = vectors


def assemble_kernel(here_ref, p0, p1, p2, p3, out_ref):
    j = here_ref[1]
    for k, piece in enumerate((p0, p1, p2, p3)):
        part = lax.rem(j - k + 4, 4)
        out_ref[:, pl.ds(pl.multiple_of(part * 512, 512), 512)] = piece[...]


def score_kernel(info_ref, doc_ref, own_ref, other_ref, out_ref, query_ref, sems):
    def spot(d):
        return pl.multiple_of(jnp.minimum((info_ref[2, d] // 16) * 16, 2048 - 128), 16)

    def copy_of(ref, d):
        return pltpu.make_async_copy(ref.at[pl.ds(spot(d), 128), :], query_ref.at[d], sems.at[d])

    for d in range(16):

        @pl.when(info_ref[4, d] == 0)
        def _():
            copy_of(own_ref, d).start()

        @pl.when(info_ref[4, d] != 0)
        def _():
            copy_of(other_ref, d).start()

    lane = lax.broadcasted_iota(jnp.int32, (1, 16), 1)
    scores = jnp.zeros((1, 16), f32)
    rows = lax.broadcasted_iota(jnp.int32, (144, 128), 0)
    columns = lax.broadcasted_iota(jnp.int32, (1, 128), 1)
    for d in range(16):
        copy_of(own_ref, d).wait()
    for d in range(16):
        first, size = info_ref[0, d], info_ref[1, d]
        q_first, q_size = info_ref[2, d], info_ref[3, d]
        at = pl.multiple_of(jnp.minimum((first // 16) * 16, 1024 - 144), 16)
        sims = lax.dot_general(
            doc_ref[pl.ds(at, 144), :],
            query_ref[d],
            (((1,), (1,)), ((), ())),
            preferred_element_type=f32,
        )
        keep = (rows >= first - at) & (rows < first - at + size)
        best = jnp.max(jnp.where(keep, sims, NEG), axis=0, keepdims=True)
        q_start = q_first - spot(d)
        used = (columns >= q_start) & (columns < q_start + q_size)
        value = jnp.sum(jnp.where(used, best, 0.0), axis=1, keepdims=True) / q_size.astype(f32)
        scores = jnp.where(lane == d, value, scores)
    out_ref[...] = scores


def vmem():
    return pl.BlockSpec(memory_space=pltpu.VMEM)


def smem():
    return pl.BlockSpec(memory_space=pltpu.SMEM)


def hbm():
    return pl.BlockSpec(memory_space=pl.ANY)


def params():
    return pltpu.CompilerParams(vmem_limit_bytes=40 << 20)


def body(
    tokens,
    request_lengths,
    w_qkv,
    qk_gain,
    w_out,
    norm_gains,
    w_router,
    routes,
    w_gate,
    w_up,
    w_down,
    w_proj,
    doc_vectors,
    doc_segment,
    doc_request,
):
    i = lax.axis_index("xh")
    j = lax.axis_index("y")
    core = lax.axis_index("core")
    wide = lax.axis_index(W)
    here = jnp.stack([i, j, wide, core])

    def pick(array, which):
        return lax.dynamic_index_in_dim(array, which, 0, keepdims=False)

    def cut(array, part, axis):
        return lax.dynamic_slice_in_dim(array, lax.rem(part, 4) * 512, 512, axis)

    attn = pl.pallas_call(
        attention_kernel,
        out_shape=(jax.ShapeDtypeStruct((TOK, 512), bf16),) * 4,
        in_specs=[smem()] * 2 + [vmem()] * 2 + [hbm()] * 3,
        out_specs=(vmem(),) * 4,
        scratch_shapes=[
            pltpu.VMEM((TOK, 2048), bf16),
            pltpu.VMEM((3, 2048, 256), bf16),
            pltpu.VMEM((256, 2048), bf16),
            pltpu.SemaphoreType.DMA((5,)),
        ],
        compiler_params=params(),
        name="attention",
    )(
        here,
        request_lengths.T,
        qk_gain,
        norm_gains,
        tokens,
        w_qkv.transpose(1, 0, 2),
        w_out,
    )
    attn_parts = [y_shift(attn[k], k) for k in (1, 2, 3)]

    own_part, w_gate, w_up = lax.optimization_barrier((attn[0], w_gate, w_up))
    gate_par = x_swap(pick(w_gate, 1 - i))
    up_par = x_swap(pick(w_up, 1 - i))
    downs = [cut(w_down, j, 2)] + [y_shift(cut(w_down, j + k, 2), k) for k in (1, 2, 3)]
    down_par = x_swap(jnp.stack([pick(d, 1 - i) for d in downs]))

    experts_here = 2 * jnp.arange(WIDE, dtype=jnp.int32) + i
    hit = jnp.sum((routes.T[None, :, :] == experts_here[:, None, None]).astype(f32), axis=1)
    places = jnp.arange(TOK, dtype=jnp.int32)
    earlier = (places[:, None] < places[None, :]).astype(bf16)
    before = jnp.dot(hit.astype(bf16), earlier, preferred_element_type=f32)
    slot = jnp.arange(CAP, dtype=jnp.int32).astype(f32)
    chosen = (before[:, None, :] == slot[None, :, None]) & (hit[:, None, :] > 0)
    choose = jnp.concatenate(
        [chosen[:, a:b].astype(bf16).reshape(WIDE * (b - a), TOK) for a, b in GROUPS], axis=0
    )

    attn = (own_part.astype(f32) + sum(p.astype(f32) for p in attn_parts)).astype(bf16)
    attn, choose = lax.optimization_barrier((attn, choose))
    attn_par = x_swap(attn)
    attn_par, gate_par = lax.optimization_barrier((attn_par, gate_par))
    hidden, *rows = pl.pallas_call(
        dispatch_kernel,
        out_shape=(
            jax.ShapeDtypeStruct((TOK, 512), bf16),
            *(jax.ShapeDtypeStruct((WIDE, b - a, 512), bf16) for a, b in GROUPS),
        ),
        in_specs=[smem()] + [vmem()] * 4,
        out_specs=(vmem(),) * (1 + len(GROUPS)),
        compiler_params=params(),
        name="dispatch",
    )(here, tokens, attn, attn_par, choose)

    backs = []
    arrived = []
    for g, group in enumerate(rows):
        if arrived:
            group, arrived[-1] = lax.optimization_barrier((group, arrived[-1]))
        arrived.append(lax.all_to_all(group, W, 0, 0, tiled=True))
    for g, x in enumerate(arrived):
        size = x.shape[1]
        x = x.reshape(WIDE * size, 512)
        if g == 0:
            x, up_par = lax.optimization_barrier((x, up_par))
        act = pl.pallas_call(
            gate_up_kernel,
            out_shape=jax.ShapeDtypeStruct((WIDE * size, 256), bf16),
            in_specs=[smem()] + [vmem()] * 5 + [hbm()] * 4,
            out_specs=vmem(),
            scratch_shapes=[pltpu.VMEM((4, 2048, 128), bf16), pltpu.SemaphoreType.DMA((4,))],
            compiler_params=params(),
            name="gate_up",
        )(here, x, *(y_shift(x, k) for k in (1, 2, 3)), norm_gains, w_gate, w_up, gate_par, up_par)
        if g == 0:
            act, down_par = lax.optimization_barrier((act, down_par))
        out = pl.pallas_call(
            down_kernel,
            out_shape=jax.ShapeDtypeStruct((WIDE, size, 512), bf16),
            in_specs=[smem()] + [vmem()] * 4 + [hbm()] * 5,
            out_specs=vmem(),
            scratch_shapes=[pltpu.VMEM((4, 256, 512), bf16), pltpu.SemaphoreType.DMA((2, 4))],
            compiler_params=params(),
            name="down",
        )(here, act, *(y_shift(act, k) for k in (1, 2, 3)), *downs, down_par)
        backs.append(lax.all_to_all(out, W, 0, 0, tiled=True))

    hf = hidden.astype(f32)
    gain_mine = lax.dynamic_slice_in_dim(norm_gains[1], j * 512, 512, 0)
    router_mine = lax.dynamic_slice_in_dim(w_router, j * 512, 512, 0)
    part = jnp.dot((hf * gain_mine).astype(bf16), router_mine, preferred_element_type=f32)
    square = jnp.sum(hf * hf, axis=1, keepdims=True)
    part = jnp.concatenate([part, jnp.broadcast_to(square, (TOK, EXPERTS))], axis=1)
    whole = part
    for k in (1, 2, 3):
        whole = whole + y_shift(part, k)
    logits = whole[:, :EXPERTS] * lax.rsqrt(whole[:, EXPERTS : EXPERTS + 1] / 2048.0 + EPS)
    lifted = jax.nn.sigmoid(logits)
    onehot = jnp.sum(
        (routes[:, :, None] == jnp.arange(EXPERTS, dtype=jnp.int32)[None, None, :]).astype(f32),
        axis=1,
    )
    lifted = lifted * onehot
    gates = lifted / jnp.sum(lifted, axis=1, keepdims=True)
    gates = lax.dynamic_index_in_dim(gates.reshape(TOK, WIDE, 2), i, 2, keepdims=False).T

    moe = jnp.zeros((TOK, 512), f32)
    contract = (((0, 1), (0, 1)), ((), ()))
    for (a, b), back in zip(GROUPS, backs):
        mixing = jnp.where(chosen[:, a:b], gates[:, None, :], 0.0)
        mixing_hi = lax.reduce_precision(mixing, 8, 7)
        mixing_lo = (mixing - mixing_hi).astype(bf16)
        for matrix in (mixing_hi.astype(bf16), mixing_lo):
            moe = moe + lax.dot_general(matrix, back, contract, preferred_element_type=f32)
    moe = moe.astype(bf16)
    moe_par = x_swap(moe)
    layer, part = pl.pallas_call(
        embed_kernel,
        out_shape=(
            jax.ShapeDtypeStruct((TOK, 512), bf16),
            jax.ShapeDtypeStruct((TOK + 8, 128), f32),
        ),
        in_specs=[smem()] + [vmem()] * 5,
        out_specs=(vmem(), vmem()),
        name="embed",
    )(here, hidden, moe, moe_par, norm_gains, w_proj)
    parts = [part] + [y_shift(part, k) for k in (1, 2, 3)]

    vectors = pl.pallas_call(
        vector_kernel,
        out_shape=jax.ShapeDtypeStruct((16, TOK, 128), bf16),
        in_specs=[vmem()] * 4,
        out_specs=vmem(),
        name="vectors",
    )(*parts)
    vectors, layer = lax.optimization_barrier((vectors, layer))
    layers = [layer] + [y_shift(layer, k) for k in (1, 2, 3)]
    own = lax.all_to_all(vectors, ("z", "xl"), 0, 0, tiled=True).reshape(16 * TOK, 128)
    segment = doc_segment[0]
    requests = doc_request[0]
    docs = jnp.arange(16, dtype=jnp.int32)
    first = jnp.sum((segment[None, :] < docs[:, None]).astype(jnp.int32), axis=1)
    size = jnp.sum((segment[None, :] == docs[:, None]).astype(jnp.int32), axis=1)
    starts = jnp.cumsum(request_lengths, axis=1) - request_lengths
    starts = (starts + TOK * (jnp.arange(WIDE, dtype=jnp.int32) // 2)[:, None]).reshape(-1)
    match = requests[:, None] == jnp.arange(96, dtype=jnp.int32)[None, :]
    q_first = jnp.sum(jnp.where(match, starts[None, :], 0), axis=1)
    q_size = jnp.sum(jnp.where(match, request_lengths.reshape(-1)[None, :], 0), axis=1)
    away = lax.rem(requests // 3, 2) ^ core
    info = jnp.stack([first, size, q_first, q_size, away])
    own, info, *layers = lax.optimization_barrier((own, info, *layers))
    other = lax.ppermute(own, "core", [(0, 1), (1, 0)])
    layer_out = pl.pallas_call(
        assemble_kernel,
        out_shape=jax.ShapeDtypeStruct((TOK, 2048), bf16),
        in_specs=[smem()] + [vmem()] * 4,
        out_specs=vmem(),
        name="assemble",
    )(here, *layers)
    doc_scores = pl.pallas_call(
        score_kernel,
        out_shape=jax.ShapeDtypeStruct((1, 16), f32),
        in_specs=[smem(), vmem(), hbm(), hbm()],
        out_specs=vmem(),
        scratch_shapes=[pltpu.VMEM((16, 128, 128), bf16), pltpu.SemaphoreType.DMA((16,))],
        name="score",
    )(info, doc_vectors, own, other)
    return (layer_out, doc_scores)


def solution(mesh):
    split = Mesh(mesh.devices.reshape(8, 2, 2, 2, 4), ("z", "xl", "core", "xh", "y"))
    placed = (
        P(W, None),
        P(),
        P(None, None, N),
        P(None, N),
        P(N, None),
        P(),
        P(),
        P(W, None),
        P(W, None, N),
        P(W, None, N),
        P(W, N, None),
        P(),
        P(W + N, None),
        P(W + N, None),
        P(W + N, None),
    )
    return jax.shard_map(
        body,
        mesh=split,
        in_specs=placed,
        out_specs=(P(W, None), P(W + N, None)),
        check_vma=False,
    )
```

```python
import math

import jax
import jax.numpy as jnp
from jax import lax
from jax.experimental import pallas as pl
from jax.experimental.pallas import tpu as pltpu
from jax.sharding import Mesh, PartitionSpec as P

HD = 128
TOPK = 8
TOK = 128
CAP = 20
EXPERTS = 64
WIDE = 32
GROUPS = ((0, 8), (8, 20))
EPS = 1e-06
THETA = 50000.0
NEG = -1e30
W = ("z", "xl", "core")
N = ("xh", "y")
f32 = jnp.float32
bf16 = jnp.bfloat16


def y_shift(x, k):
    return lax.ppermute(x, "y", [(s, (s + k) % 4) for s in range(4)])


def x_swap(x):
    return lax.ppermute(x, "xh", [(0, 1), (1, 0)])


def attention_kernel(
    here_ref,
    lengths_ref,
    qk_ref,
    gain_ref,
    x_hbm,
    w_hbm,
    out_hbm,
    out0,
    out1,
    out2,
    out3,
    x_ref,
    w_ref,
    out_w_ref,
    sems,
):
    copies = [pltpu.make_async_copy(x_hbm, x_ref, sems.at[0])]
    copies += [
        pltpu.make_async_copy(w_hbm.at[part], w_ref.at[part], sems.at[1 + part]) for part in range(3)
    ]
    copies += [pltpu.make_async_copy(out_hbm, out_w_ref, sems.at[4])]
    for copy in copies:
        copy.start()
    wide = here_ref[2]
    one = lengths_ref[0, wide]
    two = one + lengths_ref[1, wide]

    def member_of(places):
        return (places >= one).astype(jnp.int32) + (places >= two).astype(jnp.int32)

    down_places = lax.broadcasted_iota(jnp.int32, (TOK, HD), 0)
    across_places = lax.broadcasted_iota(jnp.int32, (TOK, HD), 1)
    member = member_of(down_places)
    same = member == member_of(across_places)
    start = jnp.where(member == 0, 0, jnp.where(member == 1, one, two))
    half = lax.rem(across_places, HD // 2).astype(f32)
    freq = jnp.exp(half * (-math.log(THETA) / (HD // 2)))
    angle = (down_places - start).astype(f32) * freq
    cosine = jnp.cos(angle)
    sine = jnp.sin(angle)
    sine = jnp.where(across_places < HD // 2, -sine, sine)

    copies[0].wait()
    x = x_ref[...].astype(f32)
    scale = lax.rsqrt(jnp.mean(x * x, axis=1, keepdims=True) + EPS)
    normed = (x * scale * gain_ref[0:1, :]).astype(bf16)
    parts = []
    for part in range(3):
        copies[1 + part].wait()
        parts.append(jnp.dot(normed, w_ref[part], preferred_element_type=f32))
    query, keys, values = parts

    def turned(v, gain):
        v = v * lax.rsqrt(jnp.mean(v * v, axis=1, keepdims=True) + EPS) * gain
        return (v * cosine + pltpu.roll(v, HD // 2, 1) * sine).astype(bf16)

    mixed = []
    for head in range(2):
        at = slice(head * HD, (head + 1) * HD)
        q = turned(query[:, at], qk_ref[0:1, at])
        k = turned(keys[:, at], qk_ref[1:2, at])
        scores = lax.dot_general(q, k, (((1,), (1,)), ((), ())), preferred_element_type=f32)
        scores = jnp.where(same, scores * HD ** (-0.5), NEG)
        weights = jnp.exp(scores - jnp.max(scores, axis=1, keepdims=True))
        probs = (weights / jnp.sum(weights, axis=1, keepdims=True)).astype(bf16)
        mixed.append(
            jnp.dot(probs, values[:, at].astype(bf16), preferred_element_type=f32).astype(bf16)
        )
    mixed = jnp.concatenate(mixed, axis=1)
    copies[4].wait()
    j = here_ref[1]
    for k, out_ref in enumerate((out0, out1, out2, out3)):
        part = lax.rem(j + k, 4)
        columns = pl.ds(pl.multiple_of(part * 512, 512), 512)
        out_ref[...] = jnp.dot(mixed, out_w_ref[:, columns], preferred_element_type=f32).astype(bf16)


def choose_kernel(here_ref, routes_ref, *out_refs):
    expert = 2 * lax.broadcasted_iota(jnp.int32, (WIDE, TOK), 0) + here_ref[0]
    hit = jnp.zeros((WIDE, TOK), f32)
    for k in range(TOPK):
        hit = hit + (routes_ref[k : k + 1, :] == expert).astype(f32)
    sooner = lax.broadcasted_iota(jnp.int32, (TOK, TOK), 0)
    earlier = (sooner < lax.broadcasted_iota(jnp.int32, (TOK, TOK), 1)).astype(f32).astype(bf16)
    before = jnp.dot(hit.astype(bf16), earlier, preferred_element_type=f32)
    place = jnp.where(hit > 0, before, -1.0).astype(bf16)
    for (a, b), out_ref in zip(GROUPS, out_refs):
        size = b - a
        owner = size * lax.broadcasted_iota(jnp.int32, (WIDE * size, WIDE), 1)
        offset = lax.broadcasted_iota(jnp.int32, (WIDE * size, WIDE), 0) - owner
        inside = (offset >= 0) & (offset < size)
        spread = jnp.dot(
            inside.astype(f32).astype(bf16), place, preferred_element_type=f32
        )
        slot = jnp.sum(jnp.where(inside, offset + a, 0).astype(f32), axis=1, keepdims=True)
        out_ref[...] = (spread == slot).astype(f32).astype(bf16)


def dispatch_kernel(here_ref, x_ref, own_ref, par_ref, *refs):
    chooses = refs[: len(GROUPS)]
    hidden_ref = refs[len(GROUPS)]
    j = here_ref[1]
    mine = x_ref[:, pl.ds(pl.multiple_of(j * 512, 512), 512)].astype(f32)
    hidden = (mine + (own_ref[...].astype(f32) + par_ref[...].astype(f32))).astype(bf16)
    hidden_ref[...] = hidden
    for choose_ref, rows_ref in zip(chooses, refs[len(GROUPS) + 1 :]):
        rows = jnp.dot(choose_ref[...], hidden, preferred_element_type=f32)
        size = rows_ref.shape[1]
        for s in range(WIDE):
            rows_ref[s] = rows[s * size : (s + 1) * size].astype(bf16)


def gate_up_kernel(
    here_ref, x0, x1, x2, x3, gain_ref, gate_hbm, up_hbm, gate_par, up_par, out_ref, w_ref, sems
):
    i, j = here_ref[0], here_ref[1]
    sources = (gate_hbm.at[i], up_hbm.at[i], gate_par, up_par)
    copies = [
        pltpu.make_async_copy(source, w_ref.at[n], sems.at[n]) for n, source in enumerate(sources)
    ]
    for copy in copies:
        copy.start()
    xs = (x0, x1, x2, x3)
    total = jnp.zeros((x0.shape[0], 1), f32)
    for x in xs:
        v = x[...].astype(f32)
        total = total + jnp.sum(v * v, axis=1, keepdims=True)
    scale = lax.rsqrt(total / 2048.0 + EPS)
    for copy in copies:
        copy.wait()
    own = jnp.zeros((x0.shape[0], 256), f32)
    par = jnp.zeros((x0.shape[0], 256), f32)
    for k, x in enumerate(xs):
        part = lax.rem(j - k + 4, 4)
        rows = pl.ds(pl.multiple_of(part * 512, 512), 512)
        normed = (x[...].astype(f32) * scale * gain_ref[1:2, rows]).astype(bf16)
        w_own = jnp.concatenate([w_ref[0, rows, :], w_ref[1, rows, :]], axis=1)
        w_par = jnp.concatenate([w_ref[2, rows, :], w_ref[3, rows, :]], axis=1)
        own = own + jnp.dot(normed, w_own, preferred_element_type=f32)
        par = par + jnp.dot(normed, w_par, preferred_element_type=f32)
    for at, both in ((0, own), (128, par)):
        gate, up = both[:, :128], both[:, 128:]
        out_ref[:, at : at + 128] = (gate / (1.0 + jnp.exp(-gate)) * up).astype(bf16)


def down_kernel(here_ref, a0, a1, a2, a3, w0, w1, w2, w3, par_ref, out_ref, w_ref, sems):
    i = here_ref[0]
    copies = []
    for k, w in enumerate((w0, w1, w2, w3)):
        copies.append(
            (
                pltpu.make_async_copy(w.at[i], w_ref.at[k, 0:128], sems.at[0, k]),
                pltpu.make_async_copy(par_ref.at[k], w_ref.at[k, 128:256], sems.at[1, k]),
            )
        )
    for pair in copies:
        for copy in pair:
            copy.start()
    total = jnp.zeros((a0.shape[0], 512), f32)
    for k, a in enumerate((a0, a1, a2, a3)):
        for copy in copies[k]:
            copy.wait()
        total = total + jnp.dot(a[...], w_ref[k], preferred_element_type=f32)
    size = out_ref.shape[1]
    for s in range(WIDE):
        out_ref[s] = total[s * size : (s + 1) * size].astype(bf16)


def embed_kernel(here_ref, hidden_ref, moe_ref, par_ref, gain_ref, w_ref, layer_ref, part_ref):
    mine = pl.ds(pl.multiple_of(here_ref[1] * 512, 512), 512)
    layer = hidden_ref[...].astype(f32) + (moe_ref[...].astype(f32) + par_ref[...].astype(f32))
    layer = layer.astype(bf16)
    layer_ref[...] = layer
    layer = layer.astype(f32)
    scaled = (layer * gain_ref[2:3, mine]).astype(bf16)
    part_ref[0:TOK, :] = jnp.dot(scaled, w_ref[mine, :], preferred_element_type=f32)
    square = jnp.broadcast_to(jnp.sum(layer * layer, axis=1, keepdims=True), (TOK, TOK))
    part_ref[TOK:, :] = jnp.transpose(square)[0:8]


def vector_kernel(p0, p1, p2, p3, out_ref):
    whole = p0[...] + p1[...] + p2[...] + p3[...]
    square = jnp.transpose(jnp.broadcast_to(whole[TOK : TOK + 1], (TOK, TOK)))
    embedded = whole[0:TOK] * lax.rsqrt(square / 2048.0 + EPS)
    norm = jnp.sum(embedded * embedded, axis=1, keepdims=True)
    vectors = (embedded * lax.rsqrt(norm + EPS)).astype(bf16)
    for copy in range(16):
        out_ref[copy] = vectors


def assemble_kernel(here_ref, p0, p1, p2, p3, out_ref):
    j = here_ref[1]
    for k, piece in enumerate((p0, p1, p2, p3)):
        part = lax.rem(j - k + 4, 4)
        out_ref[:, pl.ds(pl.multiple_of(part * 512, 512), 512)] = piece[...]


def score_kernel(info_ref, doc_ref, own_ref, other_ref, out_ref, query_ref, sems):
    def spot(d):
        return pl.multiple_of(jnp.minimum((info_ref[2, d] // 16) * 16, 2048 - 128), 16)

    def copy_of(ref, d):
        return pltpu.make_async_copy(ref.at[pl.ds(spot(d), 128), :], query_ref.at[d], sems.at[d])

    for d in range(16):

        @pl.when(info_ref[4, d] == 0)
        def _():
            copy_of(own_ref, d).start()

        @pl.when(info_ref[4, d] != 0)
        def _():
            copy_of(other_ref, d).start()

    lane = lax.broadcasted_iota(jnp.int32, (1, 16), 1)
    scores = jnp.zeros((1, 16), f32)
    rows = lax.broadcasted_iota(jnp.int32, (144, 128), 0)
    columns = lax.broadcasted_iota(jnp.int32, (1, 128), 1)
    for d in range(16):
        copy_of(own_ref, d).wait()
    for d in range(16):
        first, size = info_ref[0, d], info_ref[1, d]
        q_first, q_size = info_ref[2, d], info_ref[3, d]
        at = pl.multiple_of(jnp.minimum((first // 16) * 16, 1024 - 144), 16)
        sims = lax.dot_general(
            doc_ref[pl.ds(at, 144), :],
            query_ref[d],
            (((1,), (1,)), ((), ())),
            preferred_element_type=f32,
        )
        keep = (rows >= first - at) & (rows < first - at + size)
        best = jnp.max(jnp.where(keep, sims, NEG), axis=0, keepdims=True)
        q_start = q_first - spot(d)
        used = (columns >= q_start) & (columns < q_start + q_size)
        value = jnp.sum(jnp.where(used, best, 0.0), axis=1, keepdims=True) / q_size.astype(f32)
        scores = jnp.where(lane == d, value, scores)
    out_ref[...] = scores


def vmem():
    return pl.BlockSpec(memory_space=pltpu.VMEM)


def smem():
    return pl.BlockSpec(memory_space=pltpu.SMEM)


def hbm():
    return pl.BlockSpec(memory_space=pltpu.HBM)


def params():
    return pltpu.CompilerParams(vmem_limit_bytes=40 << 20)


def body(
    tokens,
    request_lengths,
    w_qkv,
    qk_gain,
    w_out,
    norm_gains,
    w_router,
    routes,
    w_gate,
    w_up,
    w_down,
    w_proj,
    doc_vectors,
    doc_segment,
    doc_request,
):
    i = lax.axis_index("xh")
    j = lax.axis_index("y")
    core = lax.axis_index("core")
    wide = lax.axis_index(W)
    here = jnp.stack([i, j, wide, core])

    def pick(array, which):
        return lax.dynamic_index_in_dim(array, which, 0, keepdims=False)

    def cut(array, part, axis):
        return lax.dynamic_slice_in_dim(array, lax.rem(part, 4) * 512, 512, axis)

    attn = pl.pallas_call(
        attention_kernel,
        out_shape=(jax.ShapeDtypeStruct((TOK, 512), bf16),) * 4,
        in_specs=[smem()] * 2 + [vmem()] * 2 + [hbm()] * 3,
        out_specs=(vmem(),) * 4,
        scratch_shapes=[
            pltpu.VMEM((TOK, 2048), bf16),
            pltpu.VMEM((3, 2048, 256), bf16),
            pltpu.VMEM((256, 2048), bf16),
            pltpu.SemaphoreType.DMA((5,)),
        ],
        compiler_params=params(),
        name="attention",
    )(
        here,
        request_lengths.T,
        qk_gain,
        norm_gains,
        tokens,
        w_qkv.transpose(1, 0, 2),
        w_out,
    )
    attn_parts = [y_shift(attn[k], k) for k in (1, 2, 3)]

    own_part, w_gate, w_up = lax.optimization_barrier((attn[0], w_gate, w_up))
    gate_par = x_swap(pick(w_gate, 1 - i))
    up_par = x_swap(pick(w_up, 1 - i))
    downs = [cut(w_down, j, 2)] + [y_shift(cut(w_down, j + k, 2), k) for k in (1, 2, 3)]
    down_par = x_swap(jnp.stack([pick(d, 1 - i) for d in downs]))

    experts_here = 2 * jnp.arange(WIDE, dtype=jnp.int32) + i
    hit = jnp.sum((routes.T[None, :, :] == experts_here[:, None, None]).astype(f32), axis=1)
    places = jnp.arange(TOK, dtype=jnp.int32)
    earlier = (places[:, None] < places[None, :]).astype(bf16)
    before = jnp.dot(hit.astype(bf16), earlier, preferred_element_type=f32)
    slot = jnp.arange(CAP, dtype=jnp.int32).astype(f32)
    chosen = (before[:, None, :] == slot[None, :, None]) & (hit[:, None, :] > 0)
    chooses = pl.pallas_call(
        choose_kernel,
        out_shape=tuple(jax.ShapeDtypeStruct((WIDE * (b - a), TOK), bf16) for a, b in GROUPS),
        in_specs=[smem(), vmem()],
        out_specs=(vmem(),) * len(GROUPS),
        compiler_params=params(),
        name="choose",
    )(here, routes.T)

    attn = (own_part.astype(f32) + sum(p.astype(f32) for p in attn_parts)).astype(bf16)
    attn, *chooses = lax.optimization_barrier((attn, *chooses))
    attn_par = x_swap(attn)
    attn_par, gate_par = lax.optimization_barrier((attn_par, gate_par))
    hidden, *rows = pl.pallas_call(
        dispatch_kernel,
        out_shape=(
            jax.ShapeDtypeStruct((TOK, 512), bf16),
            *(jax.ShapeDtypeStruct((WIDE, b - a, 512), bf16) for a, b in GROUPS),
        ),
        in_specs=[smem()] + [vmem()] * (3 + len(GROUPS)),
        out_specs=(vmem(),) * (1 + len(GROUPS)),
        compiler_params=params(),
        name="dispatch",
    )(here, tokens, attn, attn_par, *chooses)

    backs = []
    arrived = []
    for g, group in enumerate(rows):
        if arrived:
            group, arrived[-1] = lax.optimization_barrier((group, arrived[-1]))
        arrived.append(lax.all_to_all(group, W, 0, 0, tiled=True))
    for g, x in enumerate(arrived):
        size = x.shape[1]
        x = x.reshape(WIDE * size, 512)
        if g == 0:
            x, up_par = lax.optimization_barrier((x, up_par))
        act = pl.pallas_call(
            gate_up_kernel,
            out_shape=jax.ShapeDtypeStruct((WIDE * size, 256), bf16),
            in_specs=[smem()] + [vmem()] * 5 + [hbm()] * 4,
            out_specs=vmem(),
            scratch_shapes=[pltpu.VMEM((4, 2048, 128), bf16), pltpu.SemaphoreType.DMA((4,))],
            compiler_params=params(),
            name="gate_up",
        )(here, x, *(y_shift(x, k) for k in (1, 2, 3)), norm_gains, w_gate, w_up, gate_par, up_par)
        if g == 0:
            act, down_par = lax.optimization_barrier((act, down_par))
        out = pl.pallas_call(
            down_kernel,
            out_shape=jax.ShapeDtypeStruct((WIDE, size, 512), bf16),
            in_specs=[smem()] + [vmem()] * 4 + [hbm()] * 5,
            out_specs=vmem(),
            scratch_shapes=[pltpu.VMEM((4, 256, 512), bf16), pltpu.SemaphoreType.DMA((2, 4))],
            compiler_params=params(),
            name="down",
        )(here, act, *(y_shift(act, k) for k in (1, 2, 3)), *downs, down_par)
        backs.append(lax.all_to_all(out, W, 0, 0, tiled=True))

    hf = hidden.astype(f32)
    gain_mine = lax.dynamic_slice_in_dim(norm_gains[1], j * 512, 512, 0)
    router_mine = lax.dynamic_slice_in_dim(w_router, j * 512, 512, 0)
    part = jnp.dot((hf * gain_mine).astype(bf16), router_mine, preferred_element_type=f32)
    square = jnp.sum(hf * hf, axis=1, keepdims=True)
    part = jnp.concatenate([part, jnp.broadcast_to(square, (TOK, EXPERTS))], axis=1)
    whole = part
    for k in (1, 2, 3):
        whole = whole + y_shift(part, k)
    logits = whole[:, :EXPERTS] * lax.rsqrt(whole[:, EXPERTS : EXPERTS + 1] / 2048.0 + EPS)
    lifted = jax.nn.sigmoid(logits)
    onehot = jnp.sum(
        (routes[:, :, None] == jnp.arange(EXPERTS, dtype=jnp.int32)[None, None, :]).astype(f32),
        axis=1,
    )
    lifted = lifted * onehot
    gates = lifted / jnp.sum(lifted, axis=1, keepdims=True)
    gates = lax.dynamic_index_in_dim(gates.reshape(TOK, WIDE, 2), i, 2, keepdims=False).T

    moe = jnp.zeros((TOK, 512), f32)
    contract = (((0, 1), (0, 1)), ((), ()))
    for (a, b), back in zip(GROUPS, backs):
        mixing = jnp.where(chosen[:, a:b], gates[:, None, :], 0.0)
        mixing_hi = lax.reduce_precision(mixing, 8, 7)
        mixing_lo = (mixing - mixing_hi).astype(bf16)
        for matrix in (mixing_hi.astype(bf16), mixing_lo):
            moe = moe + lax.dot_general(matrix, back, contract, preferred_element_type=f32)
    moe = moe.astype(bf16)
    moe_par = x_swap(moe)
    layer, part = pl.pallas_call(
        embed_kernel,
        out_shape=(
            jax.ShapeDtypeStruct((TOK, 512), bf16),
            jax.ShapeDtypeStruct((TOK + 8, 128), f32),
        ),
        in_specs=[smem()] + [vmem()] * 5,
        out_specs=(vmem(), vmem()),
        name="embed",
    )(here, hidden, moe, moe_par, norm_gains, w_proj)
    parts = [part] + [y_shift(part, k) for k in (1, 2, 3)]

    vectors = pl.pallas_call(
        vector_kernel,
        out_shape=jax.ShapeDtypeStruct((16, TOK, 128), bf16),
        in_specs=[vmem()] * 4,
        out_specs=vmem(),
        name="vectors",
    )(*parts)
    vectors, layer = lax.optimization_barrier((vectors, layer))
    layers = [layer] + [y_shift(layer, k) for k in (1, 2, 3)]
    own = lax.all_to_all(vectors, ("z", "xl"), 0, 0, tiled=True).reshape(16 * TOK, 128)
    segment = doc_segment[0]
    requests = doc_request[0]
    docs = jnp.arange(16, dtype=jnp.int32)
    first = jnp.sum((segment[None, :] < docs[:, None]).astype(jnp.int32), axis=1)
    size = jnp.sum((segment[None, :] == docs[:, None]).astype(jnp.int32), axis=1)
    starts = jnp.cumsum(request_lengths, axis=1) - request_lengths
    starts = (starts + TOK * (jnp.arange(WIDE, dtype=jnp.int32) // 2)[:, None]).reshape(-1)
    match = requests[:, None] == jnp.arange(96, dtype=jnp.int32)[None, :]
    q_first = jnp.sum(jnp.where(match, starts[None, :], 0), axis=1)
    q_size = jnp.sum(jnp.where(match, request_lengths.reshape(-1)[None, :], 0), axis=1)
    away = lax.rem(requests // 3, 2) ^ core
    info = jnp.stack([first, size, q_first, q_size, away])
    own, info, *layers = lax.optimization_barrier((own, info, *layers))
    other = lax.ppermute(own, "core", [(0, 1), (1, 0)])
    layer_out = pl.pallas_call(
        assemble_kernel,
        out_shape=jax.ShapeDtypeStruct((TOK, 2048), bf16),
        in_specs=[smem()] + [vmem()] * 4,
        out_specs=vmem(),
        name="assemble",
    )(here, *layers)
    doc_scores = pl.pallas_call(
        score_kernel,
        out_shape=jax.ShapeDtypeStruct((1, 16), f32),
        in_specs=[smem(), vmem(), hbm(), hbm()],
        out_specs=vmem(),
        scratch_shapes=[pltpu.VMEM((16, 128, 128), bf16), pltpu.SemaphoreType.DMA((16,))],
        name="score",
    )(info, doc_vectors, own, other)
    return (layer_out, doc_scores)


def solution(mesh):
    split = Mesh(mesh.devices.reshape(8, 2, 2, 2, 4), ("z", "xl", "core", "xh", "y"))
    placed = (
        P(W, None),
        P(),
        P(None, None, N),
        P(None, N),
        P(N, None),
        P(),
        P(),
        P(W, None),
        P(W, None, N),
        P(W, None, N),
        P(W, N, None),
        P(),
        P(W + N, None),
        P(W + N, None),
        P(W + N, None),
    )
    return jax.shard_map(
        body,
        mesh=split,
        in_specs=placed,
        out_specs=(P(W, None), P(W + N, None)),
        check_vma=False,
    )
```

```python
import math

import jax
import jax.numpy as jnp
from jax import lax
from jax.experimental import pallas as pl
from jax.experimental.pallas import tpu as pltpu
from jax.sharding import Mesh, PartitionSpec as P

HD = 128
TOPK = 8
TOK = 128
CAP = 20
EXPERTS = 64
WIDE = 32
GROUPS = ((0, 20),)
SPLIT = ((0, 20),)
EPS = 1e-06
THETA = 50000.0
NEG = -1e30
W = ("z", "xl", "core")
N = ("xh", "y")
f32 = jnp.float32
bf16 = jnp.bfloat16


def y_shift(x, k):
    return lax.ppermute(x, "y", [(s, (s + k) % 4) for s in range(4)])


def x_swap(x):
    return lax.ppermute(x, "xh", [(0, 1), (1, 0)])


def attention_kernel(
    here_ref,
    lengths_ref,
    qk_ref,
    gain_ref,
    x_hbm,
    w_hbm,
    out_hbm,
    out0,
    out1,
    out2,
    out3,
    x_ref,
    w_ref,
    out_w_ref,
    sems,
):
    copies = [pltpu.make_async_copy(x_hbm, x_ref, sems.at[0])]
    copies += [
        pltpu.make_async_copy(w_hbm.at[part], w_ref.at[part], sems.at[1 + part]) for part in range(3)
    ]
    copies += [pltpu.make_async_copy(out_hbm, out_w_ref, sems.at[4])]
    for copy in copies:
        copy.start()
    wide = here_ref[2]
    one = lengths_ref[0, wide]
    two = one + lengths_ref[1, wide]

    def member_of(places):
        return (places >= one).astype(jnp.int32) + (places >= two).astype(jnp.int32)

    down_places = lax.broadcasted_iota(jnp.int32, (TOK, HD), 0)
    across_places = lax.broadcasted_iota(jnp.int32, (TOK, HD), 1)
    member = member_of(down_places)
    same = member == member_of(across_places)
    start = jnp.where(member == 0, 0, jnp.where(member == 1, one, two))
    half = lax.rem(across_places, HD // 2).astype(f32)
    freq = jnp.exp(half * (-math.log(THETA) / (HD // 2)))
    angle = (down_places - start).astype(f32) * freq
    cosine = jnp.cos(angle)
    sine = jnp.sin(angle)
    sine = jnp.where(across_places < HD // 2, -sine, sine)

    copies[0].wait()
    x = x_ref[...].astype(f32)
    scale = lax.rsqrt(jnp.mean(x * x, axis=1, keepdims=True) + EPS)
    normed = (x * scale * gain_ref[0:1, :]).astype(bf16)
    parts = []
    for part in range(3):
        copies[1 + part].wait()
        parts.append(jnp.dot(normed, w_ref[part], preferred_element_type=f32))
    query, keys, values = parts

    def turned(v, gain):
        v = v * lax.rsqrt(jnp.mean(v * v, axis=1, keepdims=True) + EPS) * gain
        return (v * cosine + pltpu.roll(v, HD // 2, 1) * sine).astype(bf16)

    mixed = []
    for head in range(2):
        at = slice(head * HD, (head + 1) * HD)
        q = turned(query[:, at], qk_ref[0:1, at])
        k = turned(keys[:, at], qk_ref[1:2, at])
        scores = lax.dot_general(q, k, (((1,), (1,)), ((), ())), preferred_element_type=f32)
        scores = jnp.where(same, scores * HD ** (-0.5), NEG)
        weights = jnp.exp(scores - jnp.max(scores, axis=1, keepdims=True))
        probs = (weights / jnp.sum(weights, axis=1, keepdims=True)).astype(bf16)
        mixed.append(
            jnp.dot(probs, values[:, at].astype(bf16), preferred_element_type=f32).astype(bf16)
        )
    mixed = jnp.concatenate(mixed, axis=1)
    copies[4].wait()
    j = here_ref[1]
    for k, out_ref in enumerate((out0, out1, out2, out3)):
        part = lax.rem(j + k, 4)
        columns = pl.ds(pl.multiple_of(part * 512, 512), 512)
        out_ref[...] = jnp.dot(mixed, out_w_ref[:, columns], preferred_element_type=f32).astype(bf16)


def choose_kernel(here_ref, routes_ref, *out_refs):
    expert = 2 * lax.broadcasted_iota(jnp.int32, (WIDE, TOK), 0) + here_ref[0]
    hit = jnp.zeros((WIDE, TOK), f32)
    for k in range(TOPK):
        hit = hit + (routes_ref[k : k + 1, :] == expert).astype(f32)
    sooner = lax.broadcasted_iota(jnp.int32, (TOK, TOK), 0)
    earlier = (sooner < lax.broadcasted_iota(jnp.int32, (TOK, TOK), 1)).astype(f32).astype(bf16)
    before = jnp.dot(hit.astype(bf16), earlier, preferred_element_type=f32)
    place = jnp.where(hit > 0, before, -1.0).astype(bf16)
    for (a, b), out_ref in zip(GROUPS, out_refs):
        size = b - a
        owner = size * lax.broadcasted_iota(jnp.int32, (WIDE * size, WIDE), 1)
        offset = lax.broadcasted_iota(jnp.int32, (WIDE * size, WIDE), 0) - owner
        inside = (offset >= 0) & (offset < size)
        spread = jnp.dot(
            inside.astype(f32).astype(bf16), place, preferred_element_type=f32
        )
        slot = jnp.sum(jnp.where(inside, offset + a, 0).astype(f32), axis=1, keepdims=True)
        out_ref[...] = (spread == slot).astype(f32).astype(bf16)


def dispatch_kernel(here_ref, x_ref, own_ref, par_ref, *refs):
    chooses = refs[: len(GROUPS)]
    hidden_ref = refs[len(GROUPS)]
    j = here_ref[1]
    mine = x_ref[:, pl.ds(pl.multiple_of(j * 512, 512), 512)].astype(f32)
    hidden = (mine + (own_ref[...].astype(f32) + par_ref[...].astype(f32))).astype(bf16)
    hidden_ref[...] = hidden
    for choose_ref, rows_ref in zip(chooses, refs[len(GROUPS) + 1 :]):
        rows = jnp.dot(choose_ref[...], hidden, preferred_element_type=f32)
        size = rows_ref.shape[1]
        for s in range(WIDE):
            rows_ref[s] = rows[s * size : (s + 1) * size].astype(bf16)


def gate_up_kernel(
    here_ref, x0, x1, x2, x3, gain_ref, gate_hbm, up_hbm, gate_par, up_par, out_ref, w_ref, sems
):
    i, j = here_ref[0], here_ref[1]
    sources = (gate_hbm.at[i], up_hbm.at[i], gate_par, up_par)
    copies = [
        pltpu.make_async_copy(source, w_ref.at[n], sems.at[n]) for n, source in enumerate(sources)
    ]
    for copy in copies:
        copy.start()
    xs = (x0, x1, x2, x3)
    total = jnp.zeros((x0.shape[0], 1), f32)
    for x in xs:
        v = x[...].astype(f32)
        total = total + jnp.sum(v * v, axis=1, keepdims=True)
    scale = lax.rsqrt(total / 2048.0 + EPS)
    for copy in copies:
        copy.wait()
    own = jnp.zeros((x0.shape[0], 256), f32)
    par = jnp.zeros((x0.shape[0], 256), f32)
    for k, x in enumerate(xs):
        part = lax.rem(j - k + 4, 4)
        rows = pl.ds(pl.multiple_of(part * 512, 512), 512)
        normed = (x[...].astype(f32) * scale * gain_ref[1:2, rows]).astype(bf16)
        w_own = jnp.concatenate([w_ref[0, rows, :], w_ref[1, rows, :]], axis=1)
        w_par = jnp.concatenate([w_ref[2, rows, :], w_ref[3, rows, :]], axis=1)
        own = own + jnp.dot(normed, w_own, preferred_element_type=f32)
        par = par + jnp.dot(normed, w_par, preferred_element_type=f32)
    for at, both in ((0, own), (128, par)):
        gate, up = both[:, :128], both[:, 128:]
        out_ref[:, at : at + 128] = (gate / (1.0 + jnp.exp(-gate)) * up).astype(bf16)


def down_kernel(here_ref, a0, a1, a2, a3, w0, w1, w2, w3, par_ref, out_ref, w_ref, sems):
    i = here_ref[0]
    copies = []
    for k, w in enumerate((w0, w1, w2, w3)):
        copies.append(
            (
                pltpu.make_async_copy(w.at[i], w_ref.at[k, 0:128], sems.at[0, k]),
                pltpu.make_async_copy(par_ref.at[k], w_ref.at[k, 128:256], sems.at[1, k]),
            )
        )
    for pair in copies:
        for copy in pair:
            copy.start()
    total = jnp.zeros((a0.shape[0], 512), f32)
    for k, a in enumerate((a0, a1, a2, a3)):
        for copy in copies[k]:
            copy.wait()
        total = total + jnp.dot(a[...], w_ref[k], preferred_element_type=f32)
    size = out_ref.shape[1]
    for s in range(WIDE):
        out_ref[s] = total[s * size : (s + 1) * size].astype(bf16)


def embed_kernel(here_ref, hidden_ref, moe_ref, par_ref, gain_ref, w_ref, layer_ref, part_ref):
    mine = pl.ds(pl.multiple_of(here_ref[1] * 512, 512), 512)
    layer = hidden_ref[...].astype(f32) + (moe_ref[...].astype(f32) + par_ref[...].astype(f32))
    layer = layer.astype(bf16)
    layer_ref[...] = layer
    layer = layer.astype(f32)
    scaled = (layer * gain_ref[2:3, mine]).astype(bf16)
    part_ref[0:TOK, :] = jnp.dot(scaled, w_ref[mine, :], preferred_element_type=f32)
    square = jnp.broadcast_to(jnp.sum(layer * layer, axis=1, keepdims=True), (TOK, TOK))
    part_ref[TOK:, :] = jnp.transpose(square)[0:8]


def vector_kernel(p0, p1, p2, p3, out_ref):
    whole = p0[...] + p1[...] + p2[...] + p3[...]
    square = jnp.transpose(jnp.broadcast_to(whole[TOK : TOK + 1], (TOK, TOK)))
    embedded = whole[0:TOK] * lax.rsqrt(square / 2048.0 + EPS)
    norm = jnp.sum(embedded * embedded, axis=1, keepdims=True)
    vectors = (embedded * lax.rsqrt(norm + EPS)).astype(bf16)
    for copy in range(16):
        out_ref[copy] = vectors


def assemble_kernel(here_ref, p0, p1, p2, p3, out_ref):
    j = here_ref[1]
    for k, piece in enumerate((p0, p1, p2, p3)):
        part = lax.rem(j - k + 4, 4)
        out_ref[:, pl.ds(pl.multiple_of(part * 512, 512), 512)] = piece[...]


def score_kernel(info_ref, doc_ref, own_ref, other_ref, out_ref, query_ref, sems):
    def spot(d):
        return pl.multiple_of(jnp.minimum((info_ref[2, d] // 16) * 16, 2048 - 128), 16)

    def copy_of(ref, d):
        return pltpu.make_async_copy(ref.at[pl.ds(spot(d), 128), :], query_ref.at[d], sems.at[d])

    for d in range(16):

        @pl.when(info_ref[4, d] == 0)
        def _():
            copy_of(own_ref, d).start()

        @pl.when(info_ref[4, d] != 0)
        def _():
            copy_of(other_ref, d).start()

    lane = lax.broadcasted_iota(jnp.int32, (1, 16), 1)
    scores = jnp.zeros((1, 16), f32)
    rows = lax.broadcasted_iota(jnp.int32, (144, 128), 0)
    columns = lax.broadcasted_iota(jnp.int32, (1, 128), 1)
    for d in range(16):
        copy_of(own_ref, d).wait()
    for d in range(16):
        first, size = info_ref[0, d], info_ref[1, d]
        q_first, q_size = info_ref[2, d], info_ref[3, d]
        at = pl.multiple_of(jnp.minimum((first // 16) * 16, 1024 - 144), 16)
        sims = lax.dot_general(
            doc_ref[pl.ds(at, 144), :],
            query_ref[d],
            (((1,), (1,)), ((), ())),
            preferred_element_type=f32,
        )
        keep = (rows >= first - at) & (rows < first - at + size)
        best = jnp.max(jnp.where(keep, sims, NEG), axis=0, keepdims=True)
        q_start = q_first - spot(d)
        used = (columns >= q_start) & (columns < q_start + q_size)
        value = jnp.sum(jnp.where(used, best, 0.0), axis=1, keepdims=True) / q_size.astype(f32)
        scores = jnp.where(lane == d, value, scores)
    out_ref[...] = scores


def vmem():
    return pl.BlockSpec(memory_space=pltpu.VMEM)


def smem():
    return pl.BlockSpec(memory_space=pltpu.SMEM)


def hbm():
    return pl.BlockSpec(memory_space=pltpu.HBM)


def params():
    return pltpu.CompilerParams(vmem_limit_bytes=40 << 20)


def body(
    tokens,
    request_lengths,
    w_qkv,
    qk_gain,
    w_out,
    norm_gains,
    w_router,
    routes,
    w_gate,
    w_up,
    w_down,
    w_proj,
    doc_vectors,
    doc_segment,
    doc_request,
):
    i = lax.axis_index("xh")
    j = lax.axis_index("y")
    core = lax.axis_index("core")
    wide = lax.axis_index(W)
    here = jnp.stack([i, j, wide, core])

    def pick(array, which):
        return lax.dynamic_index_in_dim(array, which, 0, keepdims=False)

    def cut(array, part, axis):
        return lax.dynamic_slice_in_dim(array, lax.rem(part, 4) * 512, 512, axis)

    gate_sent, tokens = lax.optimization_barrier((pick(w_gate, 1 - i), tokens))
    gate_par = x_swap(gate_sent)

    attn = pl.pallas_call(
        attention_kernel,
        out_shape=(jax.ShapeDtypeStruct((TOK, 512), bf16),) * 4,
        in_specs=[smem()] * 2 + [vmem()] * 2 + [hbm()] * 3,
        out_specs=(vmem(),) * 4,
        scratch_shapes=[
            pltpu.VMEM((TOK, 2048), bf16),
            pltpu.VMEM((3, 2048, 256), bf16),
            pltpu.VMEM((256, 2048), bf16),
            pltpu.SemaphoreType.DMA((5,)),
        ],
        compiler_params=pltpu.CompilerParams(vmem_limit_bytes=60 << 20),
        name="attention",
    )(
        here,
        request_lengths.T,
        qk_gain,
        norm_gains,
        tokens,
        w_qkv.transpose(1, 0, 2),
        w_out,
    )
    attn_parts = [y_shift(attn[k], k) for k in (1, 2, 3)]

    up_par = x_swap(pick(w_up, 1 - i))
    downs = [cut(w_down, j, 2)] + [y_shift(cut(w_down, j + k, 2), k) for k in (1, 2, 3)]
    down_par = x_swap(jnp.stack([pick(d, 1 - i) for d in downs]))

    experts_here = 2 * jnp.arange(WIDE, dtype=jnp.int32) + i
    hit = jnp.sum((routes.T[None, :, :] == experts_here[:, None, None]).astype(f32), axis=1)
    places = jnp.arange(TOK, dtype=jnp.int32)
    earlier = (places[:, None] < places[None, :]).astype(bf16)
    before = jnp.dot(hit.astype(bf16), earlier, preferred_element_type=f32)
    slot = jnp.arange(CAP, dtype=jnp.int32).astype(f32)
    chosen = (before[:, None, :] == slot[None, :, None]) & (hit[:, None, :] > 0)
    chooses = pl.pallas_call(
        choose_kernel,
        out_shape=tuple(jax.ShapeDtypeStruct((WIDE * (b - a), TOK), bf16) for a, b in GROUPS),
        in_specs=[smem(), vmem()],
        out_specs=(vmem(),) * len(GROUPS),
        compiler_params=params(),
        name="choose",
    )(here, routes.T)

    attn = (attn[0].astype(f32) + sum(p.astype(f32) for p in attn_parts)).astype(bf16)
    attn, *chooses = lax.optimization_barrier((attn, *chooses))
    attn_par = x_swap(attn)
    attn_par, gate_par = lax.optimization_barrier((attn_par, gate_par))
    hidden, *rows = pl.pallas_call(
        dispatch_kernel,
        out_shape=(
            jax.ShapeDtypeStruct((TOK, 512), bf16),
            *(jax.ShapeDtypeStruct((WIDE, b - a, 512), bf16) for a, b in GROUPS),
        ),
        in_specs=[smem()] + [vmem()] * (3 + len(GROUPS)),
        out_specs=(vmem(),) * (1 + len(GROUPS)),
        compiler_params=params(),
        name="dispatch",
    )(here, tokens, attn, attn_par, *chooses)

    backs = []
    arrived = lax.all_to_all(rows[0], W, 0, 0, tiled=True)
    arrived, up_par = lax.optimization_barrier((arrived, up_par))
    for g, (a, b) in enumerate(SPLIT):
        size = b - a
        x = arrived[:, a:b].reshape(WIDE * size, 512)
        act = pl.pallas_call(
            gate_up_kernel,
            out_shape=jax.ShapeDtypeStruct((WIDE * size, 256), bf16),
            in_specs=[smem()] + [vmem()] * 5 + [hbm()] * 4,
            out_specs=vmem(),
            scratch_shapes=[pltpu.VMEM((4, 2048, 128), bf16), pltpu.SemaphoreType.DMA((4,))],
            compiler_params=params(),
            name="gate_up",
        )(here, x, *(y_shift(x, k) for k in (1, 2, 3)), norm_gains, w_gate, w_up, gate_par, up_par)
        if g == 0:
            act, down_par = lax.optimization_barrier((act, down_par))
        out = pl.pallas_call(
            down_kernel,
            out_shape=jax.ShapeDtypeStruct((WIDE, size, 512), bf16),
            in_specs=[smem()] + [vmem()] * 4 + [hbm()] * 5,
            out_specs=vmem(),
            scratch_shapes=[pltpu.VMEM((4, 256, 512), bf16), pltpu.SemaphoreType.DMA((2, 4))],
            compiler_params=params(),
            name="down",
        )(here, act, *(y_shift(act, k) for k in (1, 2, 3)), *downs, down_par)
        backs.append(lax.all_to_all(out, W, 0, 0, tiled=True))

    hf = hidden.astype(f32)
    gain_mine = lax.dynamic_slice_in_dim(norm_gains[1], j * 512, 512, 0)
    router_mine = lax.dynamic_slice_in_dim(w_router, j * 512, 512, 0)
    part = jnp.dot((hf * gain_mine).astype(bf16), router_mine, preferred_element_type=f32)
    square = jnp.sum(hf * hf, axis=1, keepdims=True)
    part = jnp.concatenate([part, jnp.broadcast_to(square, (TOK, EXPERTS))], axis=1)
    whole = part
    for k in (1, 2, 3):
        whole = whole + y_shift(part, k)
    logits = whole[:, :EXPERTS] * lax.rsqrt(whole[:, EXPERTS : EXPERTS + 1] / 2048.0 + EPS)
    lifted = jax.nn.sigmoid(logits)
    onehot = jnp.sum(
        (routes[:, :, None] == jnp.arange(EXPERTS, dtype=jnp.int32)[None, None, :]).astype(f32),
        axis=1,
    )
    lifted = lifted * onehot
    gates = lifted / jnp.sum(lifted, axis=1, keepdims=True)
    gates = lax.dynamic_index_in_dim(gates.reshape(TOK, WIDE, 2), i, 2, keepdims=False).T

    moe = jnp.zeros((TOK, 512), f32)
    contract = (((0, 1), (0, 1)), ((), ()))
    for (a, b), back in zip(SPLIT, backs):
        mixing = jnp.where(chosen[:, a:b], gates[:, None, :], 0.0)
        mixing_hi = lax.reduce_precision(mixing, 8, 7)
        mixing_lo = (mixing - mixing_hi).astype(bf16)
        for matrix in (mixing_hi.astype(bf16), mixing_lo):
            moe = moe + lax.dot_general(matrix, back, contract, preferred_element_type=f32)
    moe = moe.astype(bf16)
    moe_par = x_swap(moe)
    layer, part = pl.pallas_call(
        embed_kernel,
        out_shape=(
            jax.ShapeDtypeStruct((TOK, 512), bf16),
            jax.ShapeDtypeStruct((TOK + 8, 128), f32),
        ),
        in_specs=[smem()] + [vmem()] * 5,
        out_specs=(vmem(), vmem()),
        name="embed",
    )(here, hidden, moe, moe_par, norm_gains, w_proj)
    parts = [part] + [y_shift(part, k) for k in (1, 2, 3)]

    vectors = pl.pallas_call(
        vector_kernel,
        out_shape=jax.ShapeDtypeStruct((16, TOK, 128), bf16),
        in_specs=[vmem()] * 4,
        out_specs=vmem(),
        name="vectors",
    )(*parts)
    vectors, layer = lax.optimization_barrier((vectors, layer))
    layers = [layer] + [y_shift(layer, k) for k in (1, 2, 3)]
    own = lax.all_to_all(vectors, ("z", "xl"), 0, 0, tiled=True).reshape(16 * TOK, 128)
    segment = doc_segment[0]
    requests = doc_request[0]
    docs = jnp.arange(16, dtype=jnp.int32)
    first = jnp.sum((segment[None, :] < docs[:, None]).astype(jnp.int32), axis=1)
    size = jnp.sum((segment[None, :] == docs[:, None]).astype(jnp.int32), axis=1)
    starts = jnp.cumsum(request_lengths, axis=1) - request_lengths
    starts = (starts + TOK * (jnp.arange(WIDE, dtype=jnp.int32) // 2)[:, None]).reshape(-1)
    match = requests[:, None] == jnp.arange(96, dtype=jnp.int32)[None, :]
    q_first = jnp.sum(jnp.where(match, starts[None, :], 0), axis=1)
    q_size = jnp.sum(jnp.where(match, request_lengths.reshape(-1)[None, :], 0), axis=1)
    away = lax.rem(requests // 3, 2) ^ core
    info = jnp.stack([first, size, q_first, q_size, away])
    own, info, *layers = lax.optimization_barrier((own, info, *layers))
    other = lax.ppermute(own, "core", [(0, 1), (1, 0)])
    layer_out = pl.pallas_call(
        assemble_kernel,
        out_shape=jax.ShapeDtypeStruct((TOK, 2048), bf16),
        in_specs=[smem()] + [vmem()] * 4,
        out_specs=vmem(),
        name="assemble",
    )(here, *layers)
    doc_scores = pl.pallas_call(
        score_kernel,
        out_shape=jax.ShapeDtypeStruct((1, 16), f32),
        in_specs=[smem(), vmem(), hbm(), hbm()],
        out_specs=vmem(),
        scratch_shapes=[pltpu.VMEM((16, 128, 128), bf16), pltpu.SemaphoreType.DMA((16,))],
        name="score",
    )(info, doc_vectors, own, other)
    return (layer_out, doc_scores)


def solution(mesh):
    split = Mesh(mesh.devices.reshape(8, 2, 2, 2, 4), ("z", "xl", "core", "xh", "y"))
    placed = (
        P(W, None),
        P(),
        P(None, None, N),
        P(None, N),
        P(N, None),
        P(),
        P(),
        P(W, None),
        P(W, None, N),
        P(W, None, N),
        P(W, N, None),
        P(),
        P(W + N, None),
        P(W + N, None),
        P(W + N, None),
    )
    return jax.shard_map(
        body,
        mesh=split,
        in_specs=placed,
        out_specs=(P(W, None), P(W + N, None)),
        check_vma=False,
    )
```

```python
import math

import jax
import jax.numpy as jnp
from jax import lax
from jax.experimental import pallas as pl
from jax.experimental.pallas import tpu as pltpu
from jax.sharding import Mesh, PartitionSpec as P

HD = 128
TOPK = 8
TOK = 128
CAP = 20
EXPERTS = 64
WIDE = 32
GROUPS = ((0, 20),)
HALF = WIDE * CAP // 2
EPS = 1e-06
THETA = 50000.0
NEG = -1e30
W = ("z", "xl", "core")
N = ("xh", "y")
f32 = jnp.float32
bf16 = jnp.bfloat16


def y_shift(x, k):
    return lax.ppermute(x, "y", [(s, (s + k) % 4) for s in range(4)])


def x_swap(x):
    return lax.ppermute(x, "xh", [(0, 1), (1, 0)])


def attention_kernel(
    here_ref,
    lengths_ref,
    qk_ref,
    gain_ref,
    x_hbm,
    w_hbm,
    out_hbm,
    out0,
    out1,
    out2,
    out3,
    x_ref,
    w_ref,
    out_w_ref,
    sems,
):
    copies = [pltpu.make_async_copy(x_hbm, x_ref, sems.at[0])]
    copies += [
        pltpu.make_async_copy(w_hbm.at[part], w_ref.at[part], sems.at[1 + part]) for part in range(3)
    ]
    copies += [pltpu.make_async_copy(out_hbm, out_w_ref, sems.at[4])]
    for copy in copies:
        copy.start()
    wide = here_ref[2]
    one = lengths_ref[0, wide]
    two = one + lengths_ref[1, wide]

    def member_of(places):
        return (places >= one).astype(jnp.int32) + (places >= two).astype(jnp.int32)

    down_places = lax.broadcasted_iota(jnp.int32, (TOK, HD), 0)
    across_places = lax.broadcasted_iota(jnp.int32, (TOK, HD), 1)
    member = member_of(down_places)
    same = member == member_of(across_places)
    start = jnp.where(member == 0, 0, jnp.where(member == 1, one, two))
    half = lax.rem(across_places, HD // 2).astype(f32)
    freq = jnp.exp(half * (-math.log(THETA) / (HD // 2)))
    angle = (down_places - start).astype(f32) * freq
    cosine = jnp.cos(angle)
    sine = jnp.sin(angle)
    sine = jnp.where(across_places < HD // 2, -sine, sine)

    copies[0].wait()
    x = x_ref[...].astype(f32)
    scale = lax.rsqrt(jnp.mean(x * x, axis=1, keepdims=True) + EPS)
    normed = (x * scale * gain_ref[0:1, :]).astype(bf16)
    parts = []
    for part in range(3):
        copies[1 + part].wait()
        parts.append(jnp.dot(normed, w_ref[part], preferred_element_type=f32))
    query, keys, values = parts

    def turned(v, gain):
        v = v * lax.rsqrt(jnp.mean(v * v, axis=1, keepdims=True) + EPS) * gain
        return (v * cosine + pltpu.roll(v, HD // 2, 1) * sine).astype(bf16)

    mixed = []
    for head in range(2):
        at = slice(head * HD, (head + 1) * HD)
        q = turned(query[:, at], qk_ref[0:1, at])
        k = turned(keys[:, at], qk_ref[1:2, at])
        scores = lax.dot_general(q, k, (((1,), (1,)), ((), ())), preferred_element_type=f32)
        scores = jnp.where(same, scores * HD ** (-0.5), NEG)
        weights = jnp.exp(scores - jnp.max(scores, axis=1, keepdims=True))
        probs = (weights / jnp.sum(weights, axis=1, keepdims=True)).astype(bf16)
        mixed.append(
            jnp.dot(probs, values[:, at].astype(bf16), preferred_element_type=f32).astype(bf16)
        )
    mixed = jnp.concatenate(mixed, axis=1)
    copies[4].wait()
    j = here_ref[1]
    for k, out_ref in enumerate((out0, out1, out2, out3)):
        part = lax.rem(j + k, 4)
        columns = pl.ds(pl.multiple_of(part * 512, 512), 512)
        out_ref[...] = jnp.dot(mixed, out_w_ref[:, columns], preferred_element_type=f32).astype(bf16)


def choose_kernel(here_ref, routes_ref, *out_refs):
    expert = 2 * lax.broadcasted_iota(jnp.int32, (WIDE, TOK), 0) + here_ref[0]
    hit = jnp.zeros((WIDE, TOK), f32)
    for k in range(TOPK):
        hit = hit + (routes_ref[k : k + 1, :] == expert).astype(f32)
    sooner = lax.broadcasted_iota(jnp.int32, (TOK, TOK), 0)
    earlier = (sooner < lax.broadcasted_iota(jnp.int32, (TOK, TOK), 1)).astype(f32).astype(bf16)
    before = jnp.dot(hit.astype(bf16), earlier, preferred_element_type=f32)
    place = jnp.where(hit > 0, before, -1.0).astype(bf16)
    for (a, b), out_ref in zip(GROUPS, out_refs):
        size = b - a
        owner = size * lax.broadcasted_iota(jnp.int32, (WIDE * size, WIDE), 1)
        offset = lax.broadcasted_iota(jnp.int32, (WIDE * size, WIDE), 0) - owner
        inside = (offset >= 0) & (offset < size)
        spread = jnp.dot(
            inside.astype(f32).astype(bf16), place, preferred_element_type=f32
        )
        slot = jnp.sum(jnp.where(inside, offset + a, 0).astype(f32), axis=1, keepdims=True)
        out_ref[...] = (spread == slot).astype(f32).astype(bf16)


def dispatch_kernel(here_ref, x_ref, own_ref, par_ref, *refs):
    chooses = refs[: len(GROUPS)]
    hidden_ref = refs[len(GROUPS)]
    j = here_ref[1]
    mine = x_ref[:, pl.ds(pl.multiple_of(j * 512, 512), 512)].astype(f32)
    hidden = (mine + (own_ref[...].astype(f32) + par_ref[...].astype(f32))).astype(bf16)
    hidden_ref[...] = hidden
    for choose_ref, rows_ref in zip(chooses, refs[len(GROUPS) + 1 :]):
        rows = jnp.dot(choose_ref[...], hidden, preferred_element_type=f32)
        size = rows_ref.shape[1]
        for s in range(WIDE):
            rows_ref[s] = rows[s * size : (s + 1) * size].astype(bf16)


def gate_up_kernel(
    here_ref, x0, x1, x2, x3, gain_ref, gate_hbm, up_hbm, gate_par, up_par, out_ref, w_ref, sems
):
    i, j = here_ref[0], here_ref[1]
    sources = (gate_hbm.at[i], up_hbm.at[i], gate_par, up_par)
    copies = [
        pltpu.make_async_copy(source, w_ref.at[n], sems.at[n]) for n, source in enumerate(sources)
    ]
    for copy in copies:
        copy.start()
    xs = (x0, x1, x2, x3)
    total = jnp.zeros((x0.shape[0], 1), f32)
    for x in xs:
        v = x[...].astype(f32)
        total = total + jnp.sum(v * v, axis=1, keepdims=True)
    scale = lax.rsqrt(total / 2048.0 + EPS)
    for copy in copies:
        copy.wait()
    own = jnp.zeros((x0.shape[0], 256), f32)
    par = jnp.zeros((x0.shape[0], 256), f32)
    for k, x in enumerate(xs):
        part = lax.rem(j - k + 4, 4)
        rows = pl.ds(pl.multiple_of(part * 512, 512), 512)
        normed = (x[...].astype(f32) * scale * gain_ref[1:2, rows]).astype(bf16)
        w_own = jnp.concatenate([w_ref[0, rows, :], w_ref[1, rows, :]], axis=1)
        w_par = jnp.concatenate([w_ref[2, rows, :], w_ref[3, rows, :]], axis=1)
        own = own + jnp.dot(normed, w_own, preferred_element_type=f32)
        par = par + jnp.dot(normed, w_par, preferred_element_type=f32)
    for at, both in ((0, own), (128, par)):
        gate, up = both[:, :128], both[:, 128:]
        out_ref[:, at : at + 128] = (gate / (1.0 + jnp.exp(-gate)) * up).astype(bf16)


def down_kernel(here_ref, *refs):
    acts, weights, par_ref = refs[:8], refs[8:12], refs[12]
    out_ref, w_ref, sems = refs[13:]
    i = here_ref[0]
    copies = []
    for k, w in enumerate(weights):
        copies.append(
            (
                pltpu.make_async_copy(w.at[i], w_ref.at[k, 0:128], sems.at[0, k]),
                pltpu.make_async_copy(par_ref.at[k], w_ref.at[k, 128:256], sems.at[1, k]),
            )
        )
    for pair in copies:
        for copy in pair:
            copy.start()
    for half in range(2):
        total = jnp.zeros((HALF, 512), f32)
        for k in range(4):
            if half == 0:
                for copy in copies[k]:
                    copy.wait()
            total = total + jnp.dot(
                acts[4 * half + k][...], w_ref[k], preferred_element_type=f32
            )
        for s in range(WIDE // 2):
            out_ref[half * (WIDE // 2) + s] = total[s * CAP : (s + 1) * CAP].astype(bf16)


def embed_kernel(here_ref, hidden_ref, moe_ref, par_ref, gain_ref, w_ref, layer_ref, part_ref):
    mine = pl.ds(pl.multiple_of(here_ref[1] * 512, 512), 512)
    layer = hidden_ref[...].astype(f32) + (moe_ref[...].astype(f32) + par_ref[...].astype(f32))
    layer = layer.astype(bf16)
    layer_ref[...] = layer
    layer = layer.astype(f32)
    scaled = (layer * gain_ref[2:3, mine]).astype(bf16)
    part_ref[0:TOK, :] = jnp.dot(scaled, w_ref[mine, :], preferred_element_type=f32)
    square = jnp.broadcast_to(jnp.sum(layer * layer, axis=1, keepdims=True), (TOK, TOK))
    part_ref[TOK:, :] = jnp.transpose(square)[0:8]


def vector_kernel(p0, p1, p2, p3, out_ref):
    whole = p0[...] + p1[...] + p2[...] + p3[...]
    square = jnp.transpose(jnp.broadcast_to(whole[TOK : TOK + 1], (TOK, TOK)))
    embedded = whole[0:TOK] * lax.rsqrt(square / 2048.0 + EPS)
    norm = jnp.sum(embedded * embedded, axis=1, keepdims=True)
    vectors = (embedded * lax.rsqrt(norm + EPS)).astype(bf16)
    for copy in range(16):
        out_ref[copy] = vectors


def assemble_kernel(here_ref, p0, p1, p2, p3, out_ref):
    j = here_ref[1]
    for k, piece in enumerate((p0, p1, p2, p3)):
        part = lax.rem(j - k + 4, 4)
        out_ref[:, pl.ds(pl.multiple_of(part * 512, 512), 512)] = piece[...]


def score_kernel(info_ref, doc_ref, own_ref, other_ref, out_ref, query_ref, sems):
    def spot(d):
        return pl.multiple_of(jnp.minimum((info_ref[2, d] // 16) * 16, 2048 - 128), 16)

    def copy_of(ref, d):
        return pltpu.make_async_copy(ref.at[pl.ds(spot(d), 128), :], query_ref.at[d], sems.at[d])

    for d in range(16):

        @pl.when(info_ref[4, d] == 0)
        def _():
            copy_of(own_ref, d).start()

        @pl.when(info_ref[4, d] != 0)
        def _():
            copy_of(other_ref, d).start()

    lane = lax.broadcasted_iota(jnp.int32, (1, 16), 1)
    scores = jnp.zeros((1, 16), f32)
    rows = lax.broadcasted_iota(jnp.int32, (144, 128), 0)
    columns = lax.broadcasted_iota(jnp.int32, (1, 128), 1)
    for d in range(16):
        copy_of(own_ref, d).wait()
    for d in range(16):
        first, size = info_ref[0, d], info_ref[1, d]
        q_first, q_size = info_ref[2, d], info_ref[3, d]
        at = pl.multiple_of(jnp.minimum((first // 16) * 16, 1024 - 144), 16)
        sims = lax.dot_general(
            doc_ref[pl.ds(at, 144), :],
            query_ref[d],
            (((1,), (1,)), ((), ())),
            preferred_element_type=f32,
        )
        keep = (rows >= first - at) & (rows < first - at + size)
        best = jnp.max(jnp.where(keep, sims, NEG), axis=0, keepdims=True)
        q_start = q_first - spot(d)
        used = (columns >= q_start) & (columns < q_start + q_size)
        value = jnp.sum(jnp.where(used, best, 0.0), axis=1, keepdims=True) / q_size.astype(f32)
        scores = jnp.where(lane == d, value, scores)
    out_ref[...] = scores


def vmem():
    return pl.BlockSpec(memory_space=pltpu.VMEM)


def smem():
    return pl.BlockSpec(memory_space=pltpu.SMEM)


def hbm():
    return pl.BlockSpec(memory_space=pltpu.HBM)


def params():
    return pltpu.CompilerParams(vmem_limit_bytes=40 << 20)


def body(
    tokens,
    request_lengths,
    w_qkv,
    qk_gain,
    w_out,
    norm_gains,
    w_router,
    routes,
    w_gate,
    w_up,
    w_down,
    w_proj,
    doc_vectors,
    doc_segment,
    doc_request,
):
    i = lax.axis_index("xh")
    j = lax.axis_index("y")
    core = lax.axis_index("core")
    wide = lax.axis_index(W)
    here = jnp.stack([i, j, wide, core])

    def pick(array, which):
        return lax.dynamic_index_in_dim(array, which, 0, keepdims=False)

    def cut(array, part, axis):
        return lax.dynamic_slice_in_dim(array, lax.rem(part, 4) * 512, 512, axis)

    gate_sent, tokens = lax.optimization_barrier((pick(w_gate, 1 - i), tokens))
    gate_par = x_swap(gate_sent)

    attn = pl.pallas_call(
        attention_kernel,
        out_shape=(jax.ShapeDtypeStruct((TOK, 512), bf16),) * 4,
        in_specs=[smem()] * 2 + [vmem()] * 2 + [hbm()] * 3,
        out_specs=(vmem(),) * 4,
        scratch_shapes=[
            pltpu.VMEM((TOK, 2048), bf16),
            pltpu.VMEM((3, 2048, 256), bf16),
            pltpu.VMEM((256, 2048), bf16),
            pltpu.SemaphoreType.DMA((5,)),
        ],
        compiler_params=pltpu.CompilerParams(vmem_limit_bytes=60 << 20),
        name="attention",
    )(
        here,
        request_lengths.T,
        qk_gain,
        norm_gains,
        tokens,
        w_qkv.transpose(1, 0, 2),
        w_out,
    )
    attn_parts = [y_shift(attn[k], k) for k in (1, 2, 3)]

    up_par = x_swap(pick(w_up, 1 - i))
    downs = [cut(w_down, j, 2)] + [y_shift(cut(w_down, j + k, 2), k) for k in (1, 2, 3)]
    down_par = x_swap(jnp.stack([pick(d, 1 - i) for d in downs]))

    experts_here = 2 * jnp.arange(WIDE, dtype=jnp.int32) + i
    hit = jnp.sum((routes.T[None, :, :] == experts_here[:, None, None]).astype(f32), axis=1)
    places = jnp.arange(TOK, dtype=jnp.int32)
    earlier = (places[:, None] < places[None, :]).astype(bf16)
    before = jnp.dot(hit.astype(bf16), earlier, preferred_element_type=f32)
    slot = jnp.arange(CAP, dtype=jnp.int32).astype(f32)
    chosen = (before[:, None, :] == slot[None, :, None]) & (hit[:, None, :] > 0)
    chooses = pl.pallas_call(
        choose_kernel,
        out_shape=tuple(jax.ShapeDtypeStruct((WIDE * (b - a), TOK), bf16) for a, b in GROUPS),
        in_specs=[smem(), vmem()],
        out_specs=(vmem(),) * len(GROUPS),
        compiler_params=params(),
        name="choose",
    )(here, routes.T)

    attn = (attn[0].astype(f32) + sum(p.astype(f32) for p in attn_parts)).astype(bf16)
    attn, *chooses = lax.optimization_barrier((attn, *chooses))
    attn_par = x_swap(attn)
    attn_par, gate_par = lax.optimization_barrier((attn_par, gate_par))
    hidden, *rows = pl.pallas_call(
        dispatch_kernel,
        out_shape=(
            jax.ShapeDtypeStruct((TOK, 512), bf16),
            *(jax.ShapeDtypeStruct((WIDE, b - a, 512), bf16) for a, b in GROUPS),
        ),
        in_specs=[smem()] + [vmem()] * (3 + len(GROUPS)),
        out_specs=(vmem(),) * (1 + len(GROUPS)),
        compiler_params=params(),
        name="dispatch",
    )(here, tokens, attn, attn_par, *chooses)

    arrived = lax.all_to_all(rows[0], W, 0, 0, tiled=True)
    first = arrived[: WIDE // 2].reshape(HALF, 512)
    second = arrived[WIDE // 2 :].reshape(HALF, 512)
    gathered = [first] + [y_shift(first, k) for k in (1, 2, 3)]
    others = [second] + [y_shift(second, k) for k in (1, 2, 3)]
    gathered, others[1], others[3] = lax.optimization_barrier((gathered, others[1], others[3]))

    def gate_up(xs):
        return pl.pallas_call(
            gate_up_kernel,
            out_shape=jax.ShapeDtypeStruct((HALF, 256), bf16),
            in_specs=[smem()] + [vmem()] * 5 + [hbm()] * 4,
            out_specs=vmem(),
            scratch_shapes=[pltpu.VMEM((4, 2048, 128), bf16), pltpu.SemaphoreType.DMA((4,))],
            compiler_params=params(),
            name="gate_up",
        )(here, *xs, norm_gains, w_gate, w_up, gate_par, up_par)

    act = gate_up(gathered)
    acts = [act] + [y_shift(act, k) for k in (1, 2, 3)]
    act = gate_up(others)
    acts += [act] + [y_shift(act, k) for k in (1, 2, 3)]
    out = pl.pallas_call(
        down_kernel,
        out_shape=jax.ShapeDtypeStruct((WIDE, CAP, 512), bf16),
        in_specs=[smem()] + [vmem()] * 8 + [hbm()] * 5,
        out_specs=vmem(),
        scratch_shapes=[pltpu.VMEM((4, 256, 512), bf16), pltpu.SemaphoreType.DMA((2, 4))],
        compiler_params=params(),
        name="down",
    )(here, *acts, *downs, down_par)
    back = lax.all_to_all(out, W, 0, 0, tiled=True)

    hf = hidden.astype(f32)
    gain_mine = lax.dynamic_slice_in_dim(norm_gains[1], j * 512, 512, 0)
    router_mine = lax.dynamic_slice_in_dim(w_router, j * 512, 512, 0)
    part = jnp.dot((hf * gain_mine).astype(bf16), router_mine, preferred_element_type=f32)
    square = jnp.sum(hf * hf, axis=1, keepdims=True)
    part = jnp.concatenate([part, jnp.broadcast_to(square, (TOK, EXPERTS))], axis=1)
    whole = part
    for k in (1, 2, 3):
        whole = whole + y_shift(part, k)
    logits = whole[:, :EXPERTS] * lax.rsqrt(whole[:, EXPERTS : EXPERTS + 1] / 2048.0 + EPS)
    lifted = jax.nn.sigmoid(logits)
    onehot = jnp.sum(
        (routes[:, :, None] == jnp.arange(EXPERTS, dtype=jnp.int32)[None, None, :]).astype(f32),
        axis=1,
    )
    lifted = lifted * onehot
    gates = lifted / jnp.sum(lifted, axis=1, keepdims=True)
    gates = lax.dynamic_index_in_dim(gates.reshape(TOK, WIDE, 2), i, 2, keepdims=False).T

    moe = jnp.zeros((TOK, 512), f32)
    contract = (((0, 1), (0, 1)), ((), ()))
    mixing = jnp.where(chosen, gates[:, None, :], 0.0)
    mixing_hi = lax.reduce_precision(mixing, 8, 7)
    mixing_lo = (mixing - mixing_hi).astype(bf16)
    for matrix in (mixing_hi.astype(bf16), mixing_lo):
        moe = moe + lax.dot_general(matrix, back, contract, preferred_element_type=f32)
    moe = moe.astype(bf16)
    moe_par = x_swap(moe)
    layer, part = pl.pallas_call(
        embed_kernel,
        out_shape=(
            jax.ShapeDtypeStruct((TOK, 512), bf16),
            jax.ShapeDtypeStruct((TOK + 8, 128), f32),
        ),
        in_specs=[smem()] + [vmem()] * 5,
        out_specs=(vmem(), vmem()),
        name="embed",
    )(here, hidden, moe, moe_par, norm_gains, w_proj)
    parts = [part] + [y_shift(part, k) for k in (1, 2, 3)]

    vectors = pl.pallas_call(
        vector_kernel,
        out_shape=jax.ShapeDtypeStruct((16, TOK, 128), bf16),
        in_specs=[vmem()] * 4,
        out_specs=vmem(),
        name="vectors",
    )(*parts)
    vectors, layer = lax.optimization_barrier((vectors, layer))
    layers = [layer] + [y_shift(layer, k) for k in (1, 2, 3)]
    own = lax.all_to_all(vectors, ("z", "xl"), 0, 0, tiled=True).reshape(16 * TOK, 128)
    segment = doc_segment[0]
    requests = doc_request[0]
    docs = jnp.arange(16, dtype=jnp.int32)
    first = jnp.sum((segment[None, :] < docs[:, None]).astype(jnp.int32), axis=1)
    size = jnp.sum((segment[None, :] == docs[:, None]).astype(jnp.int32), axis=1)
    starts = jnp.cumsum(request_lengths, axis=1) - request_lengths
    starts = (starts + TOK * (jnp.arange(WIDE, dtype=jnp.int32) // 2)[:, None]).reshape(-1)
    match = requests[:, None] == jnp.arange(96, dtype=jnp.int32)[None, :]
    q_first = jnp.sum(jnp.where(match, starts[None, :], 0), axis=1)
    q_size = jnp.sum(jnp.where(match, request_lengths.reshape(-1)[None, :], 0), axis=1)
    away = lax.rem(requests // 3, 2) ^ core
    info = jnp.stack([first, size, q_first, q_size, away])
    own, info, *layers = lax.optimization_barrier((own, info, *layers))
    other = lax.ppermute(own, "core", [(0, 1), (1, 0)])
    layer_out = pl.pallas_call(
        assemble_kernel,
        out_shape=jax.ShapeDtypeStruct((TOK, 2048), bf16),
        in_specs=[smem()] + [vmem()] * 4,
        out_specs=vmem(),
        name="assemble",
    )(here, *layers)
    doc_scores = pl.pallas_call(
        score_kernel,
        out_shape=jax.ShapeDtypeStruct((1, 16), f32),
        in_specs=[smem(), vmem()] + [pl.BlockSpec(memory_space=pl.ANY)] * 2,
        out_specs=vmem(),
        scratch_shapes=[pltpu.VMEM((16, 128, 128), bf16), pltpu.SemaphoreType.DMA((16,))],
        name="score",
    )(info, doc_vectors, own, other)
    return (layer_out, doc_scores)


def solution(mesh):
    split = Mesh(mesh.devices.reshape(8, 2, 2, 2, 4), ("z", "xl", "core", "xh", "y"))
    placed = (
        P(W, None),
        P(),
        P(None, None, N),
        P(None, N),
        P(N, None),
        P(),
        P(),
        P(W, None),
        P(W, None, N),
        P(W, None, N),
        P(W, N, None),
        P(),
        P(W + N, None),
        P(W + N, None),
        P(W + N, None),
    )
    return jax.shard_map(
        body,
        mesh=split,
        in_specs=placed,
        out_specs=(P(W, None), P(W + N, None)),
        check_vma=False,
    )
```

```python
import math

import jax
import jax.numpy as jnp
from jax import lax
from jax.experimental import pallas as pl
from jax.experimental.pallas import tpu as pltpu
from jax.sharding import Mesh, PartitionSpec as P

HD = 128
TOPK = 8
TOK = 128
CAP = 20
EXPERTS = 64
WIDE = 32
HALF = WIDE * CAP // 2
EPS = 1e-06
THETA = 50000.0
NEG = -1e30
W = ("z", "xl", "core")
N = ("xh", "y")
f32 = jnp.float32
bf16 = jnp.bfloat16


def y_shift(x, k):
    return lax.ppermute(x, "y", [(s, (s + k) % 4) for s in range(4)])


def x_swap(x):
    return lax.ppermute(x, "xh", [(0, 1), (1, 0)])


def attention_kernel(
    here_ref,
    lengths_ref,
    qk_ref,
    gain_ref,
    x_hbm,
    w_hbm,
    out_hbm,
    out0,
    out1,
    out2,
    out3,
    x_ref,
    w_ref,
    out_w_ref,
    sems,
):
    copies = [pltpu.make_async_copy(x_hbm, x_ref, sems.at[0])]
    copies += [
        pltpu.make_async_copy(w_hbm.at[part], w_ref.at[part], sems.at[1 + part]) for part in range(3)
    ]
    copies += [pltpu.make_async_copy(out_hbm, out_w_ref, sems.at[4])]
    for copy in copies:
        copy.start()
    wide = here_ref[2]
    one = lengths_ref[0, wide]
    two = one + lengths_ref[1, wide]

    def member_of(places):
        return (places >= one).astype(jnp.int32) + (places >= two).astype(jnp.int32)

    down_places = lax.broadcasted_iota(jnp.int32, (TOK, HD), 0)
    across_places = lax.broadcasted_iota(jnp.int32, (TOK, HD), 1)
    member = member_of(down_places)
    same = member == member_of(across_places)
    start = jnp.where(member == 0, 0, jnp.where(member == 1, one, two))
    half = lax.rem(across_places, HD // 2).astype(f32)
    freq = jnp.exp(half * (-math.log(THETA) / (HD // 2)))
    angle = (down_places - start).astype(f32) * freq
    cosine = jnp.cos(angle)
    sine = jnp.sin(angle)
    sine = jnp.where(across_places < HD // 2, -sine, sine)

    copies[0].wait()
    x = x_ref[...].astype(f32)
    scale = lax.rsqrt(jnp.mean(x * x, axis=1, keepdims=True) + EPS)
    normed = (x * scale * gain_ref[0:1, :]).astype(bf16)
    parts = []
    for part in range(3):
        copies[1 + part].wait()
        parts.append(jnp.dot(normed, w_ref[part], preferred_element_type=f32))
    query, keys, values = parts

    def turned(v, gain):
        v = v * lax.rsqrt(jnp.mean(v * v, axis=1, keepdims=True) + EPS) * gain
        return (v * cosine + pltpu.roll(v, HD // 2, 1) * sine).astype(bf16)

    mixed = []
    for head in range(2):
        at = slice(head * HD, (head + 1) * HD)
        q = turned(query[:, at], qk_ref[0:1, at])
        k = turned(keys[:, at], qk_ref[1:2, at])
        scores = lax.dot_general(q, k, (((1,), (1,)), ((), ())), preferred_element_type=f32)
        scores = jnp.where(same, scores * HD ** (-0.5), NEG)
        weights = jnp.exp(scores - jnp.max(scores, axis=1, keepdims=True))
        probs = (weights / jnp.sum(weights, axis=1, keepdims=True)).astype(bf16)
        mixed.append(
            jnp.dot(probs, values[:, at].astype(bf16), preferred_element_type=f32).astype(bf16)
        )
    mixed = jnp.concatenate(mixed, axis=1)
    copies[4].wait()
    j = here_ref[1]
    for k, out_ref in enumerate((out0, out1, out2, out3)):
        part = lax.rem(j + k, 4)
        columns = pl.ds(pl.multiple_of(part * 512, 512), 512)
        out_ref[...] = jnp.dot(mixed, out_w_ref[:, columns], preferred_element_type=f32).astype(bf16)


def choose_kernel(here_ref, routes_ref, out_ref):
    expert = 2 * lax.broadcasted_iota(jnp.int32, (WIDE, TOK), 0) + here_ref[0]
    hit = jnp.zeros((WIDE, TOK), f32)
    for k in range(TOPK):
        hit = hit + (routes_ref[k : k + 1, :] == expert).astype(f32)
    sooner = lax.broadcasted_iota(jnp.int32, (TOK, TOK), 0)
    earlier = (sooner < lax.broadcasted_iota(jnp.int32, (TOK, TOK), 1)).astype(f32).astype(bf16)
    before = jnp.dot(hit.astype(bf16), earlier, preferred_element_type=f32)
    place = jnp.where(hit > 0, before, -1.0).astype(bf16)
    owner = CAP * lax.broadcasted_iota(jnp.int32, (WIDE * CAP, WIDE), 1)
    slot = lax.broadcasted_iota(jnp.int32, (WIDE * CAP, WIDE), 0) - owner
    inside = (slot >= 0) & (slot < CAP)
    spread = jnp.dot(inside.astype(f32).astype(bf16), place, preferred_element_type=f32)
    slot = jnp.sum(jnp.where(inside, slot, 0).astype(f32), axis=1, keepdims=True)
    out_ref[...] = (spread == slot).astype(f32).astype(bf16)


def packed(rows):
    return jnp.concatenate([rows[:, 0:256], rows[:, 256:512]], axis=0).astype(bf16)


def dispatch_kernel(here_ref, x_ref, own_ref, par_ref, choose_ref, hidden_ref, rows_ref):
    j = here_ref[1]
    mine = x_ref[:, pl.ds(pl.multiple_of(j * 512, 512), 512)].astype(f32)
    hidden = (mine + (own_ref[...].astype(f32) + par_ref[...].astype(f32))).astype(bf16)
    hidden_ref[...] = hidden
    rows = jnp.dot(choose_ref[...], hidden, preferred_element_type=f32)
    for s in range(WIDE):
        rows_ref[s] = packed(rows[s * CAP : (s + 1) * CAP])


def unpack_kernel(in_ref, top_ref, bottom_ref, scratch):
    for half, out_ref in enumerate((top_ref, bottom_ref)):
        for s in range(WIDE // 2):
            rows = in_ref[half * (WIDE // 2) + s].astype(f32)
            at = slice(s * CAP, (s + 1) * CAP)
            scratch[at, 0:256] = rows[0:CAP]
            scratch[at, 256:512] = rows[CAP:]
        out_ref[...] = scratch[...].astype(bf16)


def gate_up_kernel(here_ref, *refs):
    halves = refs[0:4], refs[4:8]
    gain_hbm, gate_hbm, up_hbm, gate_par, up_par, out_ref, gain_ref, w_ref, sems = refs[8:]
    i, j = here_ref[0], here_ref[1]
    sources = (gate_hbm.at[i], up_hbm.at[i], gate_par, up_par)
    copies = [
        pltpu.make_async_copy(source, w_ref.at[n], sems.at[n]) for n, source in enumerate(sources)
    ]
    copies.append(pltpu.make_async_copy(gain_hbm, gain_ref, sems.at[4]))
    for copy in copies:
        copy.start()
    scales = []
    for xs in halves:
        total = jnp.zeros((HALF, 1), f32)
        for x in xs:
            v = x[...].astype(f32)
            total = total + jnp.sum(v * v, axis=1, keepdims=True)
        scales.append(lax.rsqrt(total / 2048.0 + EPS))
    for copy in copies:
        copy.wait()
    for half, (xs, scale) in enumerate(zip(halves, scales)):
        own = jnp.zeros((HALF, 256), f32)
        par = jnp.zeros((HALF, 256), f32)
        for k, x in enumerate(xs):
            part = lax.rem(j + 4 + (0, -1, 1, 2)[k], 4)
            rows = pl.ds(pl.multiple_of(part * 512, 512), 512)
            normed = (x[...].astype(f32) * scale * gain_ref[1:2, rows]).astype(bf16)
            w_own = jnp.concatenate([w_ref[0, rows, :], w_ref[1, rows, :]], axis=1)
            w_par = jnp.concatenate([w_ref[2, rows, :], w_ref[3, rows, :]], axis=1)
            own = own + jnp.dot(normed, w_own, preferred_element_type=f32)
            par = par + jnp.dot(normed, w_par, preferred_element_type=f32)
        for at, both in ((0, own), (128, par)):
            gate, up = both[:, :128], both[:, 128:]
            out_ref[half * HALF : (half + 1) * HALF, at : at + 128] = (
                gate / (1.0 + jnp.exp(-gate)) * up
            ).astype(bf16)


def down_kernel(here_ref, a0, a1, a2, a3, w0, w1, w2, w3, par_ref, out_ref, w_ref, sems):
    i = here_ref[0]
    copies = []
    for k, w in enumerate((w0, w1, w2, w3)):
        copies.append(
            (
                pltpu.make_async_copy(w.at[i], w_ref.at[k, 0:128], sems.at[0, k]),
                pltpu.make_async_copy(par_ref.at[k], w_ref.at[k, 128:256], sems.at[1, k]),
            )
        )
    for pair in copies:
        for copy in pair:
            copy.start()
    total = jnp.zeros((a0.shape[0], 512), f32)
    for k, a in enumerate((a0, a1, a2, a3)):
        for copy in copies[k]:
            copy.wait()
        total = total + jnp.dot(a[...], w_ref[k], preferred_element_type=f32)
    size = out_ref.shape[1]
    for s in range(WIDE):
        out_ref[s] = total[s * size : (s + 1) * size].astype(bf16)


def embed_kernel(here_ref, hidden_ref, moe_ref, par_ref, gain_ref, w_ref, layer_ref, part_ref):
    mine = pl.ds(pl.multiple_of(here_ref[1] * 512, 512), 512)
    layer = hidden_ref[...].astype(f32) + (moe_ref[...].astype(f32) + par_ref[...].astype(f32))
    layer = layer.astype(bf16)
    layer_ref[...] = layer
    layer = layer.astype(f32)
    scaled = (layer * gain_ref[2:3, mine]).astype(bf16)
    part_ref[0:TOK, :] = jnp.dot(scaled, w_ref[mine, :], preferred_element_type=f32)
    square = jnp.broadcast_to(jnp.sum(layer * layer, axis=1, keepdims=True), (TOK, TOK))
    part_ref[TOK:, :] = jnp.transpose(square)[0:8]


def vector_kernel(p0, p1, p2, p3, out_ref):
    whole = p0[...] + p1[...] + p2[...] + p3[...]
    square = jnp.transpose(jnp.broadcast_to(whole[TOK : TOK + 1], (TOK, TOK)))
    embedded = whole[0:TOK] * lax.rsqrt(square / 2048.0 + EPS)
    norm = jnp.sum(embedded * embedded, axis=1, keepdims=True)
    vectors = (embedded * lax.rsqrt(norm + EPS)).astype(bf16)
    for copy in range(16):
        out_ref[copy] = vectors


def assemble_kernel(here_ref, p0, p1, p2, p3, out_ref):
    j = here_ref[1]
    for k, piece in enumerate((p0, p1, p2, p3)):
        part = lax.rem(j - k + 4, 4)
        out_ref[:, pl.ds(pl.multiple_of(part * 512, 512), 512)] = piece[...]


def score_kernel(info_ref, doc_ref, own_ref, other_ref, out_ref, query_ref, sems):
    def spot(d):
        return pl.multiple_of(jnp.minimum((info_ref[2, d] // 16) * 16, 2048 - 128), 16)

    def copy_of(ref, d):
        return pltpu.make_async_copy(ref.at[pl.ds(spot(d), 128), :], query_ref.at[d], sems.at[d])

    for d in range(16):

        @pl.when(info_ref[4, d] == 0)
        def _():
            copy_of(own_ref, d).start()

        @pl.when(info_ref[4, d] != 0)
        def _():
            copy_of(other_ref, d).start()

    lane = lax.broadcasted_iota(jnp.int32, (1, 16), 1)
    scores = jnp.zeros((1, 16), f32)
    rows = lax.broadcasted_iota(jnp.int32, (144, 128), 0)
    columns = lax.broadcasted_iota(jnp.int32, (1, 128), 1)
    for d in range(16):
        copy_of(own_ref, d).wait()
    for d in range(16):
        first, size = info_ref[0, d], info_ref[1, d]
        q_first, q_size = info_ref[2, d], info_ref[3, d]
        at = pl.multiple_of(jnp.minimum((first // 16) * 16, 1024 - 144), 16)
        sims = lax.dot_general(
            doc_ref[pl.ds(at, 144), :],
            query_ref[d],
            (((1,), (1,)), ((), ())),
            preferred_element_type=f32,
        )
        keep = (rows >= first - at) & (rows < first - at + size)
        best = jnp.max(jnp.where(keep, sims, NEG), axis=0, keepdims=True)
        q_start = q_first - spot(d)
        used = (columns >= q_start) & (columns < q_start + q_size)
        value = jnp.sum(jnp.where(used, best, 0.0), axis=1, keepdims=True) / q_size.astype(f32)
        scores = jnp.where(lane == d, value, scores)
    out_ref[...] = scores


def vmem():
    return pl.BlockSpec(memory_space=pltpu.VMEM)


def smem():
    return pl.BlockSpec(memory_space=pltpu.SMEM)


def hbm():
    return pl.BlockSpec(memory_space=pltpu.HBM)


def params():
    return pltpu.CompilerParams(vmem_limit_bytes=40 << 20)


def body(
    tokens,
    request_lengths,
    w_qkv,
    qk_gain,
    w_out,
    norm_gains,
    w_router,
    routes,
    w_gate,
    w_up,
    w_down,
    w_proj,
    doc_vectors,
    doc_segment,
    doc_request,
):
    i = lax.axis_index("xh")
    j = lax.axis_index("y")
    core = lax.axis_index("core")
    wide = lax.axis_index(W)
    here = jnp.stack([i, j, wide, core])

    def pick(array, which):
        return lax.dynamic_index_in_dim(array, which, 0, keepdims=False)

    def cut(array, part, axis):
        return lax.dynamic_slice_in_dim(array, lax.rem(part, 4) * 512, 512, axis)

    gate_sent, tokens = lax.optimization_barrier((pick(w_gate, 1 - i), tokens))
    gate_par = x_swap(gate_sent)

    attn = pl.pallas_call(
        attention_kernel,
        out_shape=(jax.ShapeDtypeStruct((TOK, 512), bf16),) * 4,
        in_specs=[smem()] * 2 + [vmem()] * 2 + [hbm()] * 3,
        out_specs=(vmem(),) * 4,
        scratch_shapes=[
            pltpu.VMEM((TOK, 2048), bf16),
            pltpu.VMEM((3, 2048, 256), bf16),
            pltpu.VMEM((256, 2048), bf16),
            pltpu.SemaphoreType.DMA((5,)),
        ],
        compiler_params=pltpu.CompilerParams(vmem_limit_bytes=60 << 20),
        name="attention",
    )(
        here,
        request_lengths.T,
        qk_gain,
        norm_gains,
        tokens,
        w_qkv.transpose(1, 0, 2),
        w_out,
    )
    attn_parts = [y_shift(attn[k], k) for k in (1, 2, 3)]

    downs = [cut(w_down, j, 2)] + [y_shift(cut(w_down, j + k, 2), k) for k in (1, 2, 3)]
    down_par = x_swap(jnp.stack([pick(d, 1 - i) for d in downs]))

    experts_here = 2 * jnp.arange(WIDE, dtype=jnp.int32) + i
    hit = jnp.sum((routes.T[None, :, :] == experts_here[:, None, None]).astype(f32), axis=1)
    places = jnp.arange(TOK, dtype=jnp.int32)
    earlier = (places[:, None] < places[None, :]).astype(bf16)
    before = jnp.dot(hit.astype(bf16), earlier, preferred_element_type=f32)
    slot = jnp.arange(CAP, dtype=jnp.int32).astype(f32)
    chosen = (before[:, None, :] == slot[None, :, None]) & (hit[:, None, :] > 0)
    choose = pl.pallas_call(
        choose_kernel,
        out_shape=jax.ShapeDtypeStruct((WIDE * CAP, TOK), bf16),
        in_specs=[smem(), vmem()],
        out_specs=vmem(),
        compiler_params=params(),
        name="choose",
    )(here, routes.T)

    attn = (attn[0].astype(f32) + sum(p.astype(f32) for p in attn_parts)).astype(bf16)
    attn, choose = lax.optimization_barrier((attn, choose))
    attn_par = x_swap(attn)
    attn_par, gate_par = lax.optimization_barrier((attn_par, gate_par))
    hidden, rows = pl.pallas_call(
        dispatch_kernel,
        out_shape=(
            jax.ShapeDtypeStruct((TOK, 512), bf16),
            jax.ShapeDtypeStruct((WIDE, 2 * CAP, 256), bf16),
        ),
        in_specs=[smem()] + [vmem()] * 4,
        out_specs=(vmem(), vmem()),
        compiler_params=params(),
        name="dispatch",
    )(here, tokens, attn, attn_par, choose)

    arrived = lax.all_to_all(rows, W, 0, 0, tiled=True)
    top, bottom = pl.pallas_call(
        unpack_kernel,
        out_shape=(jax.ShapeDtypeStruct((HALF, 512), bf16),) * 2,
        in_specs=[vmem()],
        out_specs=(vmem(), vmem()),
        scratch_shapes=[pltpu.VMEM((HALF, 512), f32)],
        compiler_params=params(),
        name="unpack",
    )(arrived)
    top, bottom, up_sent = lax.optimization_barrier((top, bottom, pick(w_up, 1 - i)))
    up_par = x_swap(up_sent)
    top_back, bottom_ahead = y_shift(top, 1), y_shift(bottom, 3)
    bottom_back, top_ahead = y_shift(bottom, 1), y_shift(top, 3)
    top_far, bottom_far = y_shift(top_back, 1), y_shift(bottom_ahead, 3)
    act = pl.pallas_call(
        gate_up_kernel,
        out_shape=jax.ShapeDtypeStruct((2 * HALF, 256), bf16),
        in_specs=[smem()] + [vmem()] * 8 + [hbm()] * 5,
        out_specs=vmem(),
        scratch_shapes=[
            pltpu.VMEM((3, 2048), f32),
            pltpu.VMEM((4, 2048, 128), bf16),
            pltpu.SemaphoreType.DMA((5,)),
        ],
        compiler_params=params(),
        name="gate_up",
    )(
        here,
        *(top, top_back, top_ahead, top_far),
        *(bottom, bottom_back, bottom_ahead, bottom_far),
        norm_gains,
        w_gate,
        w_up,
        gate_par,
        up_par,
    )
    out = pl.pallas_call(
        down_kernel,
        out_shape=jax.ShapeDtypeStruct((WIDE, CAP, 512), bf16),
        in_specs=[smem()] + [vmem()] * 4 + [hbm()] * 5,
        out_specs=vmem(),
        scratch_shapes=[pltpu.VMEM((4, 256, 512), bf16), pltpu.SemaphoreType.DMA((2, 4))],
        compiler_params=params(),
        name="down",
    )(here, act, *(y_shift(act, k) for k in (1, 2, 3)), *downs, down_par)
    back = lax.all_to_all(out, W, 0, 0, tiled=True)

    hf = hidden.astype(f32)
    gain_mine = lax.dynamic_slice_in_dim(norm_gains[1], j * 512, 512, 0)
    router_mine = lax.dynamic_slice_in_dim(w_router, j * 512, 512, 0)
    part = jnp.dot((hf * gain_mine).astype(bf16), router_mine, preferred_element_type=f32)
    square = jnp.sum(hf * hf, axis=1, keepdims=True)
    part = jnp.concatenate([part, jnp.broadcast_to(square, (TOK, EXPERTS))], axis=1)
    whole = part
    for k in (1, 2, 3):
        whole = whole + y_shift(part, k)
    logits = whole[:, :EXPERTS] * lax.rsqrt(whole[:, EXPERTS : EXPERTS + 1] / 2048.0 + EPS)
    lifted = jax.nn.sigmoid(logits)
    onehot = jnp.sum(
        (routes[:, :, None] == jnp.arange(EXPERTS, dtype=jnp.int32)[None, None, :]).astype(f32),
        axis=1,
    )
    lifted = lifted * onehot
    gates = lifted / jnp.sum(lifted, axis=1, keepdims=True)
    gates = lax.dynamic_index_in_dim(gates.reshape(TOK, WIDE, 2), i, 2, keepdims=False).T

    moe = jnp.zeros((TOK, 512), f32)
    contract = (((0, 1), (0, 1)), ((), ()))
    mixing = jnp.where(chosen, gates[:, None, :], 0.0)
    mixing_hi = lax.reduce_precision(mixing, 8, 7)
    mixing_lo = (mixing - mixing_hi).astype(bf16)
    for matrix in (mixing_hi.astype(bf16), mixing_lo):
        moe = moe + lax.dot_general(matrix, back, contract, preferred_element_type=f32)
    moe = moe.astype(bf16)
    moe_par = x_swap(moe)
    layer, part = pl.pallas_call(
        embed_kernel,
        out_shape=(
            jax.ShapeDtypeStruct((TOK, 512), bf16),
            jax.ShapeDtypeStruct((TOK + 8, 128), f32),
        ),
        in_specs=[smem()] + [vmem()] * 5,
        out_specs=(vmem(), vmem()),
        name="embed",
    )(here, hidden, moe, moe_par, norm_gains, w_proj)
    parts = [part] + [y_shift(part, k) for k in (1, 2, 3)]

    vectors = pl.pallas_call(
        vector_kernel,
        out_shape=jax.ShapeDtypeStruct((16, TOK, 128), bf16),
        in_specs=[vmem()] * 4,
        out_specs=vmem(),
        name="vectors",
    )(*parts)
    vectors, layer = lax.optimization_barrier((vectors, layer))
    layers = [layer] + [y_shift(layer, k) for k in (1, 2, 3)]
    own = lax.all_to_all(vectors, ("z", "xl"), 0, 0, tiled=True).reshape(16 * TOK, 128)
    segment = doc_segment[0]
    requests = doc_request[0]
    docs = jnp.arange(16, dtype=jnp.int32)
    first = jnp.sum((segment[None, :] < docs[:, None]).astype(jnp.int32), axis=1)
    size = jnp.sum((segment[None, :] == docs[:, None]).astype(jnp.int32), axis=1)
    starts = jnp.cumsum(request_lengths, axis=1) - request_lengths
    starts = (starts + TOK * (jnp.arange(WIDE, dtype=jnp.int32) // 2)[:, None]).reshape(-1)
    match = requests[:, None] == jnp.arange(96, dtype=jnp.int32)[None, :]
    q_first = jnp.sum(jnp.where(match, starts[None, :], 0), axis=1)
    q_size = jnp.sum(jnp.where(match, request_lengths.reshape(-1)[None, :], 0), axis=1)
    away = lax.rem(requests // 3, 2) ^ core
    info = jnp.stack([first, size, q_first, q_size, away])
    own, info, *layers = lax.optimization_barrier((own, info, *layers))
    other = lax.ppermute(own, "core", [(0, 1), (1, 0)])
    layer_out = pl.pallas_call(
        assemble_kernel,
        out_shape=jax.ShapeDtypeStruct((TOK, 2048), bf16),
        in_specs=[smem()] + [vmem()] * 4,
        out_specs=vmem(),
        name="assemble",
    )(here, *layers)
    doc_scores = pl.pallas_call(
        score_kernel,
        out_shape=jax.ShapeDtypeStruct((1, 16), f32),
        in_specs=[smem(), vmem()] + [pl.BlockSpec(memory_space=pl.ANY)] * 2,
        out_specs=vmem(),
        scratch_shapes=[pltpu.VMEM((16, 128, 128), bf16), pltpu.SemaphoreType.DMA((16,))],
        name="score",
    )(info, doc_vectors, own, other)
    return (layer_out, doc_scores)


def solution(mesh):
    split = Mesh(mesh.devices.reshape(8, 2, 2, 2, 4), ("z", "xl", "core", "xh", "y"))
    placed = (
        P(W, None),
        P(),
        P(None, None, N),
        P(None, N),
        P(N, None),
        P(),
        P(),
        P(W, None),
        P(W, None, N),
        P(W, None, N),
        P(W, N, None),
        P(),
        P(W + N, None),
        P(W + N, None),
        P(W + N, None),
    )
    return jax.shard_map(
        body,
        mesh=split,
        in_specs=placed,
        out_specs=(P(W, None), P(W + N, None)),
        check_vma=False,
    )
```

```python
import math

import jax
import jax.numpy as jnp
from jax import lax
from jax.experimental import pallas as pl
from jax.experimental.pallas import tpu as pltpu
from jax.sharding import Mesh, PartitionSpec as P

HD = 128
TOPK = 8
TOK = 128
CAP = 20
EXPERTS = 64
WIDE = 32
HALF = WIDE * CAP // 2
EPS = 1e-06
THETA = 50000.0
NEG = -1e30
W = ("z", "xl", "core")
N = ("xh", "y")
E = W + ("xh",)
f32 = jnp.float32
bf16 = jnp.bfloat16


def y_shift(x, k):
    return lax.ppermute(x, "y", [(s, (s + k) % 4) for s in range(4)])


def x_swap(x):
    return lax.ppermute(x, "xh", [(0, 1), (1, 0)])


def attention_kernel(
    here_ref,
    lengths_ref,
    qk_ref,
    gain_ref,
    x_hbm,
    w_hbm,
    out_hbm,
    out_ref,
    x_ref,
    w_ref,
    out_w_ref,
    sems,
):
    copies = [pltpu.make_async_copy(x_hbm, x_ref, sems.at[0])]
    copies += [
        pltpu.make_async_copy(w_hbm.at[part], w_ref.at[part], sems.at[1 + part]) for part in range(3)
    ]
    copies += [pltpu.make_async_copy(out_hbm, out_w_ref, sems.at[4])]
    for copy in copies:
        copy.start()
    wide = here_ref[2]
    one = lengths_ref[0, wide]
    two = one + lengths_ref[1, wide]

    def member_of(places):
        return (places >= one).astype(jnp.int32) + (places >= two).astype(jnp.int32)

    down_places = lax.broadcasted_iota(jnp.int32, (TOK, HD), 0)
    across_places = lax.broadcasted_iota(jnp.int32, (TOK, HD), 1)
    member = member_of(down_places)
    same = member == member_of(across_places)
    start = jnp.where(member == 0, 0, jnp.where(member == 1, one, two))
    half = lax.rem(across_places, HD // 2).astype(f32)
    freq = jnp.exp(half * (-math.log(THETA) / (HD // 2)))
    angle = (down_places - start).astype(f32) * freq
    cosine = jnp.cos(angle)
    sine = jnp.sin(angle)
    sine = jnp.where(across_places < HD // 2, -sine, sine)

    copies[0].wait()
    x = x_ref[...].astype(f32)
    scale = lax.rsqrt(jnp.mean(x * x, axis=1, keepdims=True) + EPS)
    normed = (x * scale * gain_ref[0:1, :]).astype(bf16)
    parts = []
    for part in range(3):
        copies[1 + part].wait()
        parts.append(jnp.dot(normed, w_ref[part], preferred_element_type=f32))
    query, keys, values = parts

    def turned(v, gain):
        v = v * lax.rsqrt(jnp.mean(v * v, axis=1, keepdims=True) + EPS) * gain
        return (v * cosine + pltpu.roll(v, HD // 2, 1) * sine).astype(bf16)

    mixed = []
    for head in range(2):
        at = slice(head * HD, (head + 1) * HD)
        q = turned(query[:, at], qk_ref[0:1, at])
        k = turned(keys[:, at], qk_ref[1:2, at])
        scores = lax.dot_general(q, k, (((1,), (1,)), ((), ())), preferred_element_type=f32)
        scores = jnp.where(same, scores * HD ** (-0.5), NEG)
        weights = jnp.exp(scores - jnp.max(scores, axis=1, keepdims=True))
        probs = (weights / jnp.sum(weights, axis=1, keepdims=True)).astype(bf16)
        mixed.append(
            jnp.dot(probs, values[:, at].astype(bf16), preferred_element_type=f32).astype(bf16)
        )
    mixed = jnp.concatenate(mixed, axis=1)
    copies[4].wait()
    for n in range(8):
        at = 512 * (n % 4) + 256 * (n // 4)
        out_ref[n] = jnp.dot(
            mixed, out_w_ref[:, at : at + 256], preferred_element_type=f32
        ).astype(bf16)


def choose_kernel(routes_ref, out_ref):
    expert = lax.broadcasted_iota(jnp.int32, (EXPERTS, TOK), 0)
    hit = jnp.zeros((EXPERTS, TOK), f32)
    for k in range(TOPK):
        hit = hit + (routes_ref[k : k + 1, :] == expert).astype(f32)
    sooner = lax.broadcasted_iota(jnp.int32, (TOK, TOK), 0)
    earlier = (sooner < lax.broadcasted_iota(jnp.int32, (TOK, TOK), 1)).astype(f32).astype(bf16)
    before = jnp.dot(hit.astype(bf16), earlier, preferred_element_type=f32)
    place = jnp.where(hit > 0, before, -1.0).astype(bf16)
    owner = CAP * lax.broadcasted_iota(jnp.int32, (EXPERTS * CAP, EXPERTS), 1)
    slot = lax.broadcasted_iota(jnp.int32, (EXPERTS * CAP, EXPERTS), 0) - owner
    inside = (slot >= 0) & (slot < CAP)
    spread = jnp.dot(inside.astype(f32).astype(bf16), place, preferred_element_type=f32)
    slot = jnp.sum(jnp.where(inside, slot, 0).astype(f32), axis=1, keepdims=True)
    out_ref[...] = (spread == slot).astype(f32).astype(bf16)


def packed(rows):
    return jnp.concatenate([rows[:, 0:128], rows[:, 128:256]], axis=0).astype(bf16)


def mine_of(here_ref):
    return pl.ds(pl.multiple_of(here_ref[1] * 512 + here_ref[0] * 256, 256), 256)


def dispatch_kernel(here_ref, x_ref, parts_ref, choose_ref, hidden_ref, rows_ref):
    total = x_ref[:, mine_of(here_ref)].astype(f32)
    for n in range(8):
        total = total + parts_ref[n].astype(f32)
    hidden = total.astype(bf16)
    hidden_ref[...] = hidden
    rows = jnp.dot(choose_ref[...], hidden, preferred_element_type=f32)
    for e in range(EXPERTS):
        rows_ref[e] = packed(rows[e * CAP : (e + 1) * CAP])


def unpack_kernel(in_ref, top_ref, bottom_ref, scratch):
    for half, out_ref in enumerate((top_ref, bottom_ref)):
        for s in range(WIDE // 2):
            at = slice(s * CAP, (s + 1) * CAP)
            for h in range(2):
                rows = in_ref[half * WIDE + 2 * s + h].astype(f32)
                scratch[at, 256 * h : 256 * h + 128] = rows[0:CAP]
                scratch[at, 256 * h + 128 : 256 * h + 256] = rows[CAP:]
        out_ref[...] = scratch[...].astype(bf16)


def gate_up_kernel(here_ref, *refs):
    halves = refs[0:4], refs[4:8]
    gain_hbm, gate_hbm, up_hbm, both_par, out_ref, gain_ref, w_ref, sems = refs[8:]
    i, j = here_ref[0], here_ref[1]
    sources = (gate_hbm.at[i], up_hbm.at[i], both_par.at[0], both_par.at[1])
    copies = [
        pltpu.make_async_copy(source, w_ref.at[n], sems.at[n]) for n, source in enumerate(sources)
    ]
    copies.append(pltpu.make_async_copy(gain_hbm, gain_ref, sems.at[4]))
    for copy in copies:
        copy.start()
    scales = []
    for xs in halves:
        total = jnp.zeros((HALF, 1), f32)
        for x in xs:
            v = x[...].astype(f32)
            total = total + jnp.sum(v * v, axis=1, keepdims=True)
        scales.append(lax.rsqrt(total / 2048.0 + EPS))
    for copy in copies:
        copy.wait()
    for half, (xs, scale) in enumerate(zip(halves, scales)):
        own = jnp.zeros((HALF, 256), f32)
        par = jnp.zeros((HALF, 256), f32)
        for k, x in enumerate(xs):
            part = lax.rem(j + 4 + (0, -1, 1, 2)[k], 4)
            rows = pl.ds(pl.multiple_of(part * 512, 512), 512)
            normed = (x[...].astype(f32) * scale * gain_ref[1:2, rows]).astype(bf16)
            w_own = jnp.concatenate([w_ref[0, rows, :], w_ref[1, rows, :]], axis=1)
            w_par = jnp.concatenate([w_ref[2, rows, :], w_ref[3, rows, :]], axis=1)
            own = own + jnp.dot(normed, w_own, preferred_element_type=f32)
            par = par + jnp.dot(normed, w_par, preferred_element_type=f32)
        for at, both in ((0, own), (128, par)):
            gate, up = both[:, :128], both[:, 128:]
            out_ref[half * HALF : (half + 1) * HALF, at : at + 128] = (
                gate / (1.0 + jnp.exp(-gate)) * up
            ).astype(bf16)


def down_kernel(here_ref, a0, a1, a2, a3, w0, w1, w2, w3, par_ref, out_ref, w_ref, sems):
    i = here_ref[0]
    copies = []
    for k, w in enumerate((w0, w1, w2, w3)):
        copies.append(
            (
                pltpu.make_async_copy(w.at[i], w_ref.at[k, 0:128], sems.at[0, k]),
                pltpu.make_async_copy(par_ref.at[k], w_ref.at[k, 128:256], sems.at[1, k]),
            )
        )
    for pair in copies:
        for copy in pair:
            copy.start()
    total = jnp.zeros((a0.shape[0], 512), f32)
    for k, a in enumerate((a0, a1, a2, a3)):
        for copy in copies[k]:
            copy.wait()
        total = total + jnp.dot(a[...], w_ref[k], preferred_element_type=f32)
    for s in range(WIDE):
        rows = total[s * CAP : (s + 1) * CAP]
        out_ref[2 * s] = packed(rows[:, 0:256])
        out_ref[2 * s + 1] = packed(rows[:, 256:512])


def mixing_kernel(whole_ref, routes_ref, high_ref, low_ref):
    logits = whole_ref[:, 0:EXPERTS]
    logits = logits * lax.rsqrt(whole_ref[:, EXPERTS : EXPERTS + 1] / 2048.0 + EPS)
    expert = lax.broadcasted_iota(jnp.int32, (TOK, EXPERTS), 1)
    hit = jnp.zeros((TOK, EXPERTS), f32)
    for k in range(TOPK):
        hit = hit + (routes_ref[:, k : k + 1] == expert).astype(f32)
    lifted = jax.nn.sigmoid(logits) * hit
    gates = lifted / jnp.sum(lifted, axis=1, keepdims=True)
    sooner = lax.broadcasted_iota(jnp.int32, (TOK, TOK), 1)
    earlier = (sooner < lax.broadcasted_iota(jnp.int32, (TOK, TOK), 0)).astype(f32).astype(bf16)
    before = jnp.dot(earlier, hit.astype(bf16), preferred_element_type=f32)
    place = jnp.where(hit > 0, before, -1.0).astype(bf16)
    size = EXPERTS * 2 * CAP
    owner = 2 * CAP * lax.broadcasted_iota(jnp.int32, (EXPERTS, size), 0)
    offset = lax.broadcasted_iota(jnp.int32, (EXPERTS, size), 1) - owner
    inside = ((offset >= 0) & (offset < 2 * CAP)).astype(f32).astype(bf16)
    spread = jnp.dot(place, inside, preferred_element_type=f32)
    spot = lax.rem(lax.broadcasted_iota(jnp.int32, (TOK, size), 1), 2 * CAP)
    left = spread == spot.astype(f32)
    right = spread == (spot - CAP).astype(f32)
    high = gates.astype(bf16)
    low = (gates - high.astype(f32)).astype(bf16)
    for gate, ref in ((high, high_ref), (low, low_ref)):
        value = jnp.dot(gate, inside, preferred_element_type=f32)
        ref[0:TOK] = jnp.where(left & (spot < CAP), value, 0.0).astype(bf16)
        ref[TOK:] = jnp.where(right & (spot >= CAP), value, 0.0).astype(bf16)


def embed_kernel(
    here_ref, hidden_ref, high_ref, low_ref, back_ref, gain_ref, w_ref, layer_ref, part_ref
):
    mine = mine_of(here_ref)
    back = back_ref[...]
    moe = jnp.dot(high_ref[...], back, preferred_element_type=f32)
    moe = moe + jnp.dot(low_ref[...], back, preferred_element_type=f32)
    moe = jnp.concatenate([moe[0:TOK], moe[TOK:]], axis=1)
    layer = (hidden_ref[...].astype(f32) + moe).astype(bf16)
    layer_ref[...] = layer
    layer = layer.astype(f32)
    scaled = (layer * gain_ref[2:3, mine]).astype(bf16)
    part = jnp.dot(scaled, w_ref[mine, :], preferred_element_type=f32)
    square = jnp.broadcast_to(jnp.sum(layer * layer, axis=1, keepdims=True), (TOK, TOK))
    square = jnp.transpose(square)[0:8]
    for copy in range(8):
        part_ref[copy, 0:TOK, :] = part
        part_ref[copy, TOK:, :] = square


def vector_kernel(parts_ref, out_ref):
    whole = parts_ref[0]
    for n in range(1, 8):
        whole = whole + parts_ref[n]
    square = jnp.transpose(jnp.broadcast_to(whole[TOK : TOK + 1], (TOK, TOK)))
    embedded = whole[0:TOK] * lax.rsqrt(square / 2048.0 + EPS)
    norm = jnp.sum(embedded * embedded, axis=1, keepdims=True)
    vectors = (embedded * lax.rsqrt(norm + EPS)).astype(bf16)
    for copy in range(16):
        out_ref[copy] = vectors


def assemble_kernel(here_ref, p0, p1, p2, p3, out_ref):
    j = here_ref[1]
    for k, piece in enumerate((p0, p1, p2, p3)):
        part = lax.rem(j - k + 4, 4)
        out_ref[:, pl.ds(pl.multiple_of(part * 512, 512), 512)] = piece[...]


def score_kernel(info_ref, doc_ref, own_ref, other_ref, out_ref, query_ref, sems):
    def spot(d):
        return pl.multiple_of(jnp.minimum((info_ref[2, d] // 16) * 16, 2048 - 128), 16)

    def copy_of(ref, d):
        return pltpu.make_async_copy(ref.at[pl.ds(spot(d), 128), :], query_ref.at[d], sems.at[d])

    for d in range(16):

        @pl.when(info_ref[4, d] == 0)
        def _():
            copy_of(own_ref, d).start()

        @pl.when(info_ref[4, d] != 0)
        def _():
            copy_of(other_ref, d).start()

    lane = lax.broadcasted_iota(jnp.int32, (1, 16), 1)
    scores = jnp.zeros((1, 16), f32)
    rows = lax.broadcasted_iota(jnp.int32, (144, 128), 0)
    columns = lax.broadcasted_iota(jnp.int32, (1, 128), 1)
    for d in range(16):
        copy_of(own_ref, d).wait()
    for d in range(16):
        first, size = info_ref[0, d], info_ref[1, d]
        q_first, q_size = info_ref[2, d], info_ref[3, d]
        at = pl.multiple_of(jnp.minimum((first // 16) * 16, 1024 - 144), 16)
        sims = lax.dot_general(
            doc_ref[pl.ds(at, 144), :],
            query_ref[d],
            (((1,), (1,)), ((), ())),
            preferred_element_type=f32,
        )
        keep = (rows >= first - at) & (rows < first - at + size)
        best = jnp.max(jnp.where(keep, sims, NEG), axis=0, keepdims=True)
        q_start = q_first - spot(d)
        used = (columns >= q_start) & (columns < q_start + q_size)
        value = jnp.sum(jnp.where(used, best, 0.0), axis=1, keepdims=True) / q_size.astype(f32)
        scores = jnp.where(lane == d, value, scores)
    out_ref[...] = scores


def vmem():
    return pl.BlockSpec(memory_space=pltpu.VMEM)


def smem():
    return pl.BlockSpec(memory_space=pltpu.SMEM)


def hbm():
    return pl.BlockSpec(memory_space=pltpu.HBM)


def params():
    return pltpu.CompilerParams(vmem_limit_bytes=40 << 20)


def body(
    tokens,
    request_lengths,
    w_qkv,
    qk_gain,
    w_out,
    norm_gains,
    w_router,
    routes,
    w_gate,
    w_up,
    w_down,
    w_proj,
    doc_vectors,
    doc_segment,
    doc_request,
):
    i = lax.axis_index("xh")
    j = lax.axis_index("y")
    core = lax.axis_index("core")
    wide = lax.axis_index(W)
    here = jnp.stack([i, j, wide, core])

    def pick(array, which):
        return lax.dynamic_index_in_dim(array, which, 0, keepdims=False)

    def cut(array, part, axis):
        return lax.dynamic_slice_in_dim(array, lax.rem(part, 4) * 512, 512, axis)

    attn = pl.pallas_call(
        attention_kernel,
        out_shape=jax.ShapeDtypeStruct((8, TOK, 256), bf16),
        in_specs=[smem()] * 2 + [vmem()] * 2 + [hbm()] * 3,
        out_specs=vmem(),
        scratch_shapes=[
            pltpu.VMEM((TOK, 2048), bf16),
            pltpu.VMEM((3, 2048, 256), bf16),
            pltpu.VMEM((256, 2048), bf16),
            pltpu.SemaphoreType.DMA((5,)),
        ],
        compiler_params=pltpu.CompilerParams(vmem_limit_bytes=60 << 20),
        name="attention",
    )(
        here,
        request_lengths.T,
        qk_gain,
        norm_gains,
        tokens,
        w_qkv.transpose(1, 0, 2),
        w_out,
    )
    attn = lax.all_to_all(attn, N, 0, 0, tiled=True)

    choose = pl.pallas_call(
        choose_kernel,
        out_shape=jax.ShapeDtypeStruct((EXPERTS * CAP, TOK), bf16),
        in_specs=[vmem()],
        out_specs=vmem(),
        compiler_params=params(),
        name="choose",
    )(routes.T)

    hidden, rows = pl.pallas_call(
        dispatch_kernel,
        out_shape=(
            jax.ShapeDtypeStruct((TOK, 256), bf16),
            jax.ShapeDtypeStruct((EXPERTS, 2 * CAP, 128), bf16),
        ),
        in_specs=[smem()] + [vmem()] * 3,
        out_specs=(vmem(), vmem()),
        compiler_params=params(),
        name="dispatch",
    )(here, tokens, attn, choose)
    arrived = lax.all_to_all(rows, E, 0, 0, tiled=True)

    top, bottom = pl.pallas_call(
        unpack_kernel,
        out_shape=(jax.ShapeDtypeStruct((HALF, 512), bf16),) * 2,
        in_specs=[vmem()],
        out_specs=(vmem(), vmem()),
        scratch_shapes=[pltpu.VMEM((HALF, 512), f32)],
        compiler_params=params(),
        name="unpack",
    )(arrived)
    downs = [cut(w_down, j, 2)] + [y_shift(cut(w_down, j + k, 2), k) for k in (1, 2, 3)]
    both_sent = jnp.stack([pick(w_gate, 1 - i), pick(w_up, 1 - i)])
    top, bottom, both_sent, downs = lax.optimization_barrier((top, bottom, both_sent, downs))
    both_par = x_swap(both_sent)
    top_back, bottom_ahead = y_shift(top, 1), y_shift(bottom, 3)
    bottom_back, top_ahead = y_shift(bottom, 1), y_shift(top, 3)
    top_far, bottom_far = y_shift(top_back, 1), y_shift(bottom_ahead, 3)
    act = pl.pallas_call(
        gate_up_kernel,
        out_shape=jax.ShapeDtypeStruct((2 * HALF, 256), bf16),
        in_specs=[smem()] + [vmem()] * 8 + [hbm()] * 4,
        out_specs=vmem(),
        scratch_shapes=[
            pltpu.VMEM((3, 2048), f32),
            pltpu.VMEM((4, 2048, 128), bf16),
            pltpu.SemaphoreType.DMA((5,)),
        ],
        compiler_params=params(),
        name="gate_up",
    )(
        here,
        *(top, top_back, top_ahead, top_far),
        *(bottom, bottom_back, bottom_ahead, bottom_far),
        norm_gains,
        w_gate,
        w_up,
        both_par,
    )
    down_sent = jnp.stack([pick(d, 1 - i) for d in downs])
    act, down_sent = lax.optimization_barrier((act, down_sent))
    down_par = x_swap(down_sent)
    out = pl.pallas_call(
        down_kernel,
        out_shape=jax.ShapeDtypeStruct((EXPERTS, 2 * CAP, 128), bf16),
        in_specs=[smem()] + [vmem()] * 4 + [hbm()] * 5,
        out_specs=vmem(),
        scratch_shapes=[pltpu.VMEM((4, 256, 512), bf16), pltpu.SemaphoreType.DMA((2, 4))],
        compiler_params=params(),
        name="down",
    )(here, act, *(y_shift(act, k) for k in (1, 2, 3)), *downs, down_par)
    back = lax.all_to_all(out, E, 0, 0, tiled=True)

    hf = hidden.astype(f32)
    first = j * 512 + i * 256
    gain_mine = lax.dynamic_slice_in_dim(norm_gains[1], first, 256, 0)
    router_mine = lax.dynamic_slice_in_dim(w_router, first, 256, 0)
    part = jnp.dot((hf * gain_mine).astype(bf16), router_mine, preferred_element_type=f32)
    square = jnp.sum(hf * hf, axis=1, keepdims=True)
    part = jnp.concatenate([part, jnp.broadcast_to(square, (TOK, EXPERTS))], axis=1)
    whole = part
    for k in (1, 2, 3):
        whole = whole + y_shift(part, k)
    whole = whole + x_swap(whole)
    mixing = pl.pallas_call(
        mixing_kernel,
        out_shape=(jax.ShapeDtypeStruct((2 * TOK, EXPERTS * 2 * CAP), bf16),) * 2,
        in_specs=[vmem()] * 2,
        out_specs=(vmem(), vmem()),
        compiler_params=params(),
        name="mixing",
    )(whole, routes)

    layer, part = pl.pallas_call(
        embed_kernel,
        out_shape=(
            jax.ShapeDtypeStruct((TOK, 256), bf16),
            jax.ShapeDtypeStruct((8, TOK + 8, 128), f32),
        ),
        in_specs=[smem()] + [vmem()] * 6,
        out_specs=(vmem(), vmem()),
        compiler_params=params(),
        name="embed",
    )(here, hidden, *mixing, back.reshape(-1, 128), norm_gains, w_proj)
    parts = lax.all_to_all(part, N, 0, 0, tiled=True)
    layer_par = x_swap(layer)
    layer = jnp.where(i == 0, jnp.stack([layer, layer_par]), jnp.stack([layer_par, layer]))
    layer = jnp.concatenate([layer[0], layer[1]], axis=1)

    vectors = pl.pallas_call(
        vector_kernel,
        out_shape=jax.ShapeDtypeStruct((16, TOK, 128), bf16),
        in_specs=[vmem()],
        out_specs=vmem(),
        name="vectors",
    )(parts)
    vectors, layer = lax.optimization_barrier((vectors, layer))
    layers = [layer] + [y_shift(layer, k) for k in (1, 2, 3)]
    own = lax.all_to_all(vectors, ("z", "xl"), 0, 0, tiled=True).reshape(16 * TOK, 128)
    segment = doc_segment[0]
    requests = doc_request[0]
    docs = jnp.arange(16, dtype=jnp.int32)
    first = jnp.sum((segment[None, :] < docs[:, None]).astype(jnp.int32), axis=1)
    size = jnp.sum((segment[None, :] == docs[:, None]).astype(jnp.int32), axis=1)
    starts = jnp.cumsum(request_lengths, axis=1) - request_lengths
    starts = (starts + TOK * (jnp.arange(WIDE, dtype=jnp.int32) // 2)[:, None]).reshape(-1)
    match = requests[:, None] == jnp.arange(96, dtype=jnp.int32)[None, :]
    q_first = jnp.sum(jnp.where(match, starts[None, :], 0), axis=1)
    q_size = jnp.sum(jnp.where(match, request_lengths.reshape(-1)[None, :], 0), axis=1)
    away = lax.rem(requests // 3, 2) ^ core
    info = jnp.stack([first, size, q_first, q_size, away])
    own, info, *layers = lax.optimization_barrier((own, info, *layers))
    other = lax.ppermute(own, "core", [(0, 1), (1, 0)])
    layer_out = pl.pallas_call(
        assemble_kernel,
        out_shape=jax.ShapeDtypeStruct((TOK, 2048), bf16),
        in_specs=[smem()] + [vmem()] * 4,
        out_specs=vmem(),
        name="assemble",
    )(here, *layers)
    doc_scores = pl.pallas_call(
        score_kernel,
        out_shape=jax.ShapeDtypeStruct((1, 16), f32),
        in_specs=[smem(), vmem()] + [pl.BlockSpec(memory_space=pl.ANY)] * 2,
        out_specs=vmem(),
        scratch_shapes=[pltpu.VMEM((16, 128, 128), bf16), pltpu.SemaphoreType.DMA((16,))],
        name="score",
    )(info, doc_vectors, own, other)
    return (layer_out, doc_scores)


def solution(mesh):
    split = Mesh(mesh.devices.reshape(8, 2, 2, 2, 4), ("z", "xl", "core", "xh", "y"))
    placed = (
        P(W, None),
        P(),
        P(None, None, N),
        P(None, N),
        P(N, None),
        P(),
        P(),
        P(W, None),
        P(W, None, N),
        P(W, None, N),
        P(W, N, None),
        P(),
        P(W + N, None),
        P(W + N, None),
        P(W + N, None),
    )
    return jax.shard_map(
        body,
        mesh=split,
        in_specs=placed,
        out_specs=(P(W, None), P(W + N, None)),
        check_vma=False,
    )
```

```python
import math

import jax
import jax.numpy as jnp
from jax import lax
from jax.experimental import pallas as pl
from jax.experimental.pallas import tpu as pltpu
from jax.sharding import Mesh, PartitionSpec as P

HD = 128
TOPK = 8
TOK = 128
CAP = 20
EXPERTS = 64
WIDE = 32
HALF = WIDE * CAP // 2
EPS = 1e-06
THETA = 50000.0
NEG = -1e30
W = ("z", "xl", "core")
N = ("xh", "y")
f32 = jnp.float32
bf16 = jnp.bfloat16


def y_shift(x, k):
    return lax.ppermute(x, "y", [(s, (s + k) % 4) for s in range(4)])


def x_swap(x):
    return lax.ppermute(x, "xh", [(0, 1), (1, 0)])


def attention_kernel(
    here_ref,
    lengths_ref,
    qk_ref,
    gain_ref,
    x_hbm,
    w_hbm,
    out_hbm,
    gate_hbm,
    out0,
    out1,
    out2,
    out3,
    sent_hbm,
    x_ref,
    w_ref,
    out_w_ref,
    sems,
):
    copies = [pltpu.make_async_copy(x_hbm, x_ref, sems.at[0])]
    copies += [
        pltpu.make_async_copy(w_hbm.at[part], w_ref.at[part], sems.at[1 + part]) for part in range(3)
    ]
    copies += [pltpu.make_async_copy(out_hbm, out_w_ref, sems.at[4])]
    copies += [pltpu.make_async_copy(gate_hbm.at[1 - here_ref[0]], sent_hbm, sems.at[5])]
    for copy in copies:
        copy.start()
    wide = here_ref[2]
    one = lengths_ref[0, wide]
    two = one + lengths_ref[1, wide]

    def member_of(places):
        return (places >= one).astype(jnp.int32) + (places >= two).astype(jnp.int32)

    down_places = lax.broadcasted_iota(jnp.int32, (TOK, HD), 0)
    across_places = lax.broadcasted_iota(jnp.int32, (TOK, HD), 1)
    member = member_of(down_places)
    same = member == member_of(across_places)
    start = jnp.where(member == 0, 0, jnp.where(member == 1, one, two))
    half = lax.rem(across_places, HD // 2).astype(f32)
    freq = jnp.exp(half * (-math.log(THETA) / (HD // 2)))
    angle = (down_places - start).astype(f32) * freq
    cosine = jnp.cos(angle)
    sine = jnp.sin(angle)
    sine = jnp.where(across_places < HD // 2, -sine, sine)

    copies[0].wait()
    x = x_ref[...].astype(f32)
    scale = lax.rsqrt(jnp.mean(x * x, axis=1, keepdims=True) + EPS)
    normed = (x * scale * gain_ref[0:1, :]).astype(bf16)
    parts = []
    for part in range(3):
        copies[1 + part].wait()
        parts.append(jnp.dot(normed, w_ref[part], preferred_element_type=f32))
    query, keys, values = parts

    def turned(v, gain):
        v = v * lax.rsqrt(jnp.mean(v * v, axis=1, keepdims=True) + EPS) * gain
        return (v * cosine + pltpu.roll(v, HD // 2, 1) * sine).astype(bf16)

    mixed = []
    for head in range(2):
        at = slice(head * HD, (head + 1) * HD)
        q = turned(query[:, at], qk_ref[0:1, at])
        k = turned(keys[:, at], qk_ref[1:2, at])
        scores = lax.dot_general(q, k, (((1,), (1,)), ((), ())), preferred_element_type=f32)
        scores = jnp.where(same, scores * HD ** (-0.5), NEG)
        weights = jnp.exp(scores - jnp.max(scores, axis=1, keepdims=True))
        probs = (weights / jnp.sum(weights, axis=1, keepdims=True)).astype(bf16)
        mixed.append(
            jnp.dot(probs, values[:, at].astype(bf16), preferred_element_type=f32).astype(bf16)
        )
    mixed = jnp.concatenate(mixed, axis=1)
    copies[4].wait()
    j = here_ref[1]
    for k, out_ref in enumerate((out0, out1, out2, out3)):
        part = lax.rem(j + k, 4)
        columns = pl.ds(pl.multiple_of(part * 512, 512), 512)
        out_ref[...] = jnp.dot(mixed, out_w_ref[:, columns], preferred_element_type=f32).astype(bf16)
    copies[5].wait()


def choose_kernel(here_ref, routes_ref, out_ref):
    expert = 2 * lax.broadcasted_iota(jnp.int32, (WIDE, TOK), 0) + here_ref[0]
    hit = jnp.zeros((WIDE, TOK), f32)
    for k in range(TOPK):
        hit = hit + (routes_ref[k : k + 1, :] == expert).astype(f32)
    sooner = lax.broadcasted_iota(jnp.int32, (TOK, TOK), 0)
    earlier = (sooner < lax.broadcasted_iota(jnp.int32, (TOK, TOK), 1)).astype(f32).astype(bf16)
    before = jnp.dot(hit.astype(bf16), earlier, preferred_element_type=f32)
    place = jnp.where(hit > 0, before, -1.0).astype(bf16)
    owner = CAP * lax.broadcasted_iota(jnp.int32, (WIDE * CAP, WIDE), 1)
    slot = lax.broadcasted_iota(jnp.int32, (WIDE * CAP, WIDE), 0) - owner
    inside = (slot >= 0) & (slot < CAP)
    spread = jnp.dot(inside.astype(f32).astype(bf16), place, preferred_element_type=f32)
    slot = jnp.sum(jnp.where(inside, slot, 0).astype(f32), axis=1, keepdims=True)
    out_ref[...] = (spread == slot).astype(f32).astype(bf16)


def packed(rows):
    return jnp.concatenate([rows[:, 0:256], rows[:, 256:512]], axis=0).astype(bf16)


def dispatch_kernel(here_ref, x_ref, own_ref, par_ref, choose_ref, hidden_ref, rows_ref):
    j = here_ref[1]
    mine = x_ref[:, pl.ds(pl.multiple_of(j * 512, 512), 512)].astype(f32)
    hidden = (mine + (own_ref[...].astype(f32) + par_ref[...].astype(f32))).astype(bf16)
    hidden_ref[...] = hidden
    rows = jnp.dot(choose_ref[...], hidden, preferred_element_type=f32)
    for s in range(WIDE):
        rows_ref[s] = packed(rows[s * CAP : (s + 1) * CAP])


def unpack_kernel(in_ref, top_ref, bottom_ref, scratch):
    for half, out_ref in enumerate((top_ref, bottom_ref)):
        for s in range(WIDE // 2):
            rows = in_ref[half * (WIDE // 2) + s].astype(f32)
            at = slice(s * CAP, (s + 1) * CAP)
            scratch[at, 0:256] = rows[0:CAP]
            scratch[at, 256:512] = rows[CAP:]
        out_ref[...] = scratch[...].astype(bf16)


def gate_up_kernel(here_ref, *refs):
    halves = refs[0:4], refs[4:8]
    gain_hbm, gate_hbm, up_hbm, gate_par, up_par, out_ref, gain_ref, w_ref, sems = refs[8:]
    i, j = here_ref[0], here_ref[1]
    sources = (gate_hbm.at[i], up_hbm.at[i], gate_par, up_par)
    copies = [
        pltpu.make_async_copy(source, w_ref.at[n], sems.at[n]) for n, source in enumerate(sources)
    ]
    copies.append(pltpu.make_async_copy(gain_hbm, gain_ref, sems.at[4]))
    for copy in copies:
        copy.start()
    scales = []
    for xs in halves:
        total = jnp.zeros((HALF, 1), f32)
        for x in xs:
            v = x[...].astype(f32)
            total = total + jnp.sum(v * v, axis=1, keepdims=True)
        scales.append(lax.rsqrt(total / 2048.0 + EPS))
    for copy in copies:
        copy.wait()
    for half, (xs, scale) in enumerate(zip(halves, scales)):
        normed, weights = [], []
        for k, x in enumerate(xs):
            part = lax.rem(j + 4 + (0, -1, 1, 2)[k], 4)
            rows = pl.ds(pl.multiple_of(part * 512, 512), 512)
            normed.append((x[...].astype(f32) * scale * gain_ref[1:2, rows]).astype(bf16))
            weights.append(jnp.concatenate([w_ref[n, rows, :] for n in range(4)], axis=1))
        both = jnp.dot(
            jnp.concatenate(normed, axis=1),
            jnp.concatenate(weights, axis=0),
            preferred_element_type=f32,
        )
        own, par = both[:, 0:256], both[:, 256:512]
        for at, both in ((0, own), (128, par)):
            gate, up = both[:, :128], both[:, 128:]
            out_ref[half * HALF : (half + 1) * HALF, at : at + 128] = (
                gate / (1.0 + jnp.exp(-gate)) * up
            ).astype(bf16)


def down_kernel(here_ref, a0, a1, a2, a3, w0, w1, w2, w3, par_ref, out_ref, w_ref, sems):
    i = here_ref[0]
    copies = []
    for k, w in enumerate((w0, w1, w2, w3)):
        copies.append(
            (
                pltpu.make_async_copy(w.at[i], w_ref.at[k, 0:128], sems.at[0, k]),
                pltpu.make_async_copy(par_ref.at[k], w_ref.at[k, 128:256], sems.at[1, k]),
            )
        )
    for pair in copies:
        for copy in pair:
            copy.start()
    for pair in copies:
        for copy in pair:
            copy.wait()
    total = jnp.dot(
        jnp.concatenate([a0[...], a1[...], a2[...], a3[...]], axis=1),
        jnp.concatenate([w_ref[k] for k in range(4)], axis=0),
        preferred_element_type=f32,
    )
    size = out_ref.shape[1]
    for s in range(WIDE):
        out_ref[s] = total[s * size : (s + 1) * size].astype(bf16)


def embed_kernel(here_ref, hidden_ref, moe_ref, par_ref, gain_ref, w_ref, layer_ref, part_ref):
    mine = pl.ds(pl.multiple_of(here_ref[1] * 512, 512), 512)
    layer = hidden_ref[...].astype(f32) + (moe_ref[...].astype(f32) + par_ref[...].astype(f32))
    layer = layer.astype(bf16)
    layer_ref[...] = layer
    layer = layer.astype(f32)
    scaled = (layer * gain_ref[2:3, mine]).astype(bf16)
    part_ref[0:TOK, :] = jnp.dot(scaled, w_ref[mine, :], preferred_element_type=f32)
    square = jnp.broadcast_to(jnp.sum(layer * layer, axis=1, keepdims=True), (TOK, TOK))
    part_ref[TOK:, :] = jnp.transpose(square)[0:8]


def vector_kernel(p0, p1, p2, p3, out_ref):
    whole = p0[...] + p1[...] + p2[...] + p3[...]
    square = jnp.transpose(jnp.broadcast_to(whole[TOK : TOK + 1], (TOK, TOK)))
    embedded = whole[0:TOK] * lax.rsqrt(square / 2048.0 + EPS)
    norm = jnp.sum(embedded * embedded, axis=1, keepdims=True)
    vectors = (embedded * lax.rsqrt(norm + EPS)).astype(bf16)
    for copy in range(16):
        out_ref[copy] = vectors


def assemble_kernel(here_ref, p0, p1, p2, p3, out_ref):
    j = here_ref[1]
    for k, piece in enumerate((p0, p1, p2, p3)):
        part = lax.rem(j - k + 4, 4)
        out_ref[:, pl.ds(pl.multiple_of(part * 512, 512), 512)] = piece[...]


def score_kernel(info_ref, doc_ref, own_ref, other_ref, out_ref, query_ref, sems):
    def spot(d):
        return pl.multiple_of(jnp.minimum((info_ref[2, d] // 16) * 16, 2048 - 128), 16)

    def copy_of(ref, d):
        return pltpu.make_async_copy(ref.at[pl.ds(spot(d), 128), :], query_ref.at[d], sems.at[d])

    for d in range(16):

        @pl.when(info_ref[4, d] == 0)
        def _():
            copy_of(own_ref, d).start()

        @pl.when(info_ref[4, d] != 0)
        def _():
            copy_of(other_ref, d).start()

    lane = lax.broadcasted_iota(jnp.int32, (1, 16), 1)
    scores = jnp.zeros((1, 16), f32)
    rows = lax.broadcasted_iota(jnp.int32, (144, 128), 0)
    columns = lax.broadcasted_iota(jnp.int32, (1, 128), 1)
    for d in range(16):
        copy_of(own_ref, d).wait()
    for d in range(16):
        first, size = info_ref[0, d], info_ref[1, d]
        q_first, q_size = info_ref[2, d], info_ref[3, d]
        at = pl.multiple_of(jnp.minimum((first // 16) * 16, 1024 - 144), 16)
        sims = lax.dot_general(
            doc_ref[pl.ds(at, 144), :],
            query_ref[d],
            (((1,), (1,)), ((), ())),
            preferred_element_type=f32,
        )
        keep = (rows >= first - at) & (rows < first - at + size)
        best = jnp.max(jnp.where(keep, sims, NEG), axis=0, keepdims=True)
        q_start = q_first - spot(d)
        used = (columns >= q_start) & (columns < q_start + q_size)
        value = jnp.sum(jnp.where(used, best, 0.0), axis=1, keepdims=True) / q_size.astype(f32)
        scores = jnp.where(lane == d, value, scores)
    out_ref[...] = scores


def vmem():
    return pl.BlockSpec(memory_space=pltpu.VMEM)


def smem():
    return pl.BlockSpec(memory_space=pltpu.SMEM)


def hbm():
    return pl.BlockSpec(memory_space=pltpu.HBM)


def params():
    return pltpu.CompilerParams(vmem_limit_bytes=40 << 20)


def body(
    tokens,
    request_lengths,
    w_qkv,
    qk_gain,
    w_out,
    norm_gains,
    w_router,
    routes,
    w_gate,
    w_up,
    w_down,
    w_proj,
    doc_vectors,
    doc_segment,
    doc_request,
):
    i = lax.axis_index("xh")
    j = lax.axis_index("y")
    core = lax.axis_index("core")
    wide = lax.axis_index(W)
    here = jnp.stack([i, j, wide, core])

    def pick(array, which):
        return lax.dynamic_index_in_dim(array, which, 0, keepdims=False)

    def cut(array, part, axis):
        return lax.dynamic_slice_in_dim(array, lax.rem(part, 4) * 512, 512, axis)

    *attn, gate_sent = pl.pallas_call(
        attention_kernel,
        out_shape=(
            *(jax.ShapeDtypeStruct((TOK, 512), bf16),) * 4,
            jax.ShapeDtypeStruct((2048, 128), bf16),
        ),
        in_specs=[smem()] * 2 + [vmem()] * 2 + [hbm()] * 4,
        out_specs=(*(vmem(),) * 4, hbm()),
        scratch_shapes=[
            pltpu.VMEM((TOK, 2048), bf16),
            pltpu.VMEM((3, 2048, 256), bf16),
            pltpu.VMEM((256, 2048), bf16),
            pltpu.SemaphoreType.DMA((6,)),
        ],
        compiler_params=pltpu.CompilerParams(vmem_limit_bytes=60 << 20),
        name="attention",
    )(
        here,
        request_lengths.T,
        qk_gain,
        norm_gains,
        tokens,
        w_qkv.transpose(1, 0, 2),
        w_out,
        w_gate,
    )
    gate_par = x_swap(gate_sent)
    attn_parts = [y_shift(attn[k], k) for k in (1, 2, 3)]

    downs = [cut(w_down, j, 2)] + [y_shift(cut(w_down, j + k, 2), k) for k in (1, 2, 3)]
    down_sent = jnp.stack([pick(d, 1 - i) for d in downs])

    experts_here = 2 * jnp.arange(WIDE, dtype=jnp.int32) + i
    hit = jnp.sum((routes.T[None, :, :] == experts_here[:, None, None]).astype(f32), axis=1)
    places = jnp.arange(TOK, dtype=jnp.int32)
    earlier = (places[:, None] < places[None, :]).astype(bf16)
    before = jnp.dot(hit.astype(bf16), earlier, preferred_element_type=f32)
    slot = jnp.arange(CAP, dtype=jnp.int32).astype(f32)
    chosen = (before[:, None, :] == slot[None, :, None]) & (hit[:, None, :] > 0)
    choose = pl.pallas_call(
        choose_kernel,
        out_shape=jax.ShapeDtypeStruct((WIDE * CAP, TOK), bf16),
        in_specs=[smem(), vmem()],
        out_specs=vmem(),
        compiler_params=params(),
        name="choose",
    )(here, routes.T)

    attn = (attn[0].astype(f32) + sum(p.astype(f32) for p in attn_parts)).astype(bf16)
    attn, choose = lax.optimization_barrier((attn, choose))
    attn_par = x_swap(attn)
    attn_par, gate_par = lax.optimization_barrier((attn_par, gate_par))
    hidden, rows = pl.pallas_call(
        dispatch_kernel,
        out_shape=(
            jax.ShapeDtypeStruct((TOK, 512), bf16),
            jax.ShapeDtypeStruct((WIDE, 2 * CAP, 256), bf16),
        ),
        in_specs=[smem()] + [vmem()] * 4,
        out_specs=(vmem(), vmem()),
        compiler_params=params(),
        name="dispatch",
    )(here, tokens, attn, attn_par, choose)

    arrived = lax.all_to_all(rows, W, 0, 0, tiled=True)
    top, bottom = pl.pallas_call(
        unpack_kernel,
        out_shape=(jax.ShapeDtypeStruct((HALF, 512), bf16),) * 2,
        in_specs=[vmem()],
        out_specs=(vmem(), vmem()),
        scratch_shapes=[pltpu.VMEM((HALF, 512), f32)],
        compiler_params=params(),
        name="unpack",
    )(arrived)
    top, bottom, up_sent, down_sent = lax.optimization_barrier(
        (top, bottom, pick(w_up, 1 - i), down_sent)
    )
    up_par = x_swap(up_sent)
    top_back, bottom_ahead = y_shift(top, 1), y_shift(bottom, 3)
    bottom_back, top_ahead = y_shift(bottom, 1), y_shift(top, 3)
    top_far, bottom_far = y_shift(top_back, 1), y_shift(bottom_ahead, 3)
    top_ahead, down_sent = lax.optimization_barrier((top_ahead, down_sent))
    down_par = x_swap(down_sent)
    act = pl.pallas_call(
        gate_up_kernel,
        out_shape=jax.ShapeDtypeStruct((2 * HALF, 256), bf16),
        in_specs=[smem()] + [vmem()] * 8 + [hbm()] * 5,
        out_specs=vmem(),
        scratch_shapes=[
            pltpu.VMEM((3, 2048), f32),
            pltpu.VMEM((4, 2048, 128), bf16),
            pltpu.SemaphoreType.DMA((5,)),
        ],
        compiler_params=params(),
        name="gate_up",
    )(
        here,
        *(top, top_back, top_ahead, top_far),
        *(bottom, bottom_back, bottom_ahead, bottom_far),
        norm_gains,
        w_gate,
        w_up,
        gate_par,
        up_par,
    )
    out = pl.pallas_call(
        down_kernel,
        out_shape=jax.ShapeDtypeStruct((WIDE, CAP, 512), bf16),
        in_specs=[smem()] + [vmem()] * 4 + [hbm()] * 5,
        out_specs=vmem(),
        scratch_shapes=[pltpu.VMEM((4, 256, 512), bf16), pltpu.SemaphoreType.DMA((2, 4))],
        compiler_params=params(),
        name="down",
    )(here, act, *(y_shift(act, k) for k in (1, 2, 3)), *downs, down_par)
    back = lax.all_to_all(out, W, 0, 0, tiled=True)

    hf = hidden.astype(f32)
    gain_mine = lax.dynamic_slice_in_dim(norm_gains[1], j * 512, 512, 0)
    router_mine = lax.dynamic_slice_in_dim(w_router, j * 512, 512, 0)
    part = jnp.dot((hf * gain_mine).astype(bf16), router_mine, preferred_element_type=f32)
    square = jnp.sum(hf * hf, axis=1, keepdims=True)
    part = jnp.concatenate([part, jnp.broadcast_to(square, (TOK, EXPERTS))], axis=1)
    whole = part
    for k in (1, 2, 3):
        whole = whole + y_shift(part, k)
    logits = whole[:, :EXPERTS] * lax.rsqrt(whole[:, EXPERTS : EXPERTS + 1] / 2048.0 + EPS)
    lifted = jax.nn.sigmoid(logits)
    onehot = jnp.sum(
        (routes[:, :, None] == jnp.arange(EXPERTS, dtype=jnp.int32)[None, None, :]).astype(f32),
        axis=1,
    )
    lifted = lifted * onehot
    gates = lifted / jnp.sum(lifted, axis=1, keepdims=True)
    gates = lax.dynamic_index_in_dim(gates.reshape(TOK, WIDE, 2), i, 2, keepdims=False).T

    moe = jnp.zeros((TOK, 512), f32)
    contract = (((0, 1), (0, 1)), ((), ()))
    mixing = jnp.where(chosen, gates[:, None, :], 0.0)
    mixing_hi = lax.reduce_precision(mixing, 8, 7)
    mixing_lo = (mixing - mixing_hi).astype(bf16)
    for matrix in (mixing_hi.astype(bf16), mixing_lo):
        moe = moe + lax.dot_general(matrix, back, contract, preferred_element_type=f32)
    moe = moe.astype(bf16)
    moe_par = x_swap(moe)
    layer, part = pl.pallas_call(
        embed_kernel,
        out_shape=(
            jax.ShapeDtypeStruct((TOK, 512), bf16),
            jax.ShapeDtypeStruct((TOK + 8, 128), f32),
        ),
        in_specs=[smem()] + [vmem()] * 5,
        out_specs=(vmem(), vmem()),
        name="embed",
    )(here, hidden, moe, moe_par, norm_gains, w_proj)
    parts = [part] + [y_shift(part, k) for k in (1, 2, 3)]

    vectors = pl.pallas_call(
        vector_kernel,
        out_shape=jax.ShapeDtypeStruct((16, TOK, 128), bf16),
        in_specs=[vmem()] * 4,
        out_specs=vmem(),
        name="vectors",
    )(*parts)
    vectors, layer = lax.optimization_barrier((vectors, layer))
    layers = [layer] + [y_shift(layer, k) for k in (1, 2, 3)]
    own = lax.all_to_all(vectors, ("z", "xl"), 0, 0, tiled=True).reshape(16 * TOK, 128)
    segment = doc_segment[0]
    requests = doc_request[0]
    docs = jnp.arange(16, dtype=jnp.int32)
    first = jnp.sum((segment[None, :] < docs[:, None]).astype(jnp.int32), axis=1)
    size = jnp.sum((segment[None, :] == docs[:, None]).astype(jnp.int32), axis=1)
    starts = jnp.cumsum(request_lengths, axis=1) - request_lengths
    starts = (starts + TOK * (jnp.arange(WIDE, dtype=jnp.int32) // 2)[:, None]).reshape(-1)
    match = requests[:, None] == jnp.arange(96, dtype=jnp.int32)[None, :]
    q_first = jnp.sum(jnp.where(match, starts[None, :], 0), axis=1)
    q_size = jnp.sum(jnp.where(match, request_lengths.reshape(-1)[None, :], 0), axis=1)
    away = lax.rem(requests // 3, 2) ^ core
    info = jnp.stack([first, size, q_first, q_size, away])
    own, info, *layers = lax.optimization_barrier((own, info, *layers))
    other = lax.ppermute(own, "core", [(0, 1), (1, 0)])
    layer_out = pl.pallas_call(
        assemble_kernel,
        out_shape=jax.ShapeDtypeStruct((TOK, 2048), bf16),
        in_specs=[smem()] + [vmem()] * 4,
        out_specs=vmem(),
        name="assemble",
    )(here, *layers)
    doc_scores = pl.pallas_call(
        score_kernel,
        out_shape=jax.ShapeDtypeStruct((1, 16), f32),
        in_specs=[smem(), vmem()] + [pl.BlockSpec(memory_space=pl.ANY)] * 2,
        out_specs=vmem(),
        scratch_shapes=[pltpu.VMEM((16, 128, 128), bf16), pltpu.SemaphoreType.DMA((16,))],
        name="score",
    )(info, doc_vectors, own, other)
    return (layer_out, doc_scores)


def solution(mesh):
    split = Mesh(mesh.devices.reshape(8, 2, 2, 2, 4), ("z", "xl", "core", "xh", "y"))
    placed = (
        P(W, None),
        P(),
        P(None, None, N),
        P(None, N),
        P(N, None),
        P(),
        P(),
        P(W, None),
        P(W, None, N),
        P(W, None, N),
        P(W, N, None),
        P(),
        P(W + N, None),
        P(W + N, None),
        P(W + N, None),
    )
    return jax.shard_map(
        body,
        mesh=split,
        in_specs=placed,
        out_specs=(P(W, None), P(W + N, None)),
        check_vma=False,
    )
```

```python
import math

import jax
import jax.numpy as jnp
from jax import lax
from jax.experimental import pallas as pl
from jax.experimental.pallas import tpu as pltpu
from jax.sharding import Mesh, PartitionSpec as P

HD = 128
TOPK = 8
TOK = 128
CAP = 20
EXPERTS = 64
WIDE = 32
HALF = WIDE * CAP // 2
EPS = 1e-06
THETA = 50000.0
NEG = -1e30
W = ("z", "xl", "core")
N = ("xh", "y")
f32 = jnp.float32
bf16 = jnp.bfloat16


def y_shift(x, k):
    return lax.ppermute(x, "y", [(s, (s + k) % 4) for s in range(4)])


def x_swap(x):
    return lax.ppermute(x, "xh", [(0, 1), (1, 0)])


def attention_kernel(
    here_ref,
    lengths_ref,
    qk_ref,
    gain_ref,
    x_hbm,
    w_hbm,
    out_hbm,
    gate_hbm,
    out0,
    out1,
    out2,
    out3,
    sent_ref,
    x_ref,
    w_ref,
    out_w_ref,
    sems,
):
    copies = [pltpu.make_async_copy(x_hbm, x_ref, sems.at[0])]
    copies += [
        pltpu.make_async_copy(w_hbm.at[part], w_ref.at[part], sems.at[1 + part]) for part in range(3)
    ]
    copies += [pltpu.make_async_copy(out_hbm, out_w_ref, sems.at[4])]
    copies += [pltpu.make_async_copy(gate_hbm.at[1 - here_ref[0]], sent_ref, sems.at[5])]
    for copy in copies:
        copy.start()
    wide = here_ref[2]
    one = lengths_ref[0, wide]
    two = one + lengths_ref[1, wide]

    def member_of(places):
        return (places >= one).astype(jnp.int32) + (places >= two).astype(jnp.int32)

    down_places = lax.broadcasted_iota(jnp.int32, (TOK, HD), 0)
    across_places = lax.broadcasted_iota(jnp.int32, (TOK, HD), 1)
    member = member_of(down_places)
    same = member == member_of(across_places)
    start = jnp.where(member == 0, 0, jnp.where(member == 1, one, two))
    half = lax.rem(across_places, HD // 2).astype(f32)
    freq = jnp.exp(half * (-math.log(THETA) / (HD // 2)))
    angle = (down_places - start).astype(f32) * freq
    cosine = jnp.cos(angle)
    sine = jnp.sin(angle)
    sine = jnp.where(across_places < HD // 2, -sine, sine)

    copies[0].wait()
    x = x_ref[...].astype(f32)
    scale = lax.rsqrt(jnp.mean(x * x, axis=1, keepdims=True) + EPS)
    normed = (x * scale * gain_ref[0:1, :]).astype(bf16)
    parts = []
    for part in range(3):
        copies[1 + part].wait()
        parts.append(jnp.dot(normed, w_ref[part], preferred_element_type=f32))
    query, keys, values = parts

    def turned(v, gain):
        v = v * lax.rsqrt(jnp.mean(v * v, axis=1, keepdims=True) + EPS) * gain
        return (v * cosine + pltpu.roll(v, HD // 2, 1) * sine).astype(bf16)

    mixed = []
    for head in range(2):
        at = slice(head * HD, (head + 1) * HD)
        q = turned(query[:, at], qk_ref[0:1, at])
        k = turned(keys[:, at], qk_ref[1:2, at])
        scores = lax.dot_general(q, k, (((1,), (1,)), ((), ())), preferred_element_type=f32)
        scores = jnp.where(same, scores * HD ** (-0.5), NEG)
        weights = jnp.exp(scores - jnp.max(scores, axis=1, keepdims=True))
        probs = (weights / jnp.sum(weights, axis=1, keepdims=True)).astype(bf16)
        mixed.append(
            jnp.dot(probs, values[:, at].astype(bf16), preferred_element_type=f32).astype(bf16)
        )
    mixed = jnp.concatenate(mixed, axis=1)
    copies[4].wait()
    j = here_ref[1]
    for k, out_ref in enumerate((out0, out1, out2, out3)):
        part = lax.rem(j + k, 4)
        columns = pl.ds(pl.multiple_of(part * 512, 512), 512)
        out_ref[...] = jnp.dot(mixed, out_w_ref[:, columns], preferred_element_type=f32).astype(bf16)
    copies[5].wait()


def choose_kernel(here_ref, routes_ref, out_ref):
    expert = 2 * lax.broadcasted_iota(jnp.int32, (WIDE, TOK), 0) + here_ref[0]
    hit = jnp.zeros((WIDE, TOK), f32)
    for k in range(TOPK):
        hit = hit + (routes_ref[k : k + 1, :] == expert).astype(f32)
    sooner = lax.broadcasted_iota(jnp.int32, (TOK, TOK), 0)
    earlier = (sooner < lax.broadcasted_iota(jnp.int32, (TOK, TOK), 1)).astype(f32).astype(bf16)
    before = jnp.dot(hit.astype(bf16), earlier, preferred_element_type=f32)
    place = jnp.where(hit > 0, before, -1.0).astype(bf16)
    owner = CAP * lax.broadcasted_iota(jnp.int32, (WIDE * CAP, WIDE), 1)
    slot = lax.broadcasted_iota(jnp.int32, (WIDE * CAP, WIDE), 0) - owner
    inside = (slot >= 0) & (slot < CAP)
    spread = jnp.dot(inside.astype(f32).astype(bf16), place, preferred_element_type=f32)
    slot = jnp.sum(jnp.where(inside, slot, 0).astype(f32), axis=1, keepdims=True)
    out_ref[...] = (spread == slot).astype(f32).astype(bf16)


def packed(rows):
    return jnp.concatenate([rows[:, 0:256], rows[:, 256:512]], axis=0).astype(bf16)


def dispatch_kernel(here_ref, x_ref, own_ref, par_ref, choose_ref, hidden_ref, rows_ref):
    j = here_ref[1]
    mine = x_ref[:, pl.ds(pl.multiple_of(j * 512, 512), 512)].astype(f32)
    hidden = (mine + (own_ref[...].astype(f32) + par_ref[...].astype(f32))).astype(bf16)
    hidden_ref[...] = hidden
    rows = jnp.dot(choose_ref[...], hidden, preferred_element_type=f32)
    for s in range(WIDE):
        rows_ref[s] = packed(rows[s * CAP : (s + 1) * CAP])


def unpack_kernel(in_ref, top_ref, bottom_ref, scratch):
    for half, out_ref in enumerate((top_ref, bottom_ref)):
        for s in range(WIDE // 2):
            rows = in_ref[half * (WIDE // 2) + s].astype(f32)
            at = slice(s * CAP, (s + 1) * CAP)
            scratch[at, 0:256] = rows[0:CAP]
            scratch[at, 256:512] = rows[CAP:]
        out_ref[...] = scratch[...].astype(bf16)


def gate_up_kernel(here_ref, *refs):
    halves = refs[0:4], refs[4:8]
    gain_hbm, gate_hbm, up_hbm, gate_par, up_par, out_ref, gain_ref, w_ref, sems = refs[8:]
    i, j = here_ref[0], here_ref[1]
    sources = (gate_hbm.at[i], up_hbm.at[i], gate_par, up_par)
    copies = [
        pltpu.make_async_copy(source, w_ref.at[n], sems.at[n]) for n, source in enumerate(sources)
    ]
    copies.append(pltpu.make_async_copy(gain_hbm, gain_ref, sems.at[4]))
    for copy in copies:
        copy.start()
    scales = []
    for xs in halves:
        total = jnp.zeros((HALF, 1), f32)
        for x in xs:
            v = x[...].astype(f32)
            total = total + jnp.sum(v * v, axis=1, keepdims=True)
        scales.append(lax.rsqrt(total / 2048.0 + EPS))
    for copy in copies:
        copy.wait()
    for half, (xs, scale) in enumerate(zip(halves, scales)):
        own = jnp.zeros((HALF, 256), f32)
        par = jnp.zeros((HALF, 256), f32)
        for k, x in enumerate(xs):
            part = lax.rem(j + 4 + (0, -1, 1, 2)[k], 4)
            rows = pl.ds(pl.multiple_of(part * 512, 512), 512)
            normed = (x[...].astype(f32) * scale * gain_ref[1:2, rows]).astype(bf16)
            w_own = jnp.concatenate([w_ref[0, rows, :], w_ref[1, rows, :]], axis=1)
            w_par = jnp.concatenate([w_ref[2, rows, :], w_ref[3, rows, :]], axis=1)
            own = own + jnp.dot(normed, w_own, preferred_element_type=f32)
            par = par + jnp.dot(normed, w_par, preferred_element_type=f32)
        for at, both in ((0, own), (128, par)):
            gate, up = both[:, :128], both[:, 128:]
            out_ref[half * HALF : (half + 1) * HALF, at : at + 128] = (
                gate / (1.0 + jnp.exp(-gate)) * up
            ).astype(bf16)


def down_kernel(here_ref, a0, a1, a2, a3, w0, w1, w2, w3, par_ref, out_ref, w_ref, sems):
    i = here_ref[0]
    copies = []
    for k, w in enumerate((w0, w1, w2, w3)):
        copies.append(
            (
                pltpu.make_async_copy(w.at[i], w_ref.at[k, 0:128], sems.at[0, k]),
                pltpu.make_async_copy(par_ref.at[k], w_ref.at[k, 128:256], sems.at[1, k]),
            )
        )
    for pair in copies:
        for copy in pair:
            copy.start()
    total = jnp.zeros((a0.shape[0], 512), f32)
    for k, a in enumerate((a0, a1, a2, a3)):
        for copy in copies[k]:
            copy.wait()
        total = total + jnp.dot(a[...], w_ref[k], preferred_element_type=f32)
    size = out_ref.shape[1]
    for s in range(WIDE):
        out_ref[s] = total[s * size : (s + 1) * size].astype(bf16)


def embed_kernel(here_ref, hidden_ref, moe_ref, par_ref, gain_ref, w_ref, layer_ref, part_ref):
    mine = pl.ds(pl.multiple_of(here_ref[1] * 512, 512), 512)
    layer = hidden_ref[...].astype(f32) + (moe_ref[...].astype(f32) + par_ref[...].astype(f32))
    layer = layer.astype(bf16)
    layer_ref[...] = layer
    layer = layer.astype(f32)
    scaled = (layer * gain_ref[2:3, mine]).astype(bf16)
    part_ref[0:TOK, :] = jnp.dot(scaled, w_ref[mine, :], preferred_element_type=f32)
    square = jnp.broadcast_to(jnp.sum(layer * layer, axis=1, keepdims=True), (TOK, TOK))
    part_ref[TOK:, :] = jnp.transpose(square)[0:8]


def vector_kernel(p0, p1, p2, p3, out_ref):
    whole = p0[...] + p1[...] + p2[...] + p3[...]
    square = jnp.transpose(jnp.broadcast_to(whole[TOK : TOK + 1], (TOK, TOK)))
    embedded = whole[0:TOK] * lax.rsqrt(square / 2048.0 + EPS)
    norm = jnp.sum(embedded * embedded, axis=1, keepdims=True)
    vectors = (embedded * lax.rsqrt(norm + EPS)).astype(bf16)
    for copy in range(16):
        out_ref[copy] = vectors


def assemble_kernel(here_ref, p0, p1, p2, p3, out_ref):
    j = here_ref[1]
    for k, piece in enumerate((p0, p1, p2, p3)):
        part = lax.rem(j - k + 4, 4)
        out_ref[:, pl.ds(pl.multiple_of(part * 512, 512), 512)] = piece[...]


def score_kernel(info_ref, doc_ref, own_ref, other_ref, out_ref, query_ref, sems):
    def spot(d):
        return pl.multiple_of(jnp.minimum((info_ref[2, d] // 16) * 16, 2048 - 128), 16)

    def copy_of(ref, d):
        return pltpu.make_async_copy(ref.at[pl.ds(spot(d), 128), :], query_ref.at[d], sems.at[d])

    for d in range(16):

        @pl.when(info_ref[4, d] == 0)
        def _():
            copy_of(own_ref, d).start()

        @pl.when(info_ref[4, d] != 0)
        def _():
            copy_of(other_ref, d).start()

    lane = lax.broadcasted_iota(jnp.int32, (1, 16), 1)
    scores = jnp.zeros((1, 16), f32)
    rows = lax.broadcasted_iota(jnp.int32, (144, 128), 0)
    columns = lax.broadcasted_iota(jnp.int32, (1, 128), 1)
    for d in range(16):
        copy_of(own_ref, d).wait()
    for d in range(16):
        first, size = info_ref[0, d], info_ref[1, d]
        q_first, q_size = info_ref[2, d], info_ref[3, d]
        at = pl.multiple_of(jnp.minimum((first // 16) * 16, 1024 - 144), 16)
        sims = lax.dot_general(
            doc_ref[pl.ds(at, 144), :],
            query_ref[d],
            (((1,), (1,)), ((), ())),
            preferred_element_type=f32,
        )
        keep = (rows >= first - at) & (rows < first - at + size)
        best = jnp.max(jnp.where(keep, sims, NEG), axis=0, keepdims=True)
        q_start = q_first - spot(d)
        used = (columns >= q_start) & (columns < q_start + q_size)
        value = jnp.sum(jnp.where(used, best, 0.0), axis=1, keepdims=True) / q_size.astype(f32)
        scores = jnp.where(lane == d, value, scores)
    out_ref[...] = scores


def vmem():
    return pl.BlockSpec(memory_space=pltpu.VMEM)


def smem():
    return pl.BlockSpec(memory_space=pltpu.SMEM)


def hbm():
    return pl.BlockSpec(memory_space=pltpu.HBM)


def anywhere():
    return pl.BlockSpec(memory_space=pl.ANY)


def params():
    return pltpu.CompilerParams(vmem_limit_bytes=16 << 20)


def body(
    tokens,
    request_lengths,
    w_qkv,
    qk_gain,
    w_out,
    norm_gains,
    w_router,
    routes,
    w_gate,
    w_up,
    w_down,
    w_proj,
    doc_vectors,
    doc_segment,
    doc_request,
):
    i = lax.axis_index("xh")
    j = lax.axis_index("y")
    core = lax.axis_index("core")
    wide = lax.axis_index(W)
    here = jnp.stack([i, j, wide, core])

    def pick(array, which):
        return lax.dynamic_index_in_dim(array, which, 0, keepdims=False)

    def cut(array, part, axis):
        return lax.dynamic_slice_in_dim(array, lax.rem(part, 4) * 512, 512, axis)

    *attn, gate_sent = pl.pallas_call(
        attention_kernel,
        out_shape=(
            *(jax.ShapeDtypeStruct((TOK, 512), bf16),) * 4,
            jax.ShapeDtypeStruct((2048, 128), bf16),
        ),
        in_specs=[smem()] * 2 + [vmem()] * 2 + [hbm()] * 4,
        out_specs=(vmem(),) * 5,
        scratch_shapes=[
            pltpu.VMEM((TOK, 2048), bf16),
            pltpu.VMEM((3, 2048, 256), bf16),
            pltpu.VMEM((256, 2048), bf16),
            pltpu.SemaphoreType.DMA((6,)),
        ],
        compiler_params=pltpu.CompilerParams(vmem_limit_bytes=60 << 20),
        name="attention",
    )(
        here,
        request_lengths.T,
        qk_gain,
        norm_gains,
        tokens,
        w_qkv.transpose(1, 0, 2),
        w_out,
        w_gate,
    )
    gate_par = x_swap(gate_sent)
    attn_parts = [y_shift(attn[k], k) for k in (1, 2, 3)]

    downs = [cut(w_down, j, 2)] + [y_shift(cut(w_down, j + k, 2), k) for k in (1, 2, 3)]
    down_par = x_swap(jnp.stack([pick(d, 1 - i) for d in downs]))

    experts_here = 2 * jnp.arange(WIDE, dtype=jnp.int32) + i
    hit = jnp.sum((routes.T[None, :, :] == experts_here[:, None, None]).astype(f32), axis=1)
    places = jnp.arange(TOK, dtype=jnp.int32)
    earlier = (places[:, None] < places[None, :]).astype(bf16)
    before = jnp.dot(hit.astype(bf16), earlier, preferred_element_type=f32)
    slot = jnp.arange(CAP, dtype=jnp.int32).astype(f32)
    chosen = (before[:, None, :] == slot[None, :, None]) & (hit[:, None, :] > 0)
    choose = pl.pallas_call(
        choose_kernel,
        out_shape=jax.ShapeDtypeStruct((WIDE * CAP, TOK), bf16),
        in_specs=[smem(), vmem()],
        out_specs=vmem(),
        compiler_params=params(),
        name="choose",
    )(here, routes.T)

    attn = (attn[0].astype(f32) + sum(p.astype(f32) for p in attn_parts)).astype(bf16)
    attn, choose = lax.optimization_barrier((attn, choose))
    attn_par = x_swap(attn)
    attn_par, gate_par = lax.optimization_barrier((attn_par, gate_par))
    hidden, rows = pl.pallas_call(
        dispatch_kernel,
        out_shape=(
            jax.ShapeDtypeStruct((TOK, 512), bf16),
            jax.ShapeDtypeStruct((WIDE, 2 * CAP, 256), bf16),
        ),
        in_specs=[smem()] + [vmem()] * 4,
        out_specs=(vmem(), vmem()),
        compiler_params=params(),
        name="dispatch",
    )(here, tokens, attn, attn_par, choose)

    arrived = lax.all_to_all(rows, W, 0, 0, tiled=True)
    top, bottom = pl.pallas_call(
        unpack_kernel,
        out_shape=(jax.ShapeDtypeStruct((HALF, 512), bf16),) * 2,
        in_specs=[vmem()],
        out_specs=(vmem(), vmem()),
        scratch_shapes=[pltpu.VMEM((HALF, 512), f32)],
        compiler_params=params(),
        name="unpack",
    )(arrived)
    top, bottom, up_sent = lax.optimization_barrier((top, bottom, pick(w_up, 1 - i)))
    up_par = x_swap(up_sent)
    top_back, bottom_ahead = y_shift(top, 1), y_shift(bottom, 3)
    bottom_back, top_ahead = y_shift(bottom, 1), y_shift(top, 3)
    top_far, bottom_far = y_shift(top_back, 1), y_shift(bottom_ahead, 3)
    act = pl.pallas_call(
        gate_up_kernel,
        out_shape=jax.ShapeDtypeStruct((2 * HALF, 256), bf16),
        in_specs=[smem()] + [vmem()] * 8 + [anywhere()] * 5,
        out_specs=vmem(),
        scratch_shapes=[
            pltpu.VMEM((3, 2048), f32),
            pltpu.VMEM((4, 2048, 128), bf16),
            pltpu.SemaphoreType.DMA((5,)),
        ],
        compiler_params=params(),
        name="gate_up",
    )(
        here,
        *(top, top_back, top_ahead, top_far),
        *(bottom, bottom_back, bottom_ahead, bottom_far),
        norm_gains,
        w_gate,
        w_up,
        gate_par,
        up_par,
    )
    out = pl.pallas_call(
        down_kernel,
        out_shape=jax.ShapeDtypeStruct((WIDE, CAP, 512), bf16),
        in_specs=[smem()] + [vmem()] * 4 + [anywhere()] * 5,
        out_specs=vmem(),
        scratch_shapes=[pltpu.VMEM((4, 256, 512), bf16), pltpu.SemaphoreType.DMA((2, 4))],
        compiler_params=params(),
        name="down",
    )(here, act, *(y_shift(act, k) for k in (1, 2, 3)), *downs, down_par)
    back = lax.all_to_all(out, W, 0, 0, tiled=True)

    hf = hidden.astype(f32)
    gain_mine = lax.dynamic_slice_in_dim(norm_gains[1], j * 512, 512, 0)
    router_mine = lax.dynamic_slice_in_dim(w_router, j * 512, 512, 0)
    part = jnp.dot((hf * gain_mine).astype(bf16), router_mine, preferred_element_type=f32)
    square = jnp.sum(hf * hf, axis=1, keepdims=True)
    part = jnp.concatenate([part, jnp.broadcast_to(square, (TOK, EXPERTS))], axis=1)
    whole = part
    for k in (1, 2, 3):
        whole = whole + y_shift(part, k)
    logits = whole[:, :EXPERTS] * lax.rsqrt(whole[:, EXPERTS : EXPERTS + 1] / 2048.0 + EPS)
    lifted = jax.nn.sigmoid(logits)
    onehot = jnp.sum(
        (routes[:, :, None] == jnp.arange(EXPERTS, dtype=jnp.int32)[None, None, :]).astype(f32),
        axis=1,
    )
    lifted = lifted * onehot
    gates = lifted / jnp.sum(lifted, axis=1, keepdims=True)
    gates = lax.dynamic_index_in_dim(gates.reshape(TOK, WIDE, 2), i, 2, keepdims=False).T

    moe = jnp.zeros((TOK, 512), f32)
    contract = (((0, 1), (0, 1)), ((), ()))
    mixing = jnp.where(chosen, gates[:, None, :], 0.0)
    mixing_hi = lax.reduce_precision(mixing, 8, 7)
    mixing_lo = (mixing - mixing_hi).astype(bf16)
    for matrix in (mixing_hi.astype(bf16), mixing_lo):
        moe = moe + lax.dot_general(matrix, back, contract, preferred_element_type=f32)
    moe = moe.astype(bf16)
    moe_par = x_swap(moe)
    layer, part = pl.pallas_call(
        embed_kernel,
        out_shape=(
            jax.ShapeDtypeStruct((TOK, 512), bf16),
            jax.ShapeDtypeStruct((TOK + 8, 128), f32),
        ),
        in_specs=[smem()] + [vmem()] * 5,
        out_specs=(vmem(), vmem()),
        compiler_params=params(),
        name="embed",
    )(here, hidden, moe, moe_par, norm_gains, w_proj)
    parts = [part] + [y_shift(part, k) for k in (1, 2, 3)]

    vectors = pl.pallas_call(
        vector_kernel,
        out_shape=jax.ShapeDtypeStruct((16, TOK, 128), bf16),
        in_specs=[vmem()] * 4,
        out_specs=vmem(),
        compiler_params=params(),
        name="vectors",
    )(*parts)
    vectors, layer = lax.optimization_barrier((vectors, layer))
    layers = [layer] + [y_shift(layer, k) for k in (1, 2, 3)]
    own = lax.all_to_all(vectors, ("z", "xl"), 0, 0, tiled=True).reshape(16 * TOK, 128)
    segment = doc_segment[0]
    requests = doc_request[0]
    docs = jnp.arange(16, dtype=jnp.int32)
    first = jnp.sum((segment[None, :] < docs[:, None]).astype(jnp.int32), axis=1)
    size = jnp.sum((segment[None, :] == docs[:, None]).astype(jnp.int32), axis=1)
    starts = jnp.cumsum(request_lengths, axis=1) - request_lengths
    starts = (starts + TOK * (jnp.arange(WIDE, dtype=jnp.int32) // 2)[:, None]).reshape(-1)
    match = requests[:, None] == jnp.arange(96, dtype=jnp.int32)[None, :]
    q_first = jnp.sum(jnp.where(match, starts[None, :], 0), axis=1)
    q_size = jnp.sum(jnp.where(match, request_lengths.reshape(-1)[None, :], 0), axis=1)
    away = lax.rem(requests // 3, 2) ^ core
    info = jnp.stack([first, size, q_first, q_size, away])
    own, info, *layers = lax.optimization_barrier((own, info, *layers))
    other = lax.ppermute(own, "core", [(0, 1), (1, 0)])
    layer_out = pl.pallas_call(
        assemble_kernel,
        out_shape=jax.ShapeDtypeStruct((TOK, 2048), bf16),
        in_specs=[smem()] + [vmem()] * 4,
        out_specs=vmem(),
        compiler_params=params(),
        name="assemble",
    )(here, *layers)
    doc_scores = pl.pallas_call(
        score_kernel,
        out_shape=jax.ShapeDtypeStruct((1, 16), f32),
        in_specs=[smem(), vmem()] + [anywhere()] * 2,
        out_specs=vmem(),
        scratch_shapes=[pltpu.VMEM((16, 128, 128), bf16), pltpu.SemaphoreType.DMA((16,))],
        compiler_params=params(),
        name="score",
    )(info, doc_vectors, own, other)
    return (layer_out, doc_scores)


def solution(mesh):
    split = Mesh(mesh.devices.reshape(8, 2, 2, 2, 4), ("z", "xl", "core", "xh", "y"))
    placed = (
        P(W, None),
        P(),
        P(None, None, N),
        P(None, N),
        P(N, None),
        P(),
        P(),
        P(W, None),
        P(W, None, N),
        P(W, None, N),
        P(W, N, None),
        P(),
        P(W + N, None),
        P(W + N, None),
        P(W + N, None),
    )
    return jax.shard_map(
        body,
        mesh=split,
        in_specs=placed,
        out_specs=(P(W, None), P(W + N, None)),
        check_vma=False,
    )
```

```python
import math

import jax
import jax.numpy as jnp
from jax import lax
from jax.experimental import pallas as pl
from jax.experimental.pallas import tpu as pltpu
from jax.sharding import Mesh, PartitionSpec as P

HD = 128
TOPK = 8
TOK = 128
CAP = 20
EXPERTS = 64
WIDE = 32
HALF = WIDE * CAP // 2
EPS = 1e-06
THETA = 50000.0
NEG = -1e30
W = ("z", "xl", "core")
N = ("xh", "y")
f32 = jnp.float32
bf16 = jnp.bfloat16


def y_shift(x, k):
    return lax.ppermute(x, "y", [(s, (s + k) % 4) for s in range(4)])


def x_swap(x):
    return lax.ppermute(x, "xh", [(0, 1), (1, 0)])


def attention_kernel(
    i_ref,
    j_ref,
    wide_ref,
    lengths_ref,
    qk_ref,
    gain_ref,
    x_hbm,
    w_hbm,
    out_hbm,
    gate_hbm,
    out0,
    out1,
    out2,
    out3,
    sent_ref,
    x_ref,
    w_ref,
    out_w_ref,
    sems,
):
    copies = [pltpu.make_async_copy(x_hbm, x_ref, sems.at[0])]
    copies += [
        pltpu.make_async_copy(w_hbm.at[part], w_ref.at[part], sems.at[1 + part]) for part in range(3)
    ]
    copies += [pltpu.make_async_copy(out_hbm, out_w_ref, sems.at[4])]
    copies += [pltpu.make_async_copy(gate_hbm.at[1 - i_ref[0]], sent_ref, sems.at[5])]
    for copy in copies:
        copy.start()
    wide = wide_ref[0]
    one = lengths_ref[0, wide]
    two = one + lengths_ref[1, wide]

    def member_of(places):
        return (places >= one).astype(jnp.int32) + (places >= two).astype(jnp.int32)

    down_places = lax.broadcasted_iota(jnp.int32, (TOK, HD), 0)
    across_places = lax.broadcasted_iota(jnp.int32, (TOK, HD), 1)
    member = member_of(down_places)
    same = member == member_of(across_places)
    start = jnp.where(member == 0, 0, jnp.where(member == 1, one, two))
    half = lax.rem(across_places, HD // 2).astype(f32)
    freq = jnp.exp(half * (-math.log(THETA) / (HD // 2)))
    angle = (down_places - start).astype(f32) * freq
    cosine = jnp.cos(angle)
    sine = jnp.sin(angle)
    sine = jnp.where(across_places < HD // 2, -sine, sine)

    copies[0].wait()
    x = x_ref[...].astype(f32)
    scale = lax.rsqrt(jnp.mean(x * x, axis=1, keepdims=True) + EPS)
    normed = (x * scale * gain_ref[0:1, :]).astype(bf16)
    parts = []
    for part in range(3):
        copies[1 + part].wait()
        parts.append(jnp.dot(normed, w_ref[part], preferred_element_type=f32))
    query, keys, values = parts

    def turned(v, gain):
        v = v * lax.rsqrt(jnp.mean(v * v, axis=1, keepdims=True) + EPS) * gain
        return (v * cosine + pltpu.roll(v, HD // 2, 1) * sine).astype(bf16)

    mixed = []
    for head in range(2):
        at = slice(head * HD, (head + 1) * HD)
        q = turned(query[:, at], qk_ref[0:1, at])
        k = turned(keys[:, at], qk_ref[1:2, at])
        scores = lax.dot_general(q, k, (((1,), (1,)), ((), ())), preferred_element_type=f32)
        scores = jnp.where(same, scores * HD ** (-0.5), NEG)
        weights = jnp.exp(scores - jnp.max(scores, axis=1, keepdims=True))
        probs = (weights / jnp.sum(weights, axis=1, keepdims=True)).astype(bf16)
        mixed.append(
            jnp.dot(probs, values[:, at].astype(bf16), preferred_element_type=f32).astype(bf16)
        )
    mixed = jnp.concatenate(mixed, axis=1)
    copies[4].wait()
    j = j_ref[0]
    for k, out_ref in enumerate((out0, out1, out2, out3)):
        part = lax.rem(j + k, 4)
        columns = pl.ds(pl.multiple_of(part * 512, 512), 512)
        out_ref[...] = jnp.dot(mixed, out_w_ref[:, columns], preferred_element_type=f32).astype(bf16)
    copies[5].wait()


def choose_kernel(here_ref, routes_ref, out_ref):
    expert = 2 * lax.broadcasted_iota(jnp.int32, (WIDE, TOK), 0) + here_ref[0]
    hit = jnp.zeros((WIDE, TOK), f32)
    for k in range(TOPK):
        hit = hit + (routes_ref[k : k + 1, :] == expert).astype(f32)
    sooner = lax.broadcasted_iota(jnp.int32, (TOK, TOK), 0)
    earlier = (sooner < lax.broadcasted_iota(jnp.int32, (TOK, TOK), 1)).astype(f32).astype(bf16)
    before = jnp.dot(hit.astype(bf16), earlier, preferred_element_type=f32)
    place = jnp.where(hit > 0, before, -1.0).astype(bf16)
    owner = CAP * lax.broadcasted_iota(jnp.int32, (WIDE * CAP, WIDE), 1)
    slot = lax.broadcasted_iota(jnp.int32, (WIDE * CAP, WIDE), 0) - owner
    inside = (slot >= 0) & (slot < CAP)
    spread = jnp.dot(inside.astype(f32).astype(bf16), place, preferred_element_type=f32)
    slot = jnp.sum(jnp.where(inside, slot, 0).astype(f32), axis=1, keepdims=True)
    out_ref[...] = (spread == slot).astype(f32).astype(bf16)


def packed(rows):
    return jnp.concatenate([rows[:, 0:256], rows[:, 256:512]], axis=0).astype(bf16)


def dispatch_kernel(here_ref, x_ref, own_ref, par_ref, choose_ref, hidden_ref, rows_ref):
    j = here_ref[1]
    mine = x_ref[:, pl.ds(pl.multiple_of(j * 512, 512), 512)].astype(f32)
    hidden = (mine + (own_ref[...].astype(f32) + par_ref[...].astype(f32))).astype(bf16)
    hidden_ref[...] = hidden
    rows = jnp.dot(choose_ref[...], hidden, preferred_element_type=f32)
    for s in range(WIDE):
        rows_ref[s] = packed(rows[s * CAP : (s + 1) * CAP])


def unpack_kernel(in_ref, top_ref, bottom_ref, scratch):
    for half, out_ref in enumerate((top_ref, bottom_ref)):
        for s in range(WIDE // 2):
            rows = in_ref[half * (WIDE // 2) + s].astype(f32)
            at = slice(s * CAP, (s + 1) * CAP)
            scratch[at, 0:256] = rows[0:CAP]
            scratch[at, 256:512] = rows[CAP:]
        out_ref[...] = scratch[...].astype(bf16)


def gate_up_kernel(here_ref, *refs):
    halves = refs[0:4], refs[4:8]
    gain_hbm, gate_hbm, up_hbm, gate_par, up_par, out_ref, gain_ref, w_ref, sems = refs[8:]
    i, j = here_ref[0], here_ref[1]
    sources = (gate_hbm.at[i], up_hbm.at[i], gate_par, up_par)
    copies = [
        pltpu.make_async_copy(source, w_ref.at[n], sems.at[n]) for n, source in enumerate(sources)
    ]
    copies.append(pltpu.make_async_copy(gain_hbm, gain_ref, sems.at[4]))
    for copy in copies:
        copy.start()
    scales = []
    for xs in halves:
        total = jnp.zeros((HALF, 1), f32)
        for x in xs:
            v = x[...].astype(f32)
            total = total + jnp.sum(v * v, axis=1, keepdims=True)
        scales.append(lax.rsqrt(total / 2048.0 + EPS))
    for copy in copies:
        copy.wait()
    for half, (xs, scale) in enumerate(zip(halves, scales)):
        own = jnp.zeros((HALF, 256), f32)
        par = jnp.zeros((HALF, 256), f32)
        for k, x in enumerate(xs):
            part = lax.rem(j + 4 + (0, -1, 1, 2)[k], 4)
            rows = pl.ds(pl.multiple_of(part * 512, 512), 512)
            normed = (x[...].astype(f32) * scale * gain_ref[1:2, rows]).astype(bf16)
            w_own = jnp.concatenate([w_ref[0, rows, :], w_ref[1, rows, :]], axis=1)
            w_par = jnp.concatenate([w_ref[2, rows, :], w_ref[3, rows, :]], axis=1)
            own = own + jnp.dot(normed, w_own, preferred_element_type=f32)
            par = par + jnp.dot(normed, w_par, preferred_element_type=f32)
        for at, both in ((0, own), (128, par)):
            gate, up = both[:, :128], both[:, 128:]
            out_ref[half * HALF : (half + 1) * HALF, at : at + 128] = (
                gate / (1.0 + jnp.exp(-gate)) * up
            ).astype(bf16)


def down_kernel(here_ref, a0, a1, a2, a3, w0, w1, w2, w3, par_ref, out_ref, w_ref, sems):
    i = here_ref[0]
    copies = []
    for k, w in enumerate((w0, w1, w2, w3)):
        copies.append(
            (
                pltpu.make_async_copy(w.at[i], w_ref.at[k, 0:128], sems.at[0, k]),
                pltpu.make_async_copy(par_ref.at[k], w_ref.at[k, 128:256], sems.at[1, k]),
            )
        )
    for pair in copies:
        for copy in pair:
            copy.start()
    total = jnp.zeros((a0.shape[0], 512), f32)
    for k, a in enumerate((a0, a1, a2, a3)):
        for copy in copies[k]:
            copy.wait()
        total = total + jnp.dot(a[...], w_ref[k], preferred_element_type=f32)
    for s in range(WIDE):
        out_ref[s] = packed(total[s * CAP : (s + 1) * CAP])


def embed_kernel(here_ref, hidden_ref, moe_ref, par_ref, gain_ref, w_ref, layer_ref, part_ref):
    mine = pl.ds(pl.multiple_of(here_ref[1] * 512, 512), 512)
    moe = moe_ref[...].astype(f32) + par_ref[...].astype(f32)
    layer = hidden_ref[...].astype(f32) + jnp.concatenate([moe[0:TOK], moe[TOK:]], axis=1)
    layer = layer.astype(bf16)
    layer_ref[...] = layer
    layer = layer.astype(f32)
    scaled = (layer * gain_ref[2:3, mine]).astype(bf16)
    part_ref[0:TOK, :] = jnp.dot(scaled, w_ref[mine, :], preferred_element_type=f32)
    square = jnp.broadcast_to(jnp.sum(layer * layer, axis=1, keepdims=True), (TOK, TOK))
    part_ref[TOK:, :] = jnp.transpose(square)[0:8]


def vector_kernel(p0, p1, p2, p3, out_ref):
    whole = p0[...] + p1[...] + p2[...] + p3[...]
    square = jnp.transpose(jnp.broadcast_to(whole[TOK : TOK + 1], (TOK, TOK)))
    embedded = whole[0:TOK] * lax.rsqrt(square / 2048.0 + EPS)
    norm = jnp.sum(embedded * embedded, axis=1, keepdims=True)
    vectors = (embedded * lax.rsqrt(norm + EPS)).astype(bf16)
    for copy in range(16):
        out_ref[copy] = vectors


def assemble_kernel(here_ref, p0, p1, p2, p3, out_ref):
    j = here_ref[1]
    for k, piece in enumerate((p0, p1, p2, p3)):
        part = lax.rem(j - k + 4, 4)
        out_ref[:, pl.ds(pl.multiple_of(part * 512, 512), 512)] = piece[...]


def score_kernel(info_ref, doc_ref, own_ref, other_ref, out_ref, query_ref, sems):
    def spot(d):
        return pl.multiple_of(jnp.minimum((info_ref[2, d] // 16) * 16, 2048 - 128), 16)

    def copy_of(ref, d):
        return pltpu.make_async_copy(ref.at[pl.ds(spot(d), 128), :], query_ref.at[d], sems.at[d])

    for d in range(16):

        @pl.when(info_ref[4, d] == 0)
        def _():
            copy_of(own_ref, d).start()

        @pl.when(info_ref[4, d] != 0)
        def _():
            copy_of(other_ref, d).start()

    lane = lax.broadcasted_iota(jnp.int32, (1, 16), 1)
    scores = jnp.zeros((1, 16), f32)
    rows = lax.broadcasted_iota(jnp.int32, (144, 128), 0)
    columns = lax.broadcasted_iota(jnp.int32, (1, 128), 1)
    for d in range(16):
        copy_of(own_ref, d).wait()
    for d in range(16):
        first, size = info_ref[0, d], info_ref[1, d]
        q_first, q_size = info_ref[2, d], info_ref[3, d]
        at = pl.multiple_of(jnp.minimum((first // 16) * 16, 1024 - 144), 16)
        sims = lax.dot_general(
            doc_ref[pl.ds(at, 144), :],
            query_ref[d],
            (((1,), (1,)), ((), ())),
            preferred_element_type=f32,
        )
        keep = (rows >= first - at) & (rows < first - at + size)
        best = jnp.max(jnp.where(keep, sims, NEG), axis=0, keepdims=True)
        q_start = q_first - spot(d)
        used = (columns >= q_start) & (columns < q_start + q_size)
        value = jnp.sum(jnp.where(used, best, 0.0), axis=1, keepdims=True) / q_size.astype(f32)
        scores = jnp.where(lane == d, value, scores)
    out_ref[...] = scores


def vmem():
    return pl.BlockSpec(memory_space=pltpu.VMEM)


def smem():
    return pl.BlockSpec(memory_space=pltpu.SMEM)


def hbm():
    return pl.BlockSpec(memory_space=pltpu.HBM)


def anywhere():
    return pl.BlockSpec(memory_space=pl.ANY)


def params():
    return pltpu.CompilerParams(vmem_limit_bytes=16 << 20)


def body(
    tokens,
    request_lengths,
    w_qkv,
    qk_gain,
    w_out,
    norm_gains,
    w_router,
    routes,
    w_gate,
    w_up,
    w_down,
    w_proj,
    doc_vectors,
    doc_segment,
    doc_request,
):
    i = lax.axis_index("xh")
    j = lax.axis_index("y")
    core = lax.axis_index("core")
    wide = lax.axis_index(W)
    here = jnp.stack([i, j, wide, core])

    def pick(array, which):
        return lax.dynamic_index_in_dim(array, which, 0, keepdims=False)

    def cut(array, part, axis):
        return lax.dynamic_slice_in_dim(array, lax.rem(part, 4) * 512, 512, axis)

    *attn, gate_sent = pl.pallas_call(
        attention_kernel,
        out_shape=(
            *(jax.ShapeDtypeStruct((TOK, 512), bf16),) * 4,
            jax.ShapeDtypeStruct((2048, 128), bf16),
        ),
        in_specs=[smem()] * 4 + [vmem()] * 2 + [hbm()] * 4,
        out_specs=(vmem(),) * 5,
        scratch_shapes=[
            pltpu.VMEM((TOK, 2048), bf16),
            pltpu.VMEM((3, 2048, 256), bf16),
            pltpu.VMEM((256, 2048), bf16),
            pltpu.SemaphoreType.DMA((6,)),
        ],
        compiler_params=pltpu.CompilerParams(vmem_limit_bytes=60 << 20),
        name="attention",
    )(
        i.reshape(1),
        j.reshape(1),
        wide.reshape(1),
        request_lengths.T,
        qk_gain,
        norm_gains,
        tokens,
        w_qkv.transpose(1, 0, 2),
        w_out,
        w_gate,
    )
    gate_par = x_swap(gate_sent)
    attn_parts = [y_shift(attn[k], k) for k in (1, 2, 3)]

    downs = [cut(w_down, j, 2)] + [y_shift(cut(w_down, j + k, 2), k) for k in (1, 2, 3)]
    down_par = x_swap(jnp.stack([pick(d, 1 - i) for d in downs]))

    experts_here = 2 * jnp.arange(WIDE, dtype=jnp.int32) + i
    hit = jnp.sum((routes.T[None, :, :] == experts_here[:, None, None]).astype(f32), axis=1)
    places = jnp.arange(TOK, dtype=jnp.int32)
    earlier = (places[:, None] < places[None, :]).astype(bf16)
    before = jnp.dot(hit.astype(bf16), earlier, preferred_element_type=f32)
    slot = jnp.arange(CAP, dtype=jnp.int32).astype(f32)
    chosen = (before[:, None, :] == slot[None, :, None]) & (hit[:, None, :] > 0)
    choose = pl.pallas_call(
        choose_kernel,
        out_shape=jax.ShapeDtypeStruct((WIDE * CAP, TOK), bf16),
        in_specs=[smem(), vmem()],
        out_specs=vmem(),
        compiler_params=params(),
        name="choose",
    )(here, routes.T)

    attn = (attn[0].astype(f32) + sum(p.astype(f32) for p in attn_parts)).astype(bf16)
    attn, choose = lax.optimization_barrier((attn, choose))
    attn_par = x_swap(attn)
    attn_par, gate_par = lax.optimization_barrier((attn_par, gate_par))
    hidden, rows = pl.pallas_call(
        dispatch_kernel,
        out_shape=(
            jax.ShapeDtypeStruct((TOK, 512), bf16),
            jax.ShapeDtypeStruct((WIDE, 2 * CAP, 256), bf16),
        ),
        in_specs=[smem()] + [vmem()] * 4,
        out_specs=(vmem(), vmem()),
        compiler_params=params(),
        name="dispatch",
    )(here, tokens, attn, attn_par, choose)

    arrived = lax.all_to_all(rows, W, 0, 0, tiled=True)
    top, bottom = pl.pallas_call(
        unpack_kernel,
        out_shape=(jax.ShapeDtypeStruct((HALF, 512), bf16),) * 2,
        in_specs=[vmem()],
        out_specs=(vmem(), vmem()),
        scratch_shapes=[pltpu.VMEM((HALF, 512), f32)],
        compiler_params=params(),
        name="unpack",
    )(arrived)
    top, bottom, up_sent = lax.optimization_barrier((top, bottom, pick(w_up, 1 - i)))
    up_par = x_swap(up_sent)
    top_back, bottom_ahead = y_shift(top, 1), y_shift(bottom, 3)
    bottom_back, top_ahead = y_shift(bottom, 1), y_shift(top, 3)
    top_far, bottom_far = y_shift(top_back, 1), y_shift(bottom_ahead, 3)
    act = pl.pallas_call(
        gate_up_kernel,
        out_shape=jax.ShapeDtypeStruct((2 * HALF, 256), bf16),
        in_specs=[smem()] + [vmem()] * 8 + [anywhere()] * 5,
        out_specs=vmem(),
        scratch_shapes=[
            pltpu.VMEM((3, 2048), f32),
            pltpu.VMEM((4, 2048, 128), bf16),
            pltpu.SemaphoreType.DMA((5,)),
        ],
        compiler_params=params(),
        name="gate_up",
    )(
        here,
        *(top, top_back, top_ahead, top_far),
        *(bottom, bottom_back, bottom_ahead, bottom_far),
        norm_gains,
        w_gate,
        w_up,
        gate_par,
        up_par,
    )
    out = pl.pallas_call(
        down_kernel,
        out_shape=jax.ShapeDtypeStruct((WIDE, 2 * CAP, 256), bf16),
        in_specs=[smem()] + [vmem()] * 4 + [anywhere()] * 5,
        out_specs=vmem(),
        scratch_shapes=[pltpu.VMEM((4, 256, 512), bf16), pltpu.SemaphoreType.DMA((2, 4))],
        compiler_params=params(),
        name="down",
    )(here, act, *(y_shift(act, k) for k in (1, 2, 3)), *downs, down_par)
    back = lax.all_to_all(out, W, 0, 0, tiled=True)

    hf = hidden.astype(f32)
    gain_mine = lax.dynamic_slice_in_dim(norm_gains[1], j * 512, 512, 0)
    router_mine = lax.dynamic_slice_in_dim(w_router, j * 512, 512, 0)
    part = jnp.dot((hf * gain_mine).astype(bf16), router_mine, preferred_element_type=f32)
    square = jnp.sum(hf * hf, axis=1, keepdims=True)
    part = jnp.concatenate([part, jnp.broadcast_to(square, (TOK, EXPERTS))], axis=1)
    whole = part
    for k in (1, 2, 3):
        whole = whole + y_shift(part, k)
    logits = whole[:, :EXPERTS] * lax.rsqrt(whole[:, EXPERTS : EXPERTS + 1] / 2048.0 + EPS)
    lifted = jax.nn.sigmoid(logits)
    onehot = jnp.sum(
        (routes[:, :, None] == jnp.arange(EXPERTS, dtype=jnp.int32)[None, None, :]).astype(f32),
        axis=1,
    )
    lifted = lifted * onehot
    gates = lifted / jnp.sum(lifted, axis=1, keepdims=True)
    gates = lax.dynamic_index_in_dim(gates.reshape(TOK, WIDE, 2), i, 2, keepdims=False).T

    moe = jnp.zeros((2 * TOK, 256), f32)
    contract = (((0, 1), (0, 1)), ((), ()))
    mixing = jnp.where(chosen, gates[:, None, :], 0.0)
    blank = jnp.zeros_like(mixing)
    mixing = jnp.concatenate(
        [
            jnp.concatenate([mixing, blank], axis=1),
            jnp.concatenate([blank, mixing], axis=1),
        ],
        axis=2,
    )
    mixing_hi = lax.reduce_precision(mixing, 8, 7)
    mixing_lo = (mixing - mixing_hi).astype(bf16)
    for matrix in lax.optimization_barrier((mixing_hi.astype(bf16), mixing_lo)):
        moe = moe + lax.dot_general(matrix, back, contract, preferred_element_type=f32)
    moe = moe.astype(bf16)
    moe_par = x_swap(moe)
    layer, part = pl.pallas_call(
        embed_kernel,
        out_shape=(
            jax.ShapeDtypeStruct((TOK, 512), bf16),
            jax.ShapeDtypeStruct((TOK + 8, 128), f32),
        ),
        in_specs=[smem()] + [vmem()] * 5,
        out_specs=(vmem(), vmem()),
        compiler_params=params(),
        name="embed",
    )(here, hidden, moe, moe_par, norm_gains, w_proj)
    parts = [part] + [y_shift(part, k) for k in (1, 2, 3)]

    vectors = pl.pallas_call(
        vector_kernel,
        out_shape=jax.ShapeDtypeStruct((16, TOK, 128), bf16),
        in_specs=[vmem()] * 4,
        out_specs=vmem(),
        compiler_params=params(),
        name="vectors",
    )(*parts)
    vectors, layer = lax.optimization_barrier((vectors, layer))
    layers = [layer] + [y_shift(layer, k) for k in (1, 2, 3)]
    own = lax.all_to_all(vectors, ("z", "xl"), 0, 0, tiled=True).reshape(16 * TOK, 128)
    segment = doc_segment[0]
    requests = doc_request[0]
    docs = jnp.arange(16, dtype=jnp.int32)
    first = jnp.sum((segment[None, :] < docs[:, None]).astype(jnp.int32), axis=1)
    size = jnp.sum((segment[None, :] == docs[:, None]).astype(jnp.int32), axis=1)
    starts = jnp.cumsum(request_lengths, axis=1) - request_lengths
    starts = (starts + TOK * (jnp.arange(WIDE, dtype=jnp.int32) // 2)[:, None]).reshape(-1)
    match = requests[:, None] == jnp.arange(96, dtype=jnp.int32)[None, :]
    q_first = jnp.sum(jnp.where(match, starts[None, :], 0), axis=1)
    q_size = jnp.sum(jnp.where(match, request_lengths.reshape(-1)[None, :], 0), axis=1)
    away = lax.rem(requests // 3, 2) ^ core
    info = jnp.stack([first, size, q_first, q_size, away])
    own, info, *layers = lax.optimization_barrier((own, info, *layers))
    other = lax.ppermute(own, "core", [(0, 1), (1, 0)])
    layer_out = pl.pallas_call(
        assemble_kernel,
        out_shape=jax.ShapeDtypeStruct((TOK, 2048), bf16),
        in_specs=[smem()] + [vmem()] * 4,
        out_specs=vmem(),
        compiler_params=params(),
        name="assemble",
    )(here, *layers)
    doc_scores = pl.pallas_call(
        score_kernel,
        out_shape=jax.ShapeDtypeStruct((1, 16), f32),
        in_specs=[smem(), vmem()] + [anywhere()] * 2,
        out_specs=vmem(),
        scratch_shapes=[pltpu.VMEM((16, 128, 128), bf16), pltpu.SemaphoreType.DMA((16,))],
        compiler_params=params(),
        name="score",
    )(info, doc_vectors, own, other)
    return (layer_out, doc_scores)


def solution(mesh):
    split = Mesh(mesh.devices.reshape(8, 2, 2, 2, 4), ("z", "xl", "core", "xh", "y"))
    placed = (
        P(W, None),
        P(),
        P(None, None, N),
        P(None, N),
        P(N, None),
        P(),
        P(),
        P(W, None),
        P(W, None, N),
        P(W, None, N),
        P(W, N, None),
        P(),
        P(W + N, None),
        P(W + N, None),
        P(W + N, None),
    )
    return jax.shard_map(
        body,
        mesh=split,
        in_specs=placed,
        out_specs=(P(W, None), P(W + N, None)),
        check_vma=False,
    )
```

```python
import math

import jax
import jax.numpy as jnp
from jax import lax
from jax.experimental import pallas as pl
from jax.experimental.pallas import tpu as pltpu
from jax.sharding import Mesh, PartitionSpec as P

HD = 128
TOPK = 8
TOK = 128
CAP = 20
EXPERTS = 64
WIDE = 32
HALF = WIDE * CAP // 2
EPS = 1e-06
THETA = 50000.0
NEG = -1e30
W = ("z", "xl", "core")
N = ("xh", "y")
f32 = jnp.float32
bf16 = jnp.bfloat16


def y_shift(x, k):
    return lax.ppermute(x, "y", [(s, (s + k) % 4) for s in range(4)])


def x_swap(x):
    return lax.ppermute(x, "xh", [(0, 1), (1, 0)])


def attention_kernel(
    i_ref,
    j_ref,
    wide_ref,
    lengths_ref,
    qk_ref,
    gain_ref,
    x_hbm,
    w_hbm,
    out_hbm,
    gate_hbm,
    out0,
    out1,
    out2,
    out3,
    sent_ref,
    x_ref,
    w_ref,
    out_w_ref,
    sems,
):
    copies = [pltpu.make_async_copy(x_hbm, x_ref, sems.at[0])]
    copies += [
        pltpu.make_async_copy(w_hbm.at[part], w_ref.at[part], sems.at[1 + part]) for part in range(3)
    ]
    copies += [pltpu.make_async_copy(out_hbm, out_w_ref, sems.at[4])]
    copies += [pltpu.make_async_copy(gate_hbm.at[1 - i_ref[0]], sent_ref, sems.at[5])]
    for copy in copies:
        copy.start()
    wide = wide_ref[0]
    one = lengths_ref[0, wide]
    two = one + lengths_ref[1, wide]

    def member_of(places):
        return (places >= one).astype(jnp.int32) + (places >= two).astype(jnp.int32)

    down_places = lax.broadcasted_iota(jnp.int32, (TOK, HD), 0)
    across_places = lax.broadcasted_iota(jnp.int32, (TOK, HD), 1)
    member = member_of(down_places)
    same = member == member_of(across_places)
    start = jnp.where(member == 0, 0, jnp.where(member == 1, one, two))
    half = lax.rem(across_places, HD // 2).astype(f32)
    freq = jnp.exp(half * (-math.log(THETA) / (HD // 2)))
    angle = (down_places - start).astype(f32) * freq
    cosine = jnp.cos(angle)
    sine = jnp.sin(angle)
    sine = jnp.where(across_places < HD // 2, -sine, sine)

    copies[0].wait()
    x = x_ref[...].astype(f32)
    scale = lax.rsqrt(jnp.mean(x * x, axis=1, keepdims=True) + EPS)
    normed = (x * scale * gain_ref[0:1, :]).astype(bf16)
    parts = []
    for part in range(3):
        copies[1 + part].wait()
        parts.append(jnp.dot(normed, w_ref[part], preferred_element_type=f32))
    query, keys, values = parts

    def turned(v, gain):
        v = v * lax.rsqrt(jnp.mean(v * v, axis=1, keepdims=True) + EPS) * gain
        return (v * cosine + pltpu.roll(v, HD // 2, 1) * sine).astype(bf16)

    mixed = []
    for head in range(2):
        at = slice(head * HD, (head + 1) * HD)
        q = turned(query[:, at], qk_ref[0:1, at])
        k = turned(keys[:, at], qk_ref[1:2, at])
        scores = lax.dot_general(q, k, (((1,), (1,)), ((), ())), preferred_element_type=f32)
        scores = jnp.where(same, scores * HD ** (-0.5), NEG)
        weights = jnp.exp(scores - jnp.max(scores, axis=1, keepdims=True))
        probs = (weights / jnp.sum(weights, axis=1, keepdims=True)).astype(bf16)
        mixed.append(
            jnp.dot(probs, values[:, at].astype(bf16), preferred_element_type=f32).astype(bf16)
        )
    mixed = jnp.concatenate(mixed, axis=1)
    copies[4].wait()
    j = j_ref[0]
    for k, out_ref in enumerate((out0, out1, out2, out3)):
        part = lax.rem(j + k, 4)
        columns = pl.ds(pl.multiple_of(part * 512, 512), 512)
        out_ref[...] = jnp.dot(mixed, out_w_ref[:, columns], preferred_element_type=f32).astype(bf16)
    copies[5].wait()


def choose_kernel(here_ref, routes_ref, out_ref):
    expert = 2 * lax.broadcasted_iota(jnp.int32, (WIDE, TOK), 0) + here_ref[0]
    hit = jnp.zeros((WIDE, TOK), f32)
    for k in range(TOPK):
        hit = hit + (routes_ref[k : k + 1, :] == expert).astype(f32)
    sooner = lax.broadcasted_iota(jnp.int32, (TOK, TOK), 0)
    earlier = (sooner < lax.broadcasted_iota(jnp.int32, (TOK, TOK), 1)).astype(f32).astype(bf16)
    before = jnp.dot(hit.astype(bf16), earlier, preferred_element_type=f32)
    place = jnp.where(hit > 0, before, -1.0).astype(bf16)
    owner = CAP * lax.broadcasted_iota(jnp.int32, (WIDE * CAP, WIDE), 1)
    slot = lax.broadcasted_iota(jnp.int32, (WIDE * CAP, WIDE), 0) - owner
    inside = (slot >= 0) & (slot < CAP)
    spread = jnp.dot(inside.astype(f32).astype(bf16), place, preferred_element_type=f32)
    slot = jnp.sum(jnp.where(inside, slot, 0).astype(f32), axis=1, keepdims=True)
    out_ref[...] = (spread == slot).astype(f32).astype(bf16)


def packed(rows):
    return jnp.concatenate([rows[:, 0:256], rows[:, 256:512]], axis=0).astype(bf16)


def dispatch_kernel(here_ref, x_ref, own_ref, par_ref, choose_ref, hidden_ref, rows_ref):
    j = here_ref[1]
    mine = x_ref[:, pl.ds(pl.multiple_of(j * 512, 512), 512)].astype(f32)
    hidden = (mine + (own_ref[...].astype(f32) + par_ref[...].astype(f32))).astype(bf16)
    hidden_ref[...] = hidden
    rows = jnp.dot(choose_ref[...], hidden, preferred_element_type=f32)
    for s in range(WIDE):
        rows_ref[s] = packed(rows[s * CAP : (s + 1) * CAP])


def unpack_kernel(in_ref, top_ref, bottom_ref, scratch):
    for half, out_ref in enumerate((top_ref, bottom_ref)):
        for s in range(WIDE // 2):
            rows = in_ref[half * (WIDE // 2) + s].astype(f32)
            at = slice(s * CAP, (s + 1) * CAP)
            scratch[at, 0:256] = rows[0:CAP]
            scratch[at, 256:512] = rows[CAP:]
        out_ref[...] = scratch[...].astype(bf16)


def gate_up_kernel(here_ref, *refs):
    halves = refs[0:4], refs[4:8]
    gain_hbm, gate_hbm, up_hbm, gate_par, up_par, out_ref, gain_ref, w_ref, sems = refs[8:]
    i, j = here_ref[0], here_ref[1]
    sources = (gate_hbm.at[i], up_hbm.at[i], gate_par, up_par)
    copies = [
        pltpu.make_async_copy(source, w_ref.at[n], sems.at[n]) for n, source in enumerate(sources)
    ]
    copies.append(pltpu.make_async_copy(gain_hbm, gain_ref, sems.at[4]))
    for copy in copies:
        copy.start()
    scales = []
    for xs in halves:
        total = jnp.zeros((HALF, 1), f32)
        for x in xs:
            v = x[...].astype(f32)
            total = total + jnp.sum(v * v, axis=1, keepdims=True)
        scales.append(lax.rsqrt(total / 2048.0 + EPS))
    for copy in copies:
        copy.wait()
    for half, (xs, scale) in enumerate(zip(halves, scales)):
        own = jnp.zeros((HALF, 256), f32)
        par = jnp.zeros((HALF, 256), f32)
        for k, x in enumerate(xs):
            part = lax.rem(j + 4 + (0, -1, 1, 2)[k], 4)
            rows = pl.ds(pl.multiple_of(part * 512, 512), 512)
            normed = (x[...].astype(f32) * scale * gain_ref[1:2, rows]).astype(bf16)
            w_own = jnp.concatenate([w_ref[0, rows, :], w_ref[1, rows, :]], axis=1)
            w_par = jnp.concatenate([w_ref[2, rows, :], w_ref[3, rows, :]], axis=1)
            own = own + jnp.dot(normed, w_own, preferred_element_type=f32)
            par = par + jnp.dot(normed, w_par, preferred_element_type=f32)
        for at, both in ((0, own), (128, par)):
            gate, up = both[:, :128], both[:, 128:]
            out_ref[half * HALF : (half + 1) * HALF, at : at + 128] = (
                gate / (1.0 + jnp.exp(-gate)) * up
            ).astype(bf16)


def down_kernel(here_ref, a0, a1, a2, a3, w0, w1, w2, w3, par_ref, out_ref, w_ref, sems):
    i = here_ref[0]
    copies = []
    for k, w in enumerate((w0, w1, w2, w3)):
        copies.append(
            (
                pltpu.make_async_copy(w.at[i], w_ref.at[k, 0:128], sems.at[0, k]),
                pltpu.make_async_copy(par_ref.at[k], w_ref.at[k, 128:256], sems.at[1, k]),
            )
        )
    for pair in copies:
        for copy in pair:
            copy.start()
    total = jnp.zeros((a0.shape[0], 512), f32)
    for k, a in enumerate((a0, a1, a2, a3)):
        for copy in copies[k]:
            copy.wait()
        total = total + jnp.dot(a[...], w_ref[k], preferred_element_type=f32)
    for s in range(WIDE):
        out_ref[s] = packed(total[s * CAP : (s + 1) * CAP])


def embed_kernel(here_ref, hidden_ref, moe_ref, par_ref, gain_ref, w_ref, layer_ref, part_ref):
    mine = pl.ds(pl.multiple_of(here_ref[1] * 512, 512), 512)
    moe = moe_ref[...].astype(f32) + par_ref[...].astype(f32)
    layer = hidden_ref[...].astype(f32) + jnp.concatenate([moe[0:TOK], moe[TOK:]], axis=1)
    layer = layer.astype(bf16)
    layer_ref[...] = layer
    layer = layer.astype(f32)
    scaled = (layer * gain_ref[2:3, mine]).astype(bf16)
    part = jnp.dot(scaled, w_ref[mine, :], preferred_element_type=f32)
    part_ref[0:TOK, :] = part.astype(bf16)
    square = jnp.broadcast_to(jnp.sum(layer * layer, axis=1, keepdims=True), (TOK, TOK))
    part_ref[TOK:, :] = jnp.transpose(square)[0:16].astype(bf16)


def vector_kernel(p0, p1, p2, p3, out_ref):
    whole = sum(p[...].astype(f32) for p in (p0, p1, p2, p3))
    square = jnp.transpose(jnp.broadcast_to(whole[TOK : TOK + 1], (TOK, TOK)))
    embedded = whole[0:TOK] * lax.rsqrt(square / 2048.0 + EPS)
    norm = jnp.sum(embedded * embedded, axis=1, keepdims=True)
    vectors = (embedded * lax.rsqrt(norm + EPS)).astype(bf16)
    for copy in range(16):
        out_ref[copy] = vectors


def assemble_kernel(here_ref, p0, p1, p2, p3, out_ref):
    j = here_ref[1]
    for k, piece in enumerate((p0, p1, p2, p3)):
        part = lax.rem(j - k + 4, 4)
        out_ref[:, pl.ds(pl.multiple_of(part * 512, 512), 512)] = piece[...]


def score_kernel(info_ref, doc_ref, own_ref, other_ref, out_ref, query_ref, sems):
    def spot(d):
        return pl.multiple_of(jnp.minimum((info_ref[2, d] // 16) * 16, 2048 - 128), 16)

    def copy_of(ref, d):
        return pltpu.make_async_copy(ref.at[pl.ds(spot(d), 128), :], query_ref.at[d], sems.at[d])

    for d in range(16):

        @pl.when(info_ref[4, d] == 0)
        def _():
            copy_of(own_ref, d).start()

        @pl.when(info_ref[4, d] != 0)
        def _():
            copy_of(other_ref, d).start()

    lane = lax.broadcasted_iota(jnp.int32, (1, 16), 1)
    scores = jnp.zeros((1, 16), f32)
    rows = lax.broadcasted_iota(jnp.int32, (144, 128), 0)
    columns = lax.broadcasted_iota(jnp.int32, (1, 128), 1)
    for d in range(16):
        copy_of(own_ref, d).wait()
    for d in range(16):
        first, size = info_ref[0, d], info_ref[1, d]
        q_first, q_size = info_ref[2, d], info_ref[3, d]
        at = pl.multiple_of(jnp.minimum((first // 16) * 16, 1024 - 144), 16)
        sims = lax.dot_general(
            doc_ref[pl.ds(at, 144), :],
            query_ref[d],
            (((1,), (1,)), ((), ())),
            preferred_element_type=f32,
        )
        keep = (rows >= first - at) & (rows < first - at + size)
        best = jnp.max(jnp.where(keep, sims, NEG), axis=0, keepdims=True)
        q_start = q_first - spot(d)
        used = (columns >= q_start) & (columns < q_start + q_size)
        value = jnp.sum(jnp.where(used, best, 0.0), axis=1, keepdims=True) / q_size.astype(f32)
        scores = jnp.where(lane == d, value, scores)
    out_ref[...] = scores


def vmem():
    return pl.BlockSpec(memory_space=pltpu.VMEM)


def smem():
    return pl.BlockSpec(memory_space=pltpu.SMEM)


def hbm():
    return pl.BlockSpec(memory_space=pltpu.HBM)


def anywhere():
    return pl.BlockSpec(memory_space=pl.ANY)


def params():
    return pltpu.CompilerParams(vmem_limit_bytes=16 << 20)


def body(
    tokens,
    request_lengths,
    w_qkv,
    qk_gain,
    w_out,
    norm_gains,
    w_router,
    routes,
    w_gate,
    w_up,
    w_down,
    w_proj,
    doc_vectors,
    doc_segment,
    doc_request,
):
    i = lax.axis_index("xh")
    j = lax.axis_index("y")
    core = lax.axis_index("core")
    wide = lax.axis_index(W)
    here = jnp.stack([i, j, wide, core])

    def pick(array, which):
        return lax.dynamic_index_in_dim(array, which, 0, keepdims=False)

    def cut(array, part, axis):
        return lax.dynamic_slice_in_dim(array, lax.rem(part, 4) * 512, 512, axis)

    *attn, gate_sent = pl.pallas_call(
        attention_kernel,
        out_shape=(
            *(jax.ShapeDtypeStruct((TOK, 512), bf16),) * 4,
            jax.ShapeDtypeStruct((2048, 128), bf16),
        ),
        in_specs=[smem()] * 4 + [vmem()] * 2 + [hbm()] * 4,
        out_specs=(vmem(),) * 5,
        scratch_shapes=[
            pltpu.VMEM((TOK, 2048), bf16),
            pltpu.VMEM((3, 2048, 256), bf16),
            pltpu.VMEM((256, 2048), bf16),
            pltpu.SemaphoreType.DMA((6,)),
        ],
        compiler_params=pltpu.CompilerParams(vmem_limit_bytes=60 << 20),
        name="attention",
    )(
        i.reshape(1),
        j.reshape(1),
        wide.reshape(1),
        request_lengths.T,
        qk_gain,
        norm_gains,
        tokens,
        w_qkv.transpose(1, 0, 2),
        w_out,
        w_gate,
    )
    gate_par = x_swap(gate_sent)
    attn_parts = [y_shift(attn[k], k) for k in (1, 2, 3)]

    downs = [cut(w_down, j, 2)] + [y_shift(cut(w_down, j + k, 2), k) for k in (1, 2, 3)]
    down_par = x_swap(jnp.stack([pick(d, 1 - i) for d in downs]))

    experts_here = 2 * jnp.arange(WIDE, dtype=jnp.int32) + i
    hit = jnp.sum((routes.T[None, :, :] == experts_here[:, None, None]).astype(f32), axis=1)
    places = jnp.arange(TOK, dtype=jnp.int32)
    earlier = (places[:, None] < places[None, :]).astype(bf16)
    before = jnp.dot(hit.astype(bf16), earlier, preferred_element_type=f32)
    slot = jnp.arange(CAP, dtype=jnp.int32).astype(f32)
    chosen = (before[:, None, :] == slot[None, :, None]) & (hit[:, None, :] > 0)
    choose = pl.pallas_call(
        choose_kernel,
        out_shape=jax.ShapeDtypeStruct((WIDE * CAP, TOK), bf16),
        in_specs=[smem(), vmem()],
        out_specs=vmem(),
        compiler_params=params(),
        name="choose",
    )(here, routes.T)

    attn = (attn[0].astype(f32) + sum(p.astype(f32) for p in attn_parts)).astype(bf16)
    attn, choose = lax.optimization_barrier((attn, choose))
    attn_par = x_swap(attn)
    attn_par, gate_par = lax.optimization_barrier((attn_par, gate_par))
    hidden, rows = pl.pallas_call(
        dispatch_kernel,
        out_shape=(
            jax.ShapeDtypeStruct((TOK, 512), bf16),
            jax.ShapeDtypeStruct((WIDE, 2 * CAP, 256), bf16),
        ),
        in_specs=[smem()] + [vmem()] * 4,
        out_specs=(vmem(), vmem()),
        compiler_params=params(),
        name="dispatch",
    )(here, tokens, attn, attn_par, choose)

    arrived = lax.all_to_all(rows, W, 0, 0, tiled=True)
    top, bottom = pl.pallas_call(
        unpack_kernel,
        out_shape=(jax.ShapeDtypeStruct((HALF, 512), bf16),) * 2,
        in_specs=[vmem()],
        out_specs=(vmem(), vmem()),
        scratch_shapes=[pltpu.VMEM((HALF, 512), f32)],
        compiler_params=params(),
        name="unpack",
    )(arrived)
    top, bottom, up_sent = lax.optimization_barrier((top, bottom, pick(w_up, 1 - i)))
    up_par = x_swap(up_sent)
    top_back, bottom_ahead = y_shift(top, 1), y_shift(bottom, 3)
    bottom_back, top_ahead = y_shift(bottom, 1), y_shift(top, 3)
    top_far, bottom_far = y_shift(top_back, 1), y_shift(bottom_ahead, 3)
    act = pl.pallas_call(
        gate_up_kernel,
        out_shape=jax.ShapeDtypeStruct((2 * HALF, 256), bf16),
        in_specs=[smem()] + [vmem()] * 8 + [anywhere()] * 5,
        out_specs=vmem(),
        scratch_shapes=[
            pltpu.VMEM((3, 2048), f32),
            pltpu.VMEM((4, 2048, 128), bf16),
            pltpu.SemaphoreType.DMA((5,)),
        ],
        compiler_params=params(),
        name="gate_up",
    )(
        here,
        *(top, top_back, top_ahead, top_far),
        *(bottom, bottom_back, bottom_ahead, bottom_far),
        norm_gains,
        w_gate,
        w_up,
        gate_par,
        up_par,
    )
    out = pl.pallas_call(
        down_kernel,
        out_shape=jax.ShapeDtypeStruct((WIDE, 2 * CAP, 256), bf16),
        in_specs=[smem()] + [vmem()] * 4 + [anywhere()] * 5,
        out_specs=vmem(),
        scratch_shapes=[pltpu.VMEM((4, 256, 512), bf16), pltpu.SemaphoreType.DMA((2, 4))],
        compiler_params=params(),
        name="down",
    )(here, act, *(y_shift(act, k) for k in (1, 2, 3)), *downs, down_par)
    hf = hidden.astype(f32)
    gain_mine = lax.dynamic_slice_in_dim(norm_gains[1], j * 512, 512, 0)
    router_mine = lax.dynamic_slice_in_dim(w_router, j * 512, 512, 0)
    part = jnp.dot((hf * gain_mine).astype(bf16), router_mine, preferred_element_type=f32)
    square = jnp.sum(hf * hf, axis=1, keepdims=True)
    part = jnp.concatenate([part, jnp.broadcast_to(square, (TOK, EXPERTS))], axis=1)
    out, part = lax.optimization_barrier((out, part))
    back = lax.all_to_all(out, W, 0, 0, tiled=True)
    whole = part
    for k in (1, 2, 3):
        whole = whole + y_shift(part, k)
    logits = whole[:, :EXPERTS] * lax.rsqrt(whole[:, EXPERTS : EXPERTS + 1] / 2048.0 + EPS)
    lifted = jax.nn.sigmoid(logits)
    onehot = jnp.sum(
        (routes[:, :, None] == jnp.arange(EXPERTS, dtype=jnp.int32)[None, None, :]).astype(f32),
        axis=1,
    )
    lifted = lifted * onehot
    gates = lifted / jnp.sum(lifted, axis=1, keepdims=True)
    gates = lax.dynamic_index_in_dim(gates.reshape(TOK, WIDE, 2), i, 2, keepdims=False).T

    moe = jnp.zeros((2 * TOK, 256), f32)
    contract = (((0, 1), (0, 1)), ((), ()))
    mixing = jnp.where(chosen, gates[:, None, :], 0.0)
    blank = jnp.zeros_like(mixing)
    mixing = jnp.concatenate(
        [
            jnp.concatenate([mixing, blank], axis=1),
            jnp.concatenate([blank, mixing], axis=1),
        ],
        axis=2,
    )
    mixing_hi = lax.reduce_precision(mixing, 8, 7)
    mixing_lo = (mixing - mixing_hi).astype(bf16)
    for matrix in lax.optimization_barrier((mixing_hi.astype(bf16), mixing_lo)):
        moe = moe + lax.dot_general(matrix, back, contract, preferred_element_type=f32)
    moe = moe.astype(bf16)
    moe_par = x_swap(moe)
    layer, part = pl.pallas_call(
        embed_kernel,
        out_shape=(
            jax.ShapeDtypeStruct((TOK, 512), bf16),
            jax.ShapeDtypeStruct((TOK + 16, 128), bf16),
        ),
        in_specs=[smem()] + [vmem()] * 5,
        out_specs=(vmem(), vmem()),
        compiler_params=params(),
        name="embed",
    )(here, hidden, moe, moe_par, norm_gains, w_proj)
    parts = [part] + [y_shift(part, k) for k in (1, 2, 3)]

    vectors = pl.pallas_call(
        vector_kernel,
        out_shape=jax.ShapeDtypeStruct((16, TOK, 128), bf16),
        in_specs=[vmem()] * 4,
        out_specs=vmem(),
        compiler_params=params(),
        name="vectors",
    )(*parts)
    vectors, layer = lax.optimization_barrier((vectors, layer))
    layers = [layer] + [y_shift(layer, k) for k in (1, 2, 3)]
    own = lax.all_to_all(vectors, ("z", "xl"), 0, 0, tiled=True).reshape(16 * TOK, 128)
    segment = doc_segment[0]
    requests = doc_request[0]
    docs = jnp.arange(16, dtype=jnp.int32)
    first = jnp.sum((segment[None, :] < docs[:, None]).astype(jnp.int32), axis=1)
    size = jnp.sum((segment[None, :] == docs[:, None]).astype(jnp.int32), axis=1)
    starts = jnp.cumsum(request_lengths, axis=1) - request_lengths
    starts = (starts + TOK * (jnp.arange(WIDE, dtype=jnp.int32) // 2)[:, None]).reshape(-1)
    match = requests[:, None] == jnp.arange(96, dtype=jnp.int32)[None, :]
    q_first = jnp.sum(jnp.where(match, starts[None, :], 0), axis=1)
    q_size = jnp.sum(jnp.where(match, request_lengths.reshape(-1)[None, :], 0), axis=1)
    away = lax.rem(requests // 3, 2) ^ core
    info = jnp.stack([first, size, q_first, q_size, away])
    own, info, *layers = lax.optimization_barrier((own, info, *layers))
    other = lax.ppermute(own, "core", [(0, 1), (1, 0)])
    layer_out = pl.pallas_call(
        assemble_kernel,
        out_shape=jax.ShapeDtypeStruct((TOK, 2048), bf16),
        in_specs=[smem()] + [vmem()] * 4,
        out_specs=vmem(),
        compiler_params=params(),
        name="assemble",
    )(here, *layers)
    doc_scores = pl.pallas_call(
        score_kernel,
        out_shape=jax.ShapeDtypeStruct((1, 16), f32),
        in_specs=[smem(), vmem()] + [anywhere()] * 2,
        out_specs=vmem(),
        scratch_shapes=[pltpu.VMEM((16, 128, 128), bf16), pltpu.SemaphoreType.DMA((16,))],
        compiler_params=params(),
        name="score",
    )(info, doc_vectors, own, other)
    return (layer_out, doc_scores)


def solution(mesh):
    split = Mesh(mesh.devices.reshape(8, 2, 2, 2, 4), ("z", "xl", "core", "xh", "y"))
    placed = (
        P(W, None),
        P(),
        P(None, None, N),
        P(None, N),
        P(N, None),
        P(),
        P(),
        P(W, None),
        P(W, None, N),
        P(W, None, N),
        P(W, N, None),
        P(),
        P(W + N, None),
        P(W + N, None),
        P(W + N, None),
    )
    return jax.shard_map(
        body,
        mesh=split,
        in_specs=placed,
        out_specs=(P(W, None), P(W + N, None)),
        check_vma=False,
    )
```

```python
import math

import jax
import jax.numpy as jnp
from jax import lax
from jax.experimental import pallas as pl
from jax.experimental.pallas import tpu as pltpu
from jax.sharding import Mesh, PartitionSpec as P

HD = 128
TOPK = 8
TOK = 128
CAP = 20
EXPERTS = 64
WIDE = 32
HALF = WIDE * CAP // 2
EPS = 1e-06
THETA = 50000.0
NEG = -1e30
W = ("z", "xl", "core")
N = ("xh", "y")
f32 = jnp.float32
bf16 = jnp.bfloat16


def y_shift(x, k):
    return lax.ppermute(x, "y", [(s, (s + k) % 4) for s in range(4)])


def x_swap(x):
    return lax.ppermute(x, "xh", [(0, 1), (1, 0)])


def attention_kernel(
    i_ref,
    j_ref,
    wide_ref,
    lengths_ref,
    qk_ref,
    gain_ref,
    x_hbm,
    w_hbm,
    out_hbm,
    gate_hbm,
    out0,
    out1,
    out2,
    out3,
    sent_ref,
    x_ref,
    w_ref,
    out_w_ref,
    sems,
):
    copies = [pltpu.make_async_copy(x_hbm, x_ref, sems.at[0])]
    copies += [
        pltpu.make_async_copy(w_hbm.at[part], w_ref.at[part], sems.at[1 + part]) for part in range(3)
    ]
    copies += [pltpu.make_async_copy(out_hbm, out_w_ref, sems.at[4])]
    copies += [pltpu.make_async_copy(gate_hbm.at[1 - i_ref[0]], sent_ref, sems.at[5])]
    for copy in copies:
        copy.start()
    wide = wide_ref[0]
    one = lengths_ref[0, wide]
    two = one + lengths_ref[1, wide]

    def member_of(places):
        return (places >= one).astype(jnp.int32) + (places >= two).astype(jnp.int32)

    down_places = lax.broadcasted_iota(jnp.int32, (TOK, HD), 0)
    across_places = lax.broadcasted_iota(jnp.int32, (TOK, HD), 1)
    member = member_of(down_places)
    same = member == member_of(across_places)
    start = jnp.where(member == 0, 0, jnp.where(member == 1, one, two))
    half = lax.rem(across_places, HD // 2).astype(f32)
    freq = jnp.exp(half * (-math.log(THETA) / (HD // 2)))
    angle = (down_places - start).astype(f32) * freq
    cosine = jnp.cos(angle)
    sine = jnp.sin(angle)
    sine = jnp.where(across_places < HD // 2, -sine, sine)

    copies[0].wait()
    x = x_ref[...].astype(f32)
    scale = lax.rsqrt(jnp.mean(x * x, axis=1, keepdims=True) + EPS)
    normed = (x * scale * gain_ref[0:1, :]).astype(bf16)
    parts = []
    for part in range(3):
        copies[1 + part].wait()
        parts.append(jnp.dot(normed, w_ref[part], preferred_element_type=f32))
    query, keys, values = parts

    def turned(v, gain):
        v = v * lax.rsqrt(jnp.mean(v * v, axis=1, keepdims=True) + EPS) * gain
        return (v * cosine + pltpu.roll(v, HD // 2, 1) * sine).astype(bf16)

    mixed = []
    for head in range(2):
        at = slice(head * HD, (head + 1) * HD)
        q = turned(query[:, at], qk_ref[0:1, at])
        k = turned(keys[:, at], qk_ref[1:2, at])
        scores = lax.dot_general(q, k, (((1,), (1,)), ((), ())), preferred_element_type=f32)
        scores = jnp.where(same, scores * HD ** (-0.5), NEG)
        weights = jnp.exp(scores - jnp.max(scores, axis=1, keepdims=True))
        probs = (weights / jnp.sum(weights, axis=1, keepdims=True)).astype(bf16)
        mixed.append(
            jnp.dot(probs, values[:, at].astype(bf16), preferred_element_type=f32).astype(bf16)
        )
    mixed = jnp.concatenate(mixed, axis=1)
    copies[4].wait()
    j = j_ref[0]
    for k, out_ref in enumerate((out0, out1, out2, out3)):
        part = lax.rem(j + k, 4)
        columns = pl.ds(pl.multiple_of(part * 512, 512), 512)
        out_ref[...] = jnp.dot(mixed, out_w_ref[:, columns], preferred_element_type=f32).astype(bf16)
    copies[5].wait()


def choose_kernel(here_ref, routes_ref, out_ref):
    expert = 2 * lax.broadcasted_iota(jnp.int32, (WIDE, TOK), 0) + here_ref[0]
    hit = jnp.zeros((WIDE, TOK), f32)
    for k in range(TOPK):
        hit = hit + (routes_ref[k : k + 1, :] == expert).astype(f32)
    sooner = lax.broadcasted_iota(jnp.int32, (TOK, TOK), 0)
    earlier = (sooner < lax.broadcasted_iota(jnp.int32, (TOK, TOK), 1)).astype(f32).astype(bf16)
    before = jnp.dot(hit.astype(bf16), earlier, preferred_element_type=f32)
    place = jnp.where(hit > 0, before, -1.0).astype(bf16)
    owner = CAP * lax.broadcasted_iota(jnp.int32, (WIDE * CAP, WIDE), 1)
    slot = lax.broadcasted_iota(jnp.int32, (WIDE * CAP, WIDE), 0) - owner
    inside = (slot >= 0) & (slot < CAP)
    spread = jnp.dot(inside.astype(f32).astype(bf16), place, preferred_element_type=f32)
    slot = jnp.sum(jnp.where(inside, slot, 0).astype(f32), axis=1, keepdims=True)
    out_ref[...] = (spread == slot).astype(f32).astype(bf16)


def packed(rows):
    return jnp.concatenate([rows[:, 0:256], rows[:, 256:512]], axis=0).astype(bf16)


def dispatch_kernel(here_ref, x_ref, own_ref, par_ref, choose_ref, hidden_ref, rows_ref):
    j = here_ref[1]
    mine = x_ref[:, pl.ds(pl.multiple_of(j * 512, 512), 512)].astype(f32)
    hidden = (mine + (own_ref[...].astype(f32) + par_ref[...].astype(f32))).astype(bf16)
    hidden_ref[...] = hidden
    rows = jnp.dot(choose_ref[...], hidden, preferred_element_type=f32)
    for s in range(WIDE):
        rows_ref[s] = packed(rows[s * CAP : (s + 1) * CAP])


def unpack_kernel(in_ref, top_ref, bottom_ref, scratch):
    for half, out_ref in enumerate((top_ref, bottom_ref)):
        for s in range(WIDE // 2):
            rows = in_ref[half * (WIDE // 2) + s].astype(f32)
            at = slice(s * CAP, (s + 1) * CAP)
            scratch[at, 0:256] = rows[0:CAP]
            scratch[at, 256:512] = rows[CAP:]
        out_ref[...] = scratch[...].astype(bf16)


def gate_up_kernel(here_ref, *refs):
    halves = refs[0:4], refs[4:8]
    gain_hbm, gate_hbm, up_hbm, gate_par, up_par, out_ref, gain_ref, w_ref, sems = refs[8:]
    i, j = here_ref[0], here_ref[1]
    sources = (gate_hbm.at[i], up_hbm.at[i], gate_par, up_par)
    copies = [
        pltpu.make_async_copy(source, w_ref.at[n], sems.at[n]) for n, source in enumerate(sources)
    ]
    copies.append(pltpu.make_async_copy(gain_hbm, gain_ref, sems.at[4]))
    for copy in copies:
        copy.start()
    scales = []
    for xs in halves:
        total = jnp.zeros((HALF, 1), f32)
        for x in xs:
            v = x[...].astype(f32)
            total = total + jnp.sum(v * v, axis=1, keepdims=True)
        scales.append(lax.rsqrt(total / 2048.0 + EPS))
    for copy in copies:
        copy.wait()
    for half, (xs, scale) in enumerate(zip(halves, scales)):
        own = jnp.zeros((HALF, 256), f32)
        par = jnp.zeros((HALF, 256), f32)
        for k, x in enumerate(xs):
            part = lax.rem(j + 4 + (0, -1, 1, 2)[k], 4)
            rows = pl.ds(pl.multiple_of(part * 512, 512), 512)
            normed = (x[...].astype(f32) * scale * gain_ref[1:2, rows]).astype(bf16)
            w_own = jnp.concatenate([w_ref[0, rows, :], w_ref[1, rows, :]], axis=1)
            w_par = jnp.concatenate([w_ref[2, rows, :], w_ref[3, rows, :]], axis=1)
            own = own + jnp.dot(normed, w_own, preferred_element_type=f32)
            par = par + jnp.dot(normed, w_par, preferred_element_type=f32)
        for at, both in ((0, own), (128, par)):
            gate, up = both[:, :128], both[:, 128:]
            out_ref[half * HALF : (half + 1) * HALF, at : at + 128] = (
                gate / (1.0 + jnp.exp(-gate)) * up
            ).astype(bf16)


def down_kernel(here_ref, a0, a1, a2, a3, w0, w1, w2, w3, par_ref, out_ref, w_ref, sems):
    i = here_ref[0]
    copies = []
    for k, w in enumerate((w0, w1, w2, w3)):
        copies.append(
            (
                pltpu.make_async_copy(w.at[i], w_ref.at[k, 0:128], sems.at[0, k]),
                pltpu.make_async_copy(par_ref.at[k], w_ref.at[k, 128:256], sems.at[1, k]),
            )
        )
    for pair in copies:
        for copy in pair:
            copy.start()
    total = jnp.zeros((a0.shape[0], 512), f32)
    for k, a in enumerate((a0, a1, a2, a3)):
        for copy in copies[k]:
            copy.wait()
        total = total + jnp.dot(a[...], w_ref[k], preferred_element_type=f32)
    for s in range(WIDE):
        out_ref[s] = packed(total[s * CAP : (s + 1) * CAP])


def embed_kernel(here_ref, hidden_ref, moe_ref, par_ref, gain_ref, w_ref, layer_ref, part_ref):
    mine = pl.ds(pl.multiple_of(here_ref[1] * 512, 512), 512)
    moe = moe_ref[...].astype(f32) + par_ref[...].astype(f32)
    layer = hidden_ref[...].astype(f32) + jnp.concatenate([moe[0:TOK], moe[TOK:]], axis=1)
    layer = layer.astype(bf16)
    layer_ref[...] = layer
    layer = layer.astype(f32)
    scaled = (layer * gain_ref[2:3, mine]).astype(bf16)
    part = jnp.dot(scaled, w_ref[mine, :], preferred_element_type=f32)
    part_ref[0:TOK, :] = part.astype(bf16)
    square = jnp.broadcast_to(jnp.sum(layer * layer, axis=1, keepdims=True), (TOK, TOK))
    part_ref[TOK:, :] = jnp.transpose(square)[0:16].astype(bf16)


def vector_kernel(p0, p1, p2, p3, out_ref):
    whole = sum(p[...].astype(f32) for p in (p0, p1, p2, p3))
    square = jnp.transpose(jnp.broadcast_to(whole[TOK : TOK + 1], (TOK, TOK)))
    embedded = whole[0:TOK] * lax.rsqrt(square / 2048.0 + EPS)
    norm = jnp.sum(embedded * embedded, axis=1, keepdims=True)
    vectors = (embedded * lax.rsqrt(norm + EPS)).astype(bf16)
    for copy in range(16):
        out_ref[copy] = vectors


def assemble_kernel(here_ref, p0, p1, p2, p3, out_ref):
    j = here_ref[1]
    for k, piece in enumerate((p0, p1, p2, p3)):
        part = lax.rem(j - k + 4, 4)
        out_ref[:, pl.ds(pl.multiple_of(part * 512, 512), 512)] = piece[...]


def score_kernel(info_ref, doc_ref, own_ref, other_ref, out_ref, query_ref, sems):
    def spot(d):
        return pl.multiple_of(jnp.minimum((info_ref[2, d] // 16) * 16, 2048 - 128), 16)

    def copy_of(ref, d):
        return pltpu.make_async_copy(ref.at[pl.ds(spot(d), 128), :], query_ref.at[d], sems.at[d])

    for d in range(16):

        @pl.when(info_ref[4, d] == 0)
        def _():
            copy_of(own_ref, d).start()

        @pl.when(info_ref[4, d] != 0)
        def _():
            copy_of(other_ref, d).start()

    lane = lax.broadcasted_iota(jnp.int32, (1, 16), 1)
    scores = jnp.zeros((1, 16), f32)
    rows = lax.broadcasted_iota(jnp.int32, (144, 128), 0)
    columns = lax.broadcasted_iota(jnp.int32, (1, 128), 1)
    for d in range(16):
        copy_of(own_ref, d).wait()
    for d in range(16):
        first, size = info_ref[0, d], info_ref[1, d]
        q_first, q_size = info_ref[2, d], info_ref[3, d]
        at = pl.multiple_of(jnp.minimum((first // 16) * 16, 1024 - 144), 16)
        sims = lax.dot_general(
            doc_ref[pl.ds(at, 144), :],
            query_ref[d],
            (((1,), (1,)), ((), ())),
            preferred_element_type=f32,
        )
        keep = (rows >= first - at) & (rows < first - at + size)
        best = jnp.max(jnp.where(keep, sims, NEG), axis=0, keepdims=True)
        q_start = q_first - spot(d)
        used = (columns >= q_start) & (columns < q_start + q_size)
        value = jnp.sum(jnp.where(used, best, 0.0), axis=1, keepdims=True) / q_size.astype(f32)
        scores = jnp.where(lane == d, value, scores)
    out_ref[...] = scores


def vmem():
    return pl.BlockSpec(memory_space=pltpu.VMEM)


def smem():
    return pl.BlockSpec(memory_space=pltpu.SMEM)


def hbm():
    return pl.BlockSpec(memory_space=pltpu.HBM)


def anywhere():
    return pl.BlockSpec(memory_space=pl.ANY)


def params():
    return pltpu.CompilerParams(vmem_limit_bytes=16 << 20)


def body(
    tokens,
    request_lengths,
    w_qkv,
    qk_gain,
    w_out,
    norm_gains,
    w_router,
    routes,
    w_gate,
    w_up,
    w_down,
    w_proj,
    doc_vectors,
    doc_segment,
    doc_request,
):
    i = lax.axis_index("xh")
    j = lax.axis_index("y")
    core = lax.axis_index("core")
    wide = lax.axis_index(W)
    here = jnp.stack([i, j, wide, core])

    def pick(array, which):
        return lax.dynamic_index_in_dim(array, which, 0, keepdims=False)

    def cut(array, part, axis):
        return lax.dynamic_slice_in_dim(array, lax.rem(part, 4) * 512, 512, axis)

    *attn, gate_sent = pl.pallas_call(
        attention_kernel,
        out_shape=(
            *(jax.ShapeDtypeStruct((TOK, 512), bf16),) * 4,
            jax.ShapeDtypeStruct((2048, 128), bf16),
        ),
        in_specs=[smem()] * 4 + [vmem()] * 2 + [hbm()] * 4,
        out_specs=(vmem(),) * 5,
        scratch_shapes=[
            pltpu.VMEM((TOK, 2048), bf16),
            pltpu.VMEM((3, 2048, 256), bf16),
            pltpu.VMEM((256, 2048), bf16),
            pltpu.SemaphoreType.DMA((6,)),
        ],
        compiler_params=pltpu.CompilerParams(vmem_limit_bytes=60 << 20),
        name="attention",
    )(
        i.reshape(1),
        j.reshape(1),
        wide.reshape(1),
        request_lengths.T,
        qk_gain,
        norm_gains,
        tokens,
        w_qkv.transpose(1, 0, 2),
        w_out,
        w_gate,
    )
    gate_par = x_swap(gate_sent)
    attn_parts = [y_shift(attn[k], k) for k in (1, 2, 3)]

    downs = [cut(w_down, j, 2)] + [y_shift(cut(w_down, j + k, 2), k) for k in (1, 2, 3)]
    down_par = x_swap(jnp.stack([pick(d, 1 - i) for d in downs]))

    experts_here = 2 * jnp.arange(WIDE, dtype=jnp.int32) + i
    hit = jnp.sum((routes.T[None, :, :] == experts_here[:, None, None]).astype(f32), axis=1)
    places = jnp.arange(TOK, dtype=jnp.int32)
    earlier = (places[:, None] < places[None, :]).astype(bf16)
    before = jnp.dot(hit.astype(bf16), earlier, preferred_element_type=f32)
    slot = jnp.arange(CAP, dtype=jnp.int32).astype(f32)
    chosen = (before[:, None, :] == slot[None, :, None]) & (hit[:, None, :] > 0)
    choose = pl.pallas_call(
        choose_kernel,
        out_shape=jax.ShapeDtypeStruct((WIDE * CAP, TOK), bf16),
        in_specs=[smem(), vmem()],
        out_specs=vmem(),
        compiler_params=params(),
        name="choose",
    )(here, routes.T)

    attn = (attn[0].astype(f32) + sum(p.astype(f32) for p in attn_parts)).astype(bf16)
    attn, choose = lax.optimization_barrier((attn, choose))
    attn_par = x_swap(attn)
    attn_par, gate_par = lax.optimization_barrier((attn_par, gate_par))
    hidden, rows = pl.pallas_call(
        dispatch_kernel,
        out_shape=(
            jax.ShapeDtypeStruct((TOK, 512), bf16),
            jax.ShapeDtypeStruct((WIDE, 2 * CAP, 256), bf16),
        ),
        in_specs=[smem()] + [vmem()] * 4,
        out_specs=(vmem(), vmem()),
        compiler_params=params(),
        name="dispatch",
    )(here, tokens, attn, attn_par, choose)

    hf = hidden.astype(f32)
    gain_mine = lax.dynamic_slice_in_dim(norm_gains[1], j * 512, 512, 0)
    router_mine = lax.dynamic_slice_in_dim(w_router, j * 512, 512, 0)
    part = jnp.dot((hf * gain_mine).astype(bf16), router_mine, preferred_element_type=f32)
    square = jnp.sum(hf * hf, axis=1, keepdims=True)
    part = jnp.concatenate([part, jnp.broadcast_to(square, (TOK, EXPERTS))], axis=1)
    whole = part
    for k in (1, 2, 3):
        whole = whole + y_shift(part, k)

    arrived = lax.all_to_all(rows, W, 0, 0, tiled=True)
    top, bottom = pl.pallas_call(
        unpack_kernel,
        out_shape=(jax.ShapeDtypeStruct((HALF, 512), bf16),) * 2,
        in_specs=[vmem()],
        out_specs=(vmem(), vmem()),
        scratch_shapes=[pltpu.VMEM((HALF, 512), f32)],
        compiler_params=params(),
        name="unpack",
    )(arrived)
    top, bottom, up_sent, whole = lax.optimization_barrier(
        (top, bottom, pick(w_up, 1 - i), whole)
    )
    up_par = x_swap(up_sent)
    top_back, bottom_ahead = y_shift(top, 1), y_shift(bottom, 3)
    bottom_back, top_ahead = y_shift(bottom, 1), y_shift(top, 3)
    top_far, bottom_far = y_shift(top_back, 1), y_shift(bottom_ahead, 3)
    act = pl.pallas_call(
        gate_up_kernel,
        out_shape=jax.ShapeDtypeStruct((2 * HALF, 256), bf16),
        in_specs=[smem()] + [vmem()] * 8 + [anywhere()] * 5,
        out_specs=vmem(),
        scratch_shapes=[
            pltpu.VMEM((3, 2048), f32),
            pltpu.VMEM((4, 2048, 128), bf16),
            pltpu.SemaphoreType.DMA((5,)),
        ],
        compiler_params=params(),
        name="gate_up",
    )(
        here,
        *(top, top_back, top_ahead, top_far),
        *(bottom, bottom_back, bottom_ahead, bottom_far),
        norm_gains,
        w_gate,
        w_up,
        gate_par,
        up_par,
    )
    out = pl.pallas_call(
        down_kernel,
        out_shape=jax.ShapeDtypeStruct((WIDE, 2 * CAP, 256), bf16),
        in_specs=[smem()] + [vmem()] * 4 + [anywhere()] * 5,
        out_specs=vmem(),
        scratch_shapes=[pltpu.VMEM((4, 256, 512), bf16), pltpu.SemaphoreType.DMA((2, 4))],
        compiler_params=params(),
        name="down",
    )(here, act, *(y_shift(act, k) for k in (1, 2, 3)), *downs, down_par)
    back = lax.all_to_all(out, W, 0, 0, tiled=True)

    logits = whole[:, :EXPERTS] * lax.rsqrt(whole[:, EXPERTS : EXPERTS + 1] / 2048.0 + EPS)
    lifted = jax.nn.sigmoid(logits)
    onehot = jnp.sum(
        (routes[:, :, None] == jnp.arange(EXPERTS, dtype=jnp.int32)[None, None, :]).astype(f32),
        axis=1,
    )
    lifted = lifted * onehot
    gates = lifted / jnp.sum(lifted, axis=1, keepdims=True)
    gates = lax.dynamic_index_in_dim(gates.reshape(TOK, WIDE, 2), i, 2, keepdims=False).T

    moe = jnp.zeros((2 * TOK, 256), f32)
    contract = (((0, 1), (0, 1)), ((), ()))
    mixing = jnp.where(chosen, gates[:, None, :], 0.0)
    blank = jnp.zeros_like(mixing)
    mixing = jnp.concatenate(
        [
            jnp.concatenate([mixing, blank], axis=1),
            jnp.concatenate([blank, mixing], axis=1),
        ],
        axis=2,
    )
    mixing_hi = lax.reduce_precision(mixing, 8, 7)
    mixing_lo = (mixing - mixing_hi).astype(bf16)
    for matrix in lax.optimization_barrier((mixing_hi.astype(bf16), mixing_lo)):
        moe = moe + lax.dot_general(matrix, back, contract, preferred_element_type=f32)
    moe = moe.astype(bf16)
    moe_par = x_swap(moe)
    layer, part = pl.pallas_call(
        embed_kernel,
        out_shape=(
            jax.ShapeDtypeStruct((TOK, 512), bf16),
            jax.ShapeDtypeStruct((TOK + 16, 128), bf16),
        ),
        in_specs=[smem()] + [vmem()] * 5,
        out_specs=(vmem(), vmem()),
        compiler_params=params(),
        name="embed",
    )(here, hidden, moe, moe_par, norm_gains, w_proj)
    parts = [part] + [y_shift(part, k) for k in (1, 2, 3)]

    vectors = pl.pallas_call(
        vector_kernel,
        out_shape=jax.ShapeDtypeStruct((16, TOK, 128), bf16),
        in_specs=[vmem()] * 4,
        out_specs=vmem(),
        compiler_params=params(),
        name="vectors",
    )(*parts)
    vectors, layer = lax.optimization_barrier((vectors, layer))
    layers = [layer] + [y_shift(layer, k) for k in (1, 2, 3)]
    own = lax.all_to_all(vectors, ("z", "xl"), 0, 0, tiled=True).reshape(16 * TOK, 128)
    segment = doc_segment[0]
    requests = doc_request[0]
    docs = jnp.arange(16, dtype=jnp.int32)
    first = jnp.sum((segment[None, :] < docs[:, None]).astype(jnp.int32), axis=1)
    size = jnp.sum((segment[None, :] == docs[:, None]).astype(jnp.int32), axis=1)
    starts = jnp.cumsum(request_lengths, axis=1) - request_lengths
    starts = (starts + TOK * (jnp.arange(WIDE, dtype=jnp.int32) // 2)[:, None]).reshape(-1)
    match = requests[:, None] == jnp.arange(96, dtype=jnp.int32)[None, :]
    q_first = jnp.sum(jnp.where(match, starts[None, :], 0), axis=1)
    q_size = jnp.sum(jnp.where(match, request_lengths.reshape(-1)[None, :], 0), axis=1)
    away = lax.rem(requests // 3, 2) ^ core
    info = jnp.stack([first, size, q_first, q_size, away])
    own, info, *layers = lax.optimization_barrier((own, info, *layers))
    other = lax.ppermute(own, "core", [(0, 1), (1, 0)])
    layer_out = pl.pallas_call(
        assemble_kernel,
        out_shape=jax.ShapeDtypeStruct((TOK, 2048), bf16),
        in_specs=[smem()] + [vmem()] * 4,
        out_specs=vmem(),
        compiler_params=params(),
        name="assemble",
    )(here, *layers)
    doc_scores = pl.pallas_call(
        score_kernel,
        out_shape=jax.ShapeDtypeStruct((1, 16), f32),
        in_specs=[smem(), vmem()] + [anywhere()] * 2,
        out_specs=vmem(),
        scratch_shapes=[pltpu.VMEM((16, 128, 128), bf16), pltpu.SemaphoreType.DMA((16,))],
        compiler_params=params(),
        name="score",
    )(info, doc_vectors, own, other)
    return (layer_out, doc_scores)


def solution(mesh):
    split = Mesh(mesh.devices.reshape(8, 2, 2, 2, 4), ("z", "xl", "core", "xh", "y"))
    placed = (
        P(W, None),
        P(),
        P(None, None, N),
        P(None, N),
        P(N, None),
        P(),
        P(),
        P(W, None),
        P(W, None, N),
        P(W, None, N),
        P(W, N, None),
        P(),
        P(W + N, None),
        P(W + N, None),
        P(W + N, None),
    )
    return jax.shard_map(
        body,
        mesh=split,
        in_specs=placed,
        out_specs=(P(W, None), P(W + N, None)),
        check_vma=False,
    )
```

```python
import math

import jax
import jax.numpy as jnp
from jax import lax
from jax.experimental import pallas as pl
from jax.experimental.pallas import tpu as pltpu
from jax.sharding import Mesh, PartitionSpec as P

HD = 128
TOPK = 8
TOK = 128
CAP = 20
EXPERTS = 64
WIDE = 32
HALF = WIDE * CAP // 2
EPS = 1e-06
THETA = 50000.0
NEG = -1e30
W = ("z", "xl", "core")
N = ("xh", "y")
f32 = jnp.float32
bf16 = jnp.bfloat16


def y_shift(x, k):
    return lax.ppermute(x, "y", [(s, (s + k) % 4) for s in range(4)])


def x_swap(x):
    return lax.ppermute(x, "xh", [(0, 1), (1, 0)])


def attention_kernel(
    i_ref,
    j_ref,
    wide_ref,
    lengths_ref,
    qk_ref,
    gain_ref,
    x_hbm,
    w_hbm,
    out_hbm,
    gate_hbm,
    out0,
    out1,
    out2,
    out3,
    sent_ref,
    x_ref,
    w_ref,
    out_w_ref,
    sems,
):
    copies = [pltpu.make_async_copy(x_hbm, x_ref, sems.at[0])]
    copies += [
        pltpu.make_async_copy(w_hbm.at[part], w_ref.at[part], sems.at[1 + part]) for part in range(3)
    ]
    copies += [pltpu.make_async_copy(out_hbm, out_w_ref, sems.at[4])]
    copies += [pltpu.make_async_copy(gate_hbm.at[1 - i_ref[0]], sent_ref, sems.at[5])]
    for copy in copies:
        copy.start()
    wide = wide_ref[0]
    one = lengths_ref[0, wide]
    two = one + lengths_ref[1, wide]

    def member_of(places):
        return (places >= one).astype(jnp.int32) + (places >= two).astype(jnp.int32)

    down_places = lax.broadcasted_iota(jnp.int32, (TOK, HD), 0)
    across_places = lax.broadcasted_iota(jnp.int32, (TOK, HD), 1)
    member = member_of(down_places)
    same = member == member_of(across_places)
    start = jnp.where(member == 0, 0, jnp.where(member == 1, one, two))
    half = lax.rem(across_places, HD // 2).astype(f32)
    freq = jnp.exp(half * (-math.log(THETA) / (HD // 2)))
    angle = (down_places - start).astype(f32) * freq
    cosine = jnp.cos(angle)
    sine = jnp.sin(angle)
    sine = jnp.where(across_places < HD // 2, -sine, sine)

    copies[0].wait()
    x = x_ref[...].astype(f32)
    scale = lax.rsqrt(jnp.mean(x * x, axis=1, keepdims=True) + EPS)
    normed = (x * scale * gain_ref[0:1, :]).astype(bf16)
    parts = []
    for part in range(3):
        copies[1 + part].wait()
        parts.append(jnp.dot(normed, w_ref[part], preferred_element_type=f32))
    query, keys, values = parts

    def turned(v, gain):
        v = v * lax.rsqrt(jnp.mean(v * v, axis=1, keepdims=True) + EPS) * gain
        return (v * cosine + pltpu.roll(v, HD // 2, 1) * sine).astype(bf16)

    mixed = []
    for head in range(2):
        at = slice(head * HD, (head + 1) * HD)
        q = turned(query[:, at], qk_ref[0:1, at])
        k = turned(keys[:, at], qk_ref[1:2, at])
        scores = lax.dot_general(q, k, (((1,), (1,)), ((), ())), preferred_element_type=f32)
        scores = jnp.where(same, scores * HD ** (-0.5), NEG)
        weights = jnp.exp(scores - jnp.max(scores, axis=1, keepdims=True))
        probs = (weights / jnp.sum(weights, axis=1, keepdims=True)).astype(bf16)
        mixed.append(
            jnp.dot(probs, values[:, at].astype(bf16), preferred_element_type=f32).astype(bf16)
        )
    mixed = jnp.concatenate(mixed, axis=1)
    copies[4].wait()
    j = j_ref[0]
    for k, out_ref in enumerate((out0, out1, out2, out3)):
        part = lax.rem(j + k, 4)
        columns = pl.ds(pl.multiple_of(part * 512, 512), 512)
        out_ref[...] = jnp.dot(mixed, out_w_ref[:, columns], preferred_element_type=f32).astype(bf16)
    copies[5].wait()


def choose_kernel(here_ref, routes_ref, out_ref):
    expert = 2 * lax.broadcasted_iota(jnp.int32, (WIDE, TOK), 0) + here_ref[0]
    hit = jnp.zeros((WIDE, TOK), f32)
    for k in range(TOPK):
        hit = hit + (routes_ref[k : k + 1, :] == expert).astype(f32)
    sooner = lax.broadcasted_iota(jnp.int32, (TOK, TOK), 0)
    earlier = (sooner < lax.broadcasted_iota(jnp.int32, (TOK, TOK), 1)).astype(f32).astype(bf16)
    before = jnp.dot(hit.astype(bf16), earlier, preferred_element_type=f32)
    place = jnp.where(hit > 0, before, -1.0).astype(bf16)
    owner = CAP * lax.broadcasted_iota(jnp.int32, (WIDE * CAP, WIDE), 1)
    slot = lax.broadcasted_iota(jnp.int32, (WIDE * CAP, WIDE), 0) - owner
    inside = (slot >= 0) & (slot < CAP)
    spread = jnp.dot(inside.astype(f32).astype(bf16), place, preferred_element_type=f32)
    slot = jnp.sum(jnp.where(inside, slot, 0).astype(f32), axis=1, keepdims=True)
    out_ref[...] = (spread == slot).astype(f32).astype(bf16)


def packed(rows):
    return jnp.concatenate([rows[:, 0:256], rows[:, 256:512]], axis=0).astype(bf16)


def dispatch_kernel(here_ref, x_ref, own_ref, par_ref, choose_ref, hidden_ref, rows_ref):
    j = here_ref[1]
    mine = x_ref[:, pl.ds(pl.multiple_of(j * 512, 512), 512)].astype(f32)
    hidden = (mine + (own_ref[...].astype(f32) + par_ref[...].astype(f32))).astype(bf16)
    hidden_ref[...] = hidden
    rows = jnp.dot(choose_ref[...], hidden, preferred_element_type=f32)
    for s in range(WIDE):
        rows_ref[s] = packed(rows[s * CAP : (s + 1) * CAP])


def unpack_kernel(in_ref, top_ref, bottom_ref, scratch):
    for half, out_ref in enumerate((top_ref, bottom_ref)):
        for s in range(WIDE // 2):
            rows = in_ref[half * (WIDE // 2) + s].astype(f32)
            at = slice(s * CAP, (s + 1) * CAP)
            scratch[at, 0:256] = rows[0:CAP]
            scratch[at, 256:512] = rows[CAP:]
        out_ref[...] = scratch[...].astype(bf16)


def gate_up_kernel(here_ref, *refs):
    halves = refs[0:4], refs[4:8]
    gain_ref, gate_ref, up_ref, gate_par, up_par, out_ref = refs[8:]
    i, j = here_ref[0], here_ref[1]
    scales = []
    for xs in halves:
        total = jnp.zeros((HALF, 1), f32)
        for x in xs:
            v = x[...].astype(f32)
            total = total + jnp.sum(v * v, axis=1, keepdims=True)
        scales.append(lax.rsqrt(total / 2048.0 + EPS))
    for half, (xs, scale) in enumerate(zip(halves, scales)):
        own = jnp.zeros((HALF, 256), f32)
        par = jnp.zeros((HALF, 256), f32)
        for k, x in enumerate(xs):
            part = lax.rem(j + 4 + (0, -1, 1, 2)[k], 4)
            rows = pl.ds(pl.multiple_of(part * 512, 512), 512)
            normed = (x[...].astype(f32) * scale * gain_ref[1:2, rows]).astype(bf16)
            w_own = jnp.concatenate([gate_ref[i, rows, :], up_ref[i, rows, :]], axis=1)
            w_par = jnp.concatenate([gate_par[rows, :], up_par[rows, :]], axis=1)
            own = own + jnp.dot(normed, w_own, preferred_element_type=f32)
            par = par + jnp.dot(normed, w_par, preferred_element_type=f32)
        for at, both in ((0, own), (128, par)):
            gate, up = both[:, :128], both[:, 128:]
            out_ref[half * HALF : (half + 1) * HALF, at : at + 128] = (
                gate / (1.0 + jnp.exp(-gate)) * up
            ).astype(bf16)


def down_kernel(here_ref, a0, a1, a2, a3, w0, w1, w2, w3, par_ref, out_ref):
    i = here_ref[0]
    total = jnp.zeros((a0.shape[0], 512), f32)
    for k, (a, w) in enumerate(((a0, w0), (a1, w1), (a2, w2), (a3, w3))):
        weight = jnp.concatenate([w[i], par_ref[k]], axis=0)
        total = total + jnp.dot(a[...], weight, preferred_element_type=f32)
    for s in range(WIDE):
        out_ref[s] = packed(total[s * CAP : (s + 1) * CAP])


def embed_kernel(here_ref, hidden_ref, moe_ref, par_ref, gain_ref, w_ref, layer_ref, part_ref):
    mine = pl.ds(pl.multiple_of(here_ref[1] * 512, 512), 512)
    moe = moe_ref[...].astype(f32) + par_ref[...].astype(f32)
    layer = hidden_ref[...].astype(f32) + jnp.concatenate([moe[0:TOK], moe[TOK:]], axis=1)
    layer = layer.astype(bf16)
    layer_ref[...] = layer
    layer = layer.astype(f32)
    scaled = (layer * gain_ref[2:3, mine]).astype(bf16)
    part = jnp.dot(scaled, w_ref[mine, :], preferred_element_type=f32)
    part_ref[0:TOK, :] = part.astype(bf16)
    square = jnp.broadcast_to(jnp.sum(layer * layer, axis=1, keepdims=True), (TOK, TOK))
    part_ref[TOK:, :] = jnp.transpose(square)[0:16].astype(bf16)


def vector_kernel(p0, p1, p2, p3, out_ref):
    whole = sum(p[...].astype(f32) for p in (p0, p1, p2, p3))
    square = jnp.transpose(jnp.broadcast_to(whole[TOK : TOK + 1], (TOK, TOK)))
    embedded = whole[0:TOK] * lax.rsqrt(square / 2048.0 + EPS)
    norm = jnp.sum(embedded * embedded, axis=1, keepdims=True)
    vectors = (embedded * lax.rsqrt(norm + EPS)).astype(bf16)
    for copy in range(16):
        out_ref[copy] = vectors


def assemble_kernel(here_ref, p0, p1, p2, p3, out_ref):
    j = here_ref[1]
    for k, piece in enumerate((p0, p1, p2, p3)):
        part = lax.rem(j - k + 4, 4)
        out_ref[:, pl.ds(pl.multiple_of(part * 512, 512), 512)] = piece[...]


def score_kernel(info_ref, doc_ref, own_ref, other_ref, out_ref, query_ref, sems):
    def spot(d):
        return pl.multiple_of(jnp.minimum((info_ref[2, d] // 16) * 16, 2048 - 128), 16)

    def copy_of(ref, d):
        return pltpu.make_async_copy(ref.at[pl.ds(spot(d), 128), :], query_ref.at[d], sems.at[d])

    for d in range(16):

        @pl.when(info_ref[4, d] == 0)
        def _():
            copy_of(own_ref, d).start()

        @pl.when(info_ref[4, d] != 0)
        def _():
            copy_of(other_ref, d).start()

    lane = lax.broadcasted_iota(jnp.int32, (1, 16), 1)
    scores = jnp.zeros((1, 16), f32)
    rows = lax.broadcasted_iota(jnp.int32, (144, 128), 0)
    columns = lax.broadcasted_iota(jnp.int32, (1, 128), 1)
    for d in range(16):
        copy_of(own_ref, d).wait()
    for d in range(16):
        first, size = info_ref[0, d], info_ref[1, d]
        q_first, q_size = info_ref[2, d], info_ref[3, d]
        at = pl.multiple_of(jnp.minimum((first // 16) * 16, 1024 - 144), 16)
        sims = lax.dot_general(
            doc_ref[pl.ds(at, 144), :],
            query_ref[d],
            (((1,), (1,)), ((), ())),
            preferred_element_type=f32,
        )
        keep = (rows >= first - at) & (rows < first - at + size)
        best = jnp.max(jnp.where(keep, sims, NEG), axis=0, keepdims=True)
        q_start = q_first - spot(d)
        used = (columns >= q_start) & (columns < q_start + q_size)
        value = jnp.sum(jnp.where(used, best, 0.0), axis=1, keepdims=True) / q_size.astype(f32)
        scores = jnp.where(lane == d, value, scores)
    out_ref[...] = scores


def vmem():
    return pl.BlockSpec(memory_space=pltpu.VMEM)


def smem():
    return pl.BlockSpec(memory_space=pltpu.SMEM)


def hbm():
    return pl.BlockSpec(memory_space=pltpu.HBM)


def anywhere():
    return pl.BlockSpec(memory_space=pl.ANY)


def params():
    return pltpu.CompilerParams(vmem_limit_bytes=16 << 20)


def body(
    tokens,
    request_lengths,
    w_qkv,
    qk_gain,
    w_out,
    norm_gains,
    w_router,
    routes,
    w_gate,
    w_up,
    w_down,
    w_proj,
    doc_vectors,
    doc_segment,
    doc_request,
):
    i = lax.axis_index("xh")
    j = lax.axis_index("y")
    core = lax.axis_index("core")
    wide = lax.axis_index(W)
    here = jnp.stack([i, j, wide, core])

    def pick(array, which):
        return lax.dynamic_index_in_dim(array, which, 0, keepdims=False)

    def cut(array, part, axis):
        return lax.dynamic_slice_in_dim(array, lax.rem(part, 4) * 512, 512, axis)

    *attn, gate_sent = pl.pallas_call(
        attention_kernel,
        out_shape=(
            *(jax.ShapeDtypeStruct((TOK, 512), bf16),) * 4,
            jax.ShapeDtypeStruct((2048, 128), bf16),
        ),
        in_specs=[smem()] * 4 + [vmem()] * 2 + [hbm()] * 4,
        out_specs=(vmem(),) * 5,
        scratch_shapes=[
            pltpu.VMEM((TOK, 2048), bf16),
            pltpu.VMEM((3, 2048, 256), bf16),
            pltpu.VMEM((256, 2048), bf16),
            pltpu.SemaphoreType.DMA((6,)),
        ],
        compiler_params=pltpu.CompilerParams(vmem_limit_bytes=60 << 20),
        name="attention",
    )(
        i.reshape(1),
        j.reshape(1),
        wide.reshape(1),
        request_lengths.T,
        qk_gain,
        norm_gains,
        tokens,
        w_qkv.transpose(1, 0, 2),
        w_out,
        w_gate,
    )
    gate_par = x_swap(gate_sent)
    attn_parts = [y_shift(attn[k], k) for k in (1, 2, 3)]

    downs = [cut(w_down, j, 2)] + [y_shift(cut(w_down, j + k, 2), k) for k in (1, 2, 3)]
    down_par = x_swap(jnp.stack([pick(d, 1 - i) for d in downs]))

    experts_here = 2 * jnp.arange(WIDE, dtype=jnp.int32) + i
    hit = jnp.sum((routes.T[None, :, :] == experts_here[:, None, None]).astype(f32), axis=1)
    places = jnp.arange(TOK, dtype=jnp.int32)
    earlier = (places[:, None] < places[None, :]).astype(bf16)
    before = jnp.dot(hit.astype(bf16), earlier, preferred_element_type=f32)
    slot = jnp.arange(CAP, dtype=jnp.int32).astype(f32)
    chosen = (before[:, None, :] == slot[None, :, None]) & (hit[:, None, :] > 0)
    choose = pl.pallas_call(
        choose_kernel,
        out_shape=jax.ShapeDtypeStruct((WIDE * CAP, TOK), bf16),
        in_specs=[smem(), vmem()],
        out_specs=vmem(),
        compiler_params=params(),
        name="choose",
    )(here, routes.T)

    attn = (attn[0].astype(f32) + sum(p.astype(f32) for p in attn_parts)).astype(bf16)
    attn, choose = lax.optimization_barrier((attn, choose))
    attn_par = x_swap(attn)
    attn_par, gate_par = lax.optimization_barrier((attn_par, gate_par))
    hidden, rows = pl.pallas_call(
        dispatch_kernel,
        out_shape=(
            jax.ShapeDtypeStruct((TOK, 512), bf16),
            jax.ShapeDtypeStruct((WIDE, 2 * CAP, 256), bf16),
        ),
        in_specs=[smem()] + [vmem()] * 4,
        out_specs=(vmem(), vmem()),
        compiler_params=params(),
        name="dispatch",
    )(here, tokens, attn, attn_par, choose)

    hf = hidden.astype(f32)
    gain_mine = lax.dynamic_slice_in_dim(norm_gains[1], j * 512, 512, 0)
    router_mine = lax.dynamic_slice_in_dim(w_router, j * 512, 512, 0)
    part = jnp.dot((hf * gain_mine).astype(bf16), router_mine, preferred_element_type=f32)
    square = jnp.sum(hf * hf, axis=1, keepdims=True)
    part = jnp.concatenate([part, jnp.broadcast_to(square, (TOK, EXPERTS))], axis=1)
    whole = part
    for k in (1, 2, 3):
        whole = whole + y_shift(part, k)

    arrived = lax.all_to_all(rows, W, 0, 0, tiled=True)
    top, bottom = pl.pallas_call(
        unpack_kernel,
        out_shape=(jax.ShapeDtypeStruct((HALF, 512), bf16),) * 2,
        in_specs=[vmem()],
        out_specs=(vmem(), vmem()),
        scratch_shapes=[pltpu.VMEM((HALF, 512), f32)],
        compiler_params=params(),
        name="unpack",
    )(arrived)
    top, bottom, up_sent, whole = lax.optimization_barrier(
        (top, bottom, pick(w_up, 1 - i), whole)
    )
    up_par = x_swap(up_sent)
    top_back, bottom_ahead = y_shift(top, 1), y_shift(bottom, 3)
    bottom_back, top_ahead = y_shift(bottom, 1), y_shift(top, 3)
    top_far, bottom_far = y_shift(top_back, 1), y_shift(bottom_ahead, 3)
    act = pl.pallas_call(
        gate_up_kernel,
        out_shape=jax.ShapeDtypeStruct((2 * HALF, 256), bf16),
        in_specs=[smem()] + [vmem()] * 13,
        out_specs=vmem(),
        compiler_params=params(),
        name="gate_up",
    )(
        here,
        *(top, top_back, top_ahead, top_far),
        *(bottom, bottom_back, bottom_ahead, bottom_far),
        norm_gains,
        w_gate,
        w_up,
        gate_par,
        up_par,
    )
    out = pl.pallas_call(
        down_kernel,
        out_shape=jax.ShapeDtypeStruct((WIDE, 2 * CAP, 256), bf16),
        in_specs=[smem()] + [vmem()] * 9,
        out_specs=vmem(),
        compiler_params=params(),
        name="down",
    )(here, act, *(y_shift(act, k) for k in (1, 2, 3)), *downs, down_par)
    back = lax.all_to_all(out, W, 0, 0, tiled=True)

    logits = whole[:, :EXPERTS] * lax.rsqrt(whole[:, EXPERTS : EXPERTS + 1] / 2048.0 + EPS)
    lifted = jax.nn.sigmoid(logits)
    onehot = jnp.sum(
        (routes[:, :, None] == jnp.arange(EXPERTS, dtype=jnp.int32)[None, None, :]).astype(f32),
        axis=1,
    )
    lifted = lifted * onehot
    gates = lifted / jnp.sum(lifted, axis=1, keepdims=True)
    gates = lax.dynamic_index_in_dim(gates.reshape(TOK, WIDE, 2), i, 2, keepdims=False).T

    moe = jnp.zeros((2 * TOK, 256), f32)
    contract = (((0, 1), (0, 1)), ((), ()))
    mixing = jnp.where(chosen, gates[:, None, :], 0.0)
    blank = jnp.zeros_like(mixing)
    mixing = jnp.concatenate(
        [
            jnp.concatenate([mixing, blank], axis=1),
            jnp.concatenate([blank, mixing], axis=1),
        ],
        axis=2,
    )
    mixing_hi = lax.reduce_precision(mixing, 8, 7)
    mixing_lo = (mixing - mixing_hi).astype(bf16)
    for matrix in lax.optimization_barrier((mixing_hi.astype(bf16), mixing_lo)):
        moe = moe + lax.dot_general(matrix, back, contract, preferred_element_type=f32)
    moe = moe.astype(bf16)
    moe_par = x_swap(moe)
    layer, part = pl.pallas_call(
        embed_kernel,
        out_shape=(
            jax.ShapeDtypeStruct((TOK, 512), bf16),
            jax.ShapeDtypeStruct((TOK + 16, 128), bf16),
        ),
        in_specs=[smem()] + [vmem()] * 5,
        out_specs=(vmem(), vmem()),
        compiler_params=params(),
        name="embed",
    )(here, hidden, moe, moe_par, norm_gains, w_proj)
    parts = [part] + [y_shift(part, k) for k in (1, 2, 3)]

    vectors = pl.pallas_call(
        vector_kernel,
        out_shape=jax.ShapeDtypeStruct((16, TOK, 128), bf16),
        in_specs=[vmem()] * 4,
        out_specs=vmem(),
        compiler_params=params(),
        name="vectors",
    )(*parts)
    vectors, layer = lax.optimization_barrier((vectors, layer))
    layers = [layer] + [y_shift(layer, k) for k in (1, 2, 3)]
    own = lax.all_to_all(vectors, ("z", "xl"), 0, 0, tiled=True).reshape(16 * TOK, 128)
    segment = doc_segment[0]
    requests = doc_request[0]
    docs = jnp.arange(16, dtype=jnp.int32)
    first = jnp.sum((segment[None, :] < docs[:, None]).astype(jnp.int32), axis=1)
    size = jnp.sum((segment[None, :] == docs[:, None]).astype(jnp.int32), axis=1)
    starts = jnp.cumsum(request_lengths, axis=1) - request_lengths
    starts = (starts + TOK * (jnp.arange(WIDE, dtype=jnp.int32) // 2)[:, None]).reshape(-1)
    match = requests[:, None] == jnp.arange(96, dtype=jnp.int32)[None, :]
    q_first = jnp.sum(jnp.where(match, starts[None, :], 0), axis=1)
    q_size = jnp.sum(jnp.where(match, request_lengths.reshape(-1)[None, :], 0), axis=1)
    away = lax.rem(requests // 3, 2) ^ core
    info = jnp.stack([first, size, q_first, q_size, away])
    own, info, *layers = lax.optimization_barrier((own, info, *layers))
    other = lax.ppermute(own, "core", [(0, 1), (1, 0)])
    layer_out = pl.pallas_call(
        assemble_kernel,
        out_shape=jax.ShapeDtypeStruct((TOK, 2048), bf16),
        in_specs=[smem()] + [vmem()] * 4,
        out_specs=vmem(),
        compiler_params=params(),
        name="assemble",
    )(here, *layers)
    doc_scores = pl.pallas_call(
        score_kernel,
        out_shape=jax.ShapeDtypeStruct((1, 16), f32),
        in_specs=[smem(), vmem()] + [anywhere()] * 2,
        out_specs=vmem(),
        scratch_shapes=[pltpu.VMEM((16, 128, 128), bf16), pltpu.SemaphoreType.DMA((16,))],
        compiler_params=params(),
        name="score",
    )(info, doc_vectors, own, other)
    return (layer_out, doc_scores)


def solution(mesh):
    split = Mesh(mesh.devices.reshape(8, 2, 2, 2, 4), ("z", "xl", "core", "xh", "y"))
    placed = (
        P(W, None),
        P(),
        P(None, None, N),
        P(None, N),
        P(N, None),
        P(),
        P(),
        P(W, None),
        P(W, None, N),
        P(W, None, N),
        P(W, N, None),
        P(),
        P(W + N, None),
        P(W + N, None),
        P(W + N, None),
    )
    return jax.shard_map(
        body,
        mesh=split,
        in_specs=placed,
        out_specs=(P(W, None), P(W + N, None)),
        check_vma=False,
    )
```

```python
import math

import jax
import jax.numpy as jnp
from jax import lax
from jax.experimental import pallas as pl
from jax.experimental.pallas import tpu as pltpu
from jax.sharding import Mesh, PartitionSpec as P

HD = 128
TOPK = 8
TOK = 128
CAP = 20
EXPERTS = 64
WIDE = 32
HALF = WIDE * CAP // 2
EPS = 1e-06
THETA = 50000.0
NEG = -1e30
W = ("z", "xl", "core")
N = ("xh", "y")
f32 = jnp.float32
bf16 = jnp.bfloat16


def y_shift(x, k):
    return lax.ppermute(x, "y", [(s, (s + k) % 4) for s in range(4)])


def x_swap(x):
    return lax.ppermute(x, "xh", [(0, 1), (1, 0)])


def attention_kernel(
    i_ref,
    j_ref,
    wide_ref,
    lengths_ref,
    qk_ref,
    gain_ref,
    x_hbm,
    w_hbm,
    out_hbm,
    gate_hbm,
    out0,
    out1,
    out2,
    out3,
    sent_ref,
    x_ref,
    w_ref,
    out_w_ref,
    sems,
):
    copies = [pltpu.make_async_copy(x_hbm, x_ref, sems.at[0])]
    copies += [
        pltpu.make_async_copy(w_hbm.at[part], w_ref.at[part], sems.at[1 + part]) for part in range(3)
    ]
    copies += [pltpu.make_async_copy(out_hbm, out_w_ref, sems.at[4])]
    copies += [pltpu.make_async_copy(gate_hbm.at[1 - i_ref[0]], sent_ref, sems.at[5])]
    for copy in copies:
        copy.start()
    wide = wide_ref[0]
    one = lengths_ref[0, wide]
    two = one + lengths_ref[1, wide]

    def member_of(places):
        return (places >= one).astype(jnp.int32) + (places >= two).astype(jnp.int32)

    down_places = lax.broadcasted_iota(jnp.int32, (TOK, HD), 0)
    across_places = lax.broadcasted_iota(jnp.int32, (TOK, HD), 1)
    member = member_of(down_places)
    same = member == member_of(across_places)
    start = jnp.where(member == 0, 0, jnp.where(member == 1, one, two))
    half = lax.rem(across_places, HD // 2).astype(f32)
    freq = jnp.exp(half * (-math.log(THETA) / (HD // 2)))
    angle = (down_places - start).astype(f32) * freq
    cosine = jnp.cos(angle)
    sine = jnp.sin(angle)
    sine = jnp.where(across_places < HD // 2, -sine, sine)

    copies[0].wait()
    x = x_ref[...].astype(f32)
    scale = lax.rsqrt(jnp.mean(x * x, axis=1, keepdims=True) + EPS)
    normed = (x * scale * gain_ref[0:1, :]).astype(bf16)
    parts = []
    for part in range(3):
        copies[1 + part].wait()
        parts.append(jnp.dot(normed, w_ref[part], preferred_element_type=f32))
    query, keys, values = parts

    def turned(v, gain):
        v = v * lax.rsqrt(jnp.mean(v * v, axis=1, keepdims=True) + EPS) * gain
        return (v * cosine + pltpu.roll(v, HD // 2, 1) * sine).astype(bf16)

    mixed = []
    for head in range(2):
        at = slice(head * HD, (head + 1) * HD)
        q = turned(query[:, at], qk_ref[0:1, at])
        k = turned(keys[:, at], qk_ref[1:2, at])
        scores = lax.dot_general(q, k, (((1,), (1,)), ((), ())), preferred_element_type=f32)
        scores = jnp.where(same, scores * HD ** (-0.5), NEG)
        weights = jnp.exp(scores - jnp.max(scores, axis=1, keepdims=True))
        probs = (weights / jnp.sum(weights, axis=1, keepdims=True)).astype(bf16)
        mixed.append(
            jnp.dot(probs, values[:, at].astype(bf16), preferred_element_type=f32).astype(bf16)
        )
    mixed = jnp.concatenate(mixed, axis=1)
    copies[4].wait()
    j = j_ref[0]
    for k, out_ref in enumerate((out0, out1, out2, out3)):
        part = lax.rem(j + k, 4)
        columns = pl.ds(pl.multiple_of(part * 512, 512), 512)
        out_ref[...] = jnp.dot(mixed, out_w_ref[:, columns], preferred_element_type=f32).astype(bf16)
    copies[5].wait()


def choose_kernel(here_ref, routes_ref, out_ref):
    expert = 2 * lax.broadcasted_iota(jnp.int32, (WIDE, TOK), 0) + here_ref[0]
    hit = jnp.zeros((WIDE, TOK), f32)
    for k in range(TOPK):
        hit = hit + (routes_ref[k : k + 1, :] == expert).astype(f32)
    sooner = lax.broadcasted_iota(jnp.int32, (TOK, TOK), 0)
    earlier = (sooner < lax.broadcasted_iota(jnp.int32, (TOK, TOK), 1)).astype(f32).astype(bf16)
    before = jnp.dot(hit.astype(bf16), earlier, preferred_element_type=f32)
    place = jnp.where(hit > 0, before, -1.0).astype(bf16)
    owner = CAP * lax.broadcasted_iota(jnp.int32, (WIDE * CAP, WIDE), 1)
    slot = lax.broadcasted_iota(jnp.int32, (WIDE * CAP, WIDE), 0) - owner
    inside = (slot >= 0) & (slot < CAP)
    spread = jnp.dot(inside.astype(f32).astype(bf16), place, preferred_element_type=f32)
    slot = jnp.sum(jnp.where(inside, slot, 0).astype(f32), axis=1, keepdims=True)
    out_ref[...] = (spread == slot).astype(f32).astype(bf16)


def packed(rows):
    return jnp.concatenate([rows[:, 0:256], rows[:, 256:512]], axis=0).astype(bf16)


def dispatch_kernel(here_ref, x_ref, own_ref, par_ref, choose_ref, hidden_ref, rows_ref):
    j = here_ref[1]
    mine = x_ref[:, pl.ds(pl.multiple_of(j * 512, 512), 512)].astype(f32)
    hidden = (mine + (own_ref[...].astype(f32) + par_ref[...].astype(f32))).astype(bf16)
    hidden_ref[...] = hidden
    rows = jnp.dot(choose_ref[...], hidden, preferred_element_type=f32)
    for s in range(WIDE):
        rows_ref[s] = packed(rows[s * CAP : (s + 1) * CAP])


def unpack_kernel(in_ref, top_ref, bottom_ref, scratch):
    for half, out_ref in enumerate((top_ref, bottom_ref)):
        for s in range(WIDE // 2):
            rows = in_ref[half * (WIDE // 2) + s].astype(f32)
            at = slice(s * CAP, (s + 1) * CAP)
            scratch[at, 0:256] = rows[0:CAP]
            scratch[at, 256:512] = rows[CAP:]
        out_ref[...] = scratch[...].astype(bf16)


def gate_up_kernel(here_ref, *refs):
    halves = refs[0:4], refs[4:8]
    gain_ref, gate_ref, up_ref, gate_par, up_par, out_ref = refs[8:]
    i, j = here_ref[0], here_ref[1]
    scales = []
    for xs in halves:
        total = jnp.zeros((HALF, 1), f32)
        for x in xs:
            v = x[...].astype(f32)
            total = total + jnp.sum(v * v, axis=1, keepdims=True)
        scales.append(lax.rsqrt(total / 2048.0 + EPS))
    for half, (xs, scale) in enumerate(zip(halves, scales)):
        own = jnp.zeros((HALF, 256), f32)
        par = jnp.zeros((HALF, 256), f32)
        for k, x in enumerate(xs):
            part = lax.rem(j + 4 + (0, -1, 1, 2)[k], 4)
            rows = pl.ds(pl.multiple_of(part * 512, 512), 512)
            normed = (x[...].astype(f32) * scale * gain_ref[1:2, rows]).astype(bf16)
            w_own = jnp.concatenate([gate_ref[i, rows, :], up_ref[i, rows, :]], axis=1)
            w_par = jnp.concatenate([gate_par[rows, :], up_par[rows, :]], axis=1)
            own = own + jnp.dot(normed, w_own, preferred_element_type=f32)
            par = par + jnp.dot(normed, w_par, preferred_element_type=f32)
        for at, both in ((0, own), (128, par)):
            gate, up = both[:, :128], both[:, 128:]
            out_ref[half * HALF : (half + 1) * HALF, at : at + 128] = (
                gate / (1.0 + jnp.exp(-gate)) * up
            ).astype(bf16)


def down_kernel(here_ref, a0, a1, a2, a3, w0, w1, w2, w3, par_ref, out_ref):
    i = here_ref[0]
    total = jnp.zeros((a0.shape[0], 512), f32)
    for k, (a, w) in enumerate(((a0, w0), (a1, w1), (a2, w2), (a3, w3))):
        weight = jnp.concatenate([w[i], par_ref[k]], axis=0)
        total = total + jnp.dot(a[...], weight, preferred_element_type=f32)
    for s in range(WIDE):
        out_ref[s] = packed(total[s * CAP : (s + 1) * CAP])


def embed_kernel(here_ref, hidden_ref, moe_ref, par_ref, gain_ref, w_ref, layer_ref, part_ref):
    mine = pl.ds(pl.multiple_of(here_ref[1] * 512, 512), 512)
    moe = moe_ref[...].astype(f32) + par_ref[...].astype(f32)
    layer = hidden_ref[...].astype(f32) + jnp.concatenate([moe[0:TOK], moe[TOK:]], axis=1)
    layer = layer.astype(bf16)
    layer_ref[...] = layer
    layer = layer.astype(f32)
    scaled = (layer * gain_ref[2:3, mine]).astype(bf16)
    part = jnp.dot(scaled, w_ref[mine, :], preferred_element_type=f32)
    part_ref[0:TOK, :] = part.astype(bf16)
    square = jnp.broadcast_to(jnp.sum(layer * layer, axis=1, keepdims=True), (TOK, TOK))
    part_ref[TOK:, :] = jnp.transpose(square)[0:16].astype(bf16)


def vector_kernel(p0, p1, p2, p3, out_ref):
    whole = sum(p[...].astype(f32) for p in (p0, p1, p2, p3))
    square = jnp.transpose(jnp.broadcast_to(whole[TOK : TOK + 1], (TOK, TOK)))
    embedded = whole[0:TOK] * lax.rsqrt(square / 2048.0 + EPS)
    norm = jnp.sum(embedded * embedded, axis=1, keepdims=True)
    vectors = (embedded * lax.rsqrt(norm + EPS)).astype(bf16)
    for copy in range(16):
        out_ref[copy] = vectors


def assemble_kernel(here_ref, p0, p1, p2, p3, out_ref):
    j = here_ref[1]
    for k, piece in enumerate((p0, p1, p2, p3)):
        part = lax.rem(j - k + 4, 4)
        out_ref[:, pl.ds(pl.multiple_of(part * 512, 512), 512)] = piece[...]


def score_kernel(info_ref, doc_ref, own_ref, other_ref, out_ref):
    def spot(d):
        return pl.multiple_of(jnp.minimum((info_ref[2, d] // 16) * 16, 2048 - 128), 16)

    lane = lax.broadcasted_iota(jnp.int32, (1, 16), 1)
    scores = jnp.zeros((1, 16), f32)
    rows = lax.broadcasted_iota(jnp.int32, (144, 128), 0)
    columns = lax.broadcasted_iota(jnp.int32, (1, 128), 1)
    for d in range(16):
        first, size = info_ref[0, d], info_ref[1, d]
        q_first, q_size = info_ref[2, d], info_ref[3, d]
        at = pl.multiple_of(jnp.minimum((first // 16) * 16, 1024 - 144), 16)
        window = pl.ds(spot(d), 128)
        query = jnp.where(info_ref[4, d] == 0, own_ref[window, :], other_ref[window, :])
        sims = lax.dot_general(
            doc_ref[pl.ds(at, 144), :],
            query,
            (((1,), (1,)), ((), ())),
            preferred_element_type=f32,
        )
        keep = (rows >= first - at) & (rows < first - at + size)
        best = jnp.max(jnp.where(keep, sims, NEG), axis=0, keepdims=True)
        q_start = q_first - spot(d)
        used = (columns >= q_start) & (columns < q_start + q_size)
        value = jnp.sum(jnp.where(used, best, 0.0), axis=1, keepdims=True) / q_size.astype(f32)
        scores = jnp.where(lane == d, value, scores)
    out_ref[...] = scores


def vmem():
    return pl.BlockSpec(memory_space=pltpu.VMEM)


def smem():
    return pl.BlockSpec(memory_space=pltpu.SMEM)


def hbm():
    return pl.BlockSpec(memory_space=pltpu.HBM)


def anywhere():
    return pl.BlockSpec(memory_space=pl.ANY)


def params():
    return pltpu.CompilerParams(vmem_limit_bytes=16 << 20)


def body(
    tokens,
    request_lengths,
    w_qkv,
    qk_gain,
    w_out,
    norm_gains,
    w_router,
    routes,
    w_gate,
    w_up,
    w_down,
    w_proj,
    doc_vectors,
    doc_segment,
    doc_request,
):
    i = lax.axis_index("xh")
    j = lax.axis_index("y")
    core = lax.axis_index("core")
    wide = lax.axis_index(W)
    here = jnp.stack([i, j, wide, core])

    def pick(array, which):
        return lax.dynamic_index_in_dim(array, which, 0, keepdims=False)

    def cut(array, part, axis):
        return lax.dynamic_slice_in_dim(array, lax.rem(part, 4) * 512, 512, axis)

    *attn, gate_sent = pl.pallas_call(
        attention_kernel,
        out_shape=(
            *(jax.ShapeDtypeStruct((TOK, 512), bf16),) * 4,
            jax.ShapeDtypeStruct((2048, 128), bf16),
        ),
        in_specs=[smem()] * 4 + [vmem()] * 2 + [hbm()] * 4,
        out_specs=(vmem(),) * 5,
        scratch_shapes=[
            pltpu.VMEM((TOK, 2048), bf16),
            pltpu.VMEM((3, 2048, 256), bf16),
            pltpu.VMEM((256, 2048), bf16),
            pltpu.SemaphoreType.DMA((6,)),
        ],
        compiler_params=pltpu.CompilerParams(vmem_limit_bytes=60 << 20),
        name="attention",
    )(
        i.reshape(1),
        j.reshape(1),
        wide.reshape(1),
        request_lengths.T,
        qk_gain,
        norm_gains,
        tokens,
        w_qkv.transpose(1, 0, 2),
        w_out,
        w_gate,
    )
    gate_par = x_swap(gate_sent)
    attn_parts = [y_shift(attn[k], k) for k in (1, 2, 3)]

    downs = [cut(w_down, j, 2)] + [y_shift(cut(w_down, j + k, 2), k) for k in (1, 2, 3)]
    down_par = x_swap(jnp.stack([pick(d, 1 - i) for d in downs]))

    experts_here = 2 * jnp.arange(WIDE, dtype=jnp.int32) + i
    hit = jnp.sum((routes.T[None, :, :] == experts_here[:, None, None]).astype(f32), axis=1)
    places = jnp.arange(TOK, dtype=jnp.int32)
    earlier = (places[:, None] < places[None, :]).astype(bf16)
    before = jnp.dot(hit.astype(bf16), earlier, preferred_element_type=f32)
    slot = jnp.arange(CAP, dtype=jnp.int32).astype(f32)
    chosen = (before[:, None, :] == slot[None, :, None]) & (hit[:, None, :] > 0)
    choose = pl.pallas_call(
        choose_kernel,
        out_shape=jax.ShapeDtypeStruct((WIDE * CAP, TOK), bf16),
        in_specs=[smem(), vmem()],
        out_specs=vmem(),
        compiler_params=params(),
        name="choose",
    )(here, routes.T)

    attn = (attn[0].astype(f32) + sum(p.astype(f32) for p in attn_parts)).astype(bf16)
    attn, choose = lax.optimization_barrier((attn, choose))
    attn_par = x_swap(attn)
    attn_par, gate_par = lax.optimization_barrier((attn_par, gate_par))
    hidden, rows = pl.pallas_call(
        dispatch_kernel,
        out_shape=(
            jax.ShapeDtypeStruct((TOK, 512), bf16),
            jax.ShapeDtypeStruct((WIDE, 2 * CAP, 256), bf16),
        ),
        in_specs=[smem()] + [vmem()] * 4,
        out_specs=(vmem(), vmem()),
        compiler_params=params(),
        name="dispatch",
    )(here, tokens, attn, attn_par, choose)

    hf = hidden.astype(f32)
    gain_mine = lax.dynamic_slice_in_dim(norm_gains[1], j * 512, 512, 0)
    router_mine = lax.dynamic_slice_in_dim(w_router, j * 512, 512, 0)
    part = jnp.dot((hf * gain_mine).astype(bf16), router_mine, preferred_element_type=f32)
    square = jnp.sum(hf * hf, axis=1, keepdims=True)
    part = jnp.concatenate([part, jnp.broadcast_to(square, (TOK, EXPERTS))], axis=1)
    whole = part
    for k in (1, 2, 3):
        whole = whole + y_shift(part, k)

    arrived = lax.all_to_all(rows, W, 0, 0, tiled=True)
    top, bottom = pl.pallas_call(
        unpack_kernel,
        out_shape=(jax.ShapeDtypeStruct((HALF, 512), bf16),) * 2,
        in_specs=[vmem()],
        out_specs=(vmem(), vmem()),
        scratch_shapes=[pltpu.VMEM((HALF, 512), f32)],
        compiler_params=params(),
        name="unpack",
    )(arrived)
    top, bottom, up_sent, whole = lax.optimization_barrier(
        (top, bottom, pick(w_up, 1 - i), whole)
    )
    up_par = x_swap(up_sent)
    top_back, bottom_ahead = y_shift(top, 1), y_shift(bottom, 3)
    bottom_back, top_ahead = y_shift(bottom, 1), y_shift(top, 3)
    top_far, bottom_far = y_shift(top_back, 1), y_shift(bottom_ahead, 3)
    act = pl.pallas_call(
        gate_up_kernel,
        out_shape=jax.ShapeDtypeStruct((2 * HALF, 256), bf16),
        in_specs=[smem()] + [vmem()] * 13,
        out_specs=vmem(),
        compiler_params=params(),
        name="gate_up",
    )(
        here,
        *(top, top_back, top_ahead, top_far),
        *(bottom, bottom_back, bottom_ahead, bottom_far),
        norm_gains,
        w_gate,
        w_up,
        gate_par,
        up_par,
    )
    out = pl.pallas_call(
        down_kernel,
        out_shape=jax.ShapeDtypeStruct((WIDE, 2 * CAP, 256), bf16),
        in_specs=[smem()] + [vmem()] * 9,
        out_specs=vmem(),
        compiler_params=params(),
        name="down",
    )(here, act, *(y_shift(act, k) for k in (1, 2, 3)), *downs, down_par)
    back = lax.all_to_all(out, W, 0, 0, tiled=True)

    logits = whole[:, :EXPERTS] * lax.rsqrt(whole[:, EXPERTS : EXPERTS + 1] / 2048.0 + EPS)
    lifted = jax.nn.sigmoid(logits)
    onehot = jnp.sum(
        (routes[:, :, None] == jnp.arange(EXPERTS, dtype=jnp.int32)[None, None, :]).astype(f32),
        axis=1,
    )
    lifted = lifted * onehot
    gates = lifted / jnp.sum(lifted, axis=1, keepdims=True)
    gates = lax.dynamic_index_in_dim(gates.reshape(TOK, WIDE, 2), i, 2, keepdims=False).T

    moe = jnp.zeros((2 * TOK, 256), f32)
    contract = (((0, 1), (0, 1)), ((), ()))
    mixing = jnp.where(chosen, gates[:, None, :], 0.0)
    blank = jnp.zeros_like(mixing)
    mixing = jnp.concatenate(
        [
            jnp.concatenate([mixing, blank], axis=1),
            jnp.concatenate([blank, mixing], axis=1),
        ],
        axis=2,
    )
    mixing_hi = lax.reduce_precision(mixing, 8, 7)
    mixing_lo = (mixing - mixing_hi).astype(bf16)
    for matrix in lax.optimization_barrier((mixing_hi.astype(bf16), mixing_lo)):
        moe = moe + lax.dot_general(matrix, back, contract, preferred_element_type=f32)
    moe = moe.astype(bf16)
    moe_par = x_swap(moe)
    layer, part = pl.pallas_call(
        embed_kernel,
        out_shape=(
            jax.ShapeDtypeStruct((TOK, 512), bf16),
            jax.ShapeDtypeStruct((TOK + 16, 128), bf16),
        ),
        in_specs=[smem()] + [vmem()] * 5,
        out_specs=(vmem(), vmem()),
        compiler_params=params(),
        name="embed",
    )(here, hidden, moe, moe_par, norm_gains, w_proj)
    parts = [part] + [y_shift(part, k) for k in (1, 2, 3)]

    vectors = pl.pallas_call(
        vector_kernel,
        out_shape=jax.ShapeDtypeStruct((16, TOK, 128), bf16),
        in_specs=[vmem()] * 4,
        out_specs=vmem(),
        compiler_params=params(),
        name="vectors",
    )(*parts)
    vectors, layer = lax.optimization_barrier((vectors, layer))
    layers = [layer] + [y_shift(layer, k) for k in (1, 2, 3)]
    own = lax.all_to_all(vectors, ("z", "xl"), 0, 0, tiled=True).reshape(16 * TOK, 128)
    segment = doc_segment[0]
    requests = doc_request[0]
    docs = jnp.arange(16, dtype=jnp.int32)
    first = jnp.sum((segment[None, :] < docs[:, None]).astype(jnp.int32), axis=1)
    size = jnp.sum((segment[None, :] == docs[:, None]).astype(jnp.int32), axis=1)
    starts = jnp.cumsum(request_lengths, axis=1) - request_lengths
    starts = (starts + TOK * (jnp.arange(WIDE, dtype=jnp.int32) // 2)[:, None]).reshape(-1)
    match = requests[:, None] == jnp.arange(96, dtype=jnp.int32)[None, :]
    q_first = jnp.sum(jnp.where(match, starts[None, :], 0), axis=1)
    q_size = jnp.sum(jnp.where(match, request_lengths.reshape(-1)[None, :], 0), axis=1)
    away = lax.rem(requests // 3, 2) ^ core
    info = jnp.stack([first, size, q_first, q_size, away])
    own, info, *layers = lax.optimization_barrier((own, info, *layers))
    other = lax.ppermute(own, "core", [(0, 1), (1, 0)])
    layer_out = pl.pallas_call(
        assemble_kernel,
        out_shape=jax.ShapeDtypeStruct((TOK, 2048), bf16),
        in_specs=[smem()] + [vmem()] * 4,
        out_specs=vmem(),
        compiler_params=params(),
        name="assemble",
    )(here, *layers)
    doc_scores = pl.pallas_call(
        score_kernel,
        out_shape=jax.ShapeDtypeStruct((1, 16), f32),
        in_specs=[smem()] + [vmem()] * 3,
        out_specs=vmem(),
        compiler_params=params(),
        name="score",
    )(info, doc_vectors, own, other)
    return (layer_out, doc_scores)


def solution(mesh):
    split = Mesh(mesh.devices.reshape(8, 2, 2, 2, 4), ("z", "xl", "core", "xh", "y"))
    placed = (
        P(W, None),
        P(),
        P(None, None, N),
        P(None, N),
        P(N, None),
        P(),
        P(),
        P(W, None),
        P(W, None, N),
        P(W, None, N),
        P(W, N, None),
        P(),
        P(W + N, None),
        P(W + N, None),
        P(W + N, None),
    )
    return jax.shard_map(
        body,
        mesh=split,
        in_specs=placed,
        out_specs=(P(W, None), P(W + N, None)),
        check_vma=False,
    )
```
